32 devices in a mesh: groups: 2 (over y), gcol: 8 (over z, x), grow: 2 (over core).
Axes of the slice: x: 2, y: 2, z: 4, core: 2. Of those that a mesh axis runs over, the one named last changes fastest.
Arguments:
- patches: bfloat16 [16, 256, 1024], P(('groups', 'grow'), 'gcol'), parts along dimension 0, may hold values from -6 to 6
- mask_token: bfloat16 [1024], replicated, may hold values from -6 to 6
- masked: int32 [16, 256], P(('groups', 'grow'), 'gcol'), parts along dimension 0, may hold values 0 or 1
- tissue: int32 [16, 256], P(('groups', 'grow'), 'gcol'), parts along dimension 0, may hold values 0 or 1
- in_weight: bfloat16 [2304, 1024], P(None, 'grow'), may hold values from -0.1875 to 0.1875
- out_weight: bfloat16 [1024, 1024], P(None, 'grow'), may hold values from -0.1875 to 0.1875
- row_decay: float32 [8, 16, 256], P(None, ('groups', 'grow'), 'gcol'), parts along dimension 1, may hold values from -1.5 to 0
- col_decay: float32 [8, 16, 256], P(None, ('groups', 'grow'), 'gcol'), parts along dimension 1, may hold values from -1.5 to 0
- cotangent: bfloat16 [16, 256, 1024], P(('groups', 'grow'), 'gcol'), parts along dimension 0, may hold values from -6 to 6
Outputs:
- patch_grad: bfloat16 [16, 256, 1024], P(('groups', 'grow'), 'gcol'), parts along dimension 0
- out_weight_grad: float32 [2048, 1024], P(('groups', 'gcol', 'grow')), parts along dimension 0
The draws below stay inside these ranges and needn't reach their ends.
There are 2 independent parts, one for each index of `groups`. The reference program is written for one: setup_inputs(seed, part) draws one part's arguments, and reference() takes and returns one part's arrays. A program takes and returns all parts, laid end to end along the dimension named above; an argument that names none is the same for every part. Nothing has to cross between parts.
All inputs are finite; a program needn't handle non-finite values. No bound on the sum of `masked` or of `tissue` on one device may be relied on, other than what follows from the above.
Results may differ from the reference program's by a relative error of at most 0.0095.
The reference program's roundings to bfloat16 on the way count: a program that leaves them out, or rounds other values in their place, can miss the bound.
Values may be sent and summed in bfloat16 or wider, within the bound.
A program may use at most 320 MiB of HBM per device.

```python
import math
import jax
import jax.numpy as jnp
from jax import lax

D = 1024
E = 1024
HEADS = 16
N = 64
CH = 4
CW = 32
PATCH_GRID_ROWS = 8
PATCH_GRID_COLS = 256


def decay_field(key, sequence_length):
    number_of_heads = HEADS // 2
    random_split_keys = jax.random.split(key, 7)
    ranking = jax.random.permutation(random_split_keys[0], number_of_heads)
    slow_count = number_of_heads // 2
    is_slow = ranking < slow_count
    slow_rate = jax.random.uniform(random_split_keys[1], (number_of_heads,), jnp.float32, 0.1, 0.4) * (math.log(10.0) / sequence_length)
    fast_rate = jax.random.uniform(random_split_keys[2], (number_of_heads,), jnp.float32, 1.0 / 50.0, 1.0 / 30.0)
    base_rate = jnp.where(is_slow, slow_rate, fast_rate)
    blocks = jax.random.uniform(random_split_keys[3], (number_of_heads, PATCH_GRID_ROWS // CH, PATCH_GRID_COLS // CW), jnp.float32, -0.5, 0.5)
    blocks = jnp.repeat(jnp.repeat(blocks, CH, axis=1), CW, axis=2)
    jitter = jax.random.uniform(random_split_keys[4], (number_of_heads, PATCH_GRID_ROWS, PATCH_GRID_COLS), jnp.float32, -0.35, 0.35)
    spike_position = jax.random.randint(random_split_keys[5], (number_of_heads, PATCH_GRID_ROWS, PATCH_GRID_COLS), 0, sequence_length) < 2
    spike_loss_value = jax.random.uniform(random_split_keys[6], (number_of_heads, PATCH_GRID_ROWS, PATCH_GRID_COLS), jnp.float32, 0.22, 0.69)
    stable_baseline = base_rate[:, None, None] * jnp.exp(blocks + jitter)
    return -stable_baseline - jnp.where(spike_position, spike_loss_value, 0.0)


def draw_row_decay(key, part):
    return decay_field(jax.random.fold_in(key, 7), PATCH_GRID_COLS)


def draw_col_decay(key, part):
    return decay_field(jax.random.fold_in(key, 11), PATCH_GRID_ROWS)


def place_ends(array, own_key, smallest, high):
    place = [jax.random.randint(jax.random.fold_in(own_key, axis), (), 0, length) for axis, length in enumerate(array.shape)]
    longest = array.shape.index(max(array.shape))
    next_to = place[:longest] + [(place[longest] + 1) % array.shape[longest]] + place[longest + 1:]
    return array.at[tuple(place)].set(smallest).at[tuple(next_to)].set(high)


def spiked(drawn, rng, source, target, parts, factor):
    owner, partner = [(jnp.arange(drawn.shape[position]) // (drawn.shape[position] // parts)).reshape([-1 if axis == position else 1 for axis in range(drawn.ndim)]) for position in (source, target)]
    chosen = jax.random.permutation(rng, parts)[partner]
    strong = (owner == chosen) | (owner == (partner + parts // 2) % parts)
    return jnp.where(strong, factor * drawn, drawn)


def block_levels(stream_key, dims, shards, least, largest):
    loudness, own = 1.0, jax.random.fold_in(stream_key, 6)
    for position, blocks in shards:
        steps = jnp.exp(jax.random.uniform(jax.random.fold_in(own, position), (blocks,), jnp.float32, least / len(shards), largest / len(shards)))
        loudness = loudness * jnp.repeat(steps, dims[position] // blocks).reshape([-1 if axis == position else 1 for axis in range(len(dims))])
    return loudness


def bell_draw(stream_key, shape, width, bound, cuts=(), kind=jnp.bfloat16):
    array = jax.random.normal(stream_key, shape, jnp.float32) * width
    if len(cuts) > 0:
        array = block_levels(stream_key, shape, cuts, -0.22, 0.18) * array
    return jnp.clip(array, min=-bound, max=bound).astype(kind)


def bell_draw_with(own_key, extent, scale, limit, cuts, heavy, held_as=jnp.bfloat16):
    drawn = scale * jax.random.normal(own_key, extent, jnp.float32)
    if cuts:
        drawn = drawn * block_levels(own_key, extent, cuts, -0.22, 0.18)
    return jnp.clip(spiked(drawn, jax.random.fold_in(own_key, 3), *heavy), -limit, limit).astype(held_as)


def setup_inputs(seed: int = 0, part: int = 0) -> dict:
    splits = jax.random.split(jax.random.key(seed), 10)
    own_keys = jax.random.split(jax.random.fold_in(splits[9], part), 10)
    return {
        "patches": bell_draw(own_keys[0], (PATCH_GRID_ROWS, PATCH_GRID_COLS, D), 1.0, 6.0, ((0, 2), (1, 8))),
        "mask_token": bell_draw(splits[1], (D,), 1.0, 6.0),
        "masked": place_ends((jax.random.randint(own_keys[2], (PATCH_GRID_ROWS, PATCH_GRID_COLS), 0, 4) < 3).astype(jnp.int32), jax.random.fold_in(own_keys[2], 1), 0, 1),
        "tissue": place_ends((jax.random.randint(own_keys[3], (PATCH_GRID_ROWS, PATCH_GRID_COLS), 0, 5) < 4).astype(jnp.int32), jax.random.fold_in(own_keys[3], 1), 0, 1),
        "in_weight": bell_draw(splits[4], (2 * E + 4 * N, D), D ** -0.5, 0.1875, ((1, 2),)),
        "out_weight": bell_draw(splits[5], (D, E), E ** -0.5, 0.1875, ((1, 2),)),
        "row_decay": draw_row_decay(jax.random.fold_in(jax.random.fold_in(splits[9], part), 71), part),
        "col_decay": draw_col_decay(jax.random.fold_in(jax.random.fold_in(splits[9], part), 71), part),
        "cotangent": bell_draw_with(own_keys[8], (PATCH_GRID_ROWS, PATCH_GRID_COLS, D), 1.0, 6.0, ((0, 2), (1, 8)), (1, 2, 8, 2.0)),
    }


EPSILON = 1e-05
PRECISE = lax.Precision.HIGHEST

def scan_lines(inputs, key_vecs, query_vecs, log_decay):
    line_count, length, number_of_heads, head_size = inputs.shape
    state_size = key_vecs.shape[2]
    block_len = math.gcd(length, 64)
    block_count = length // block_len
    pieces_in = inputs.reshape(line_count, block_count, block_len, number_of_heads, head_size).transpose(1, 0, 2, 3, 4)
    pieces_key = key_vecs.reshape(line_count, block_count, block_len, state_size).transpose(1, 0, 2, 3)
    pieces_query = query_vecs.reshape(line_count, block_count, block_len, state_size).transpose(1, 0, 2, 3)
    pieces_log = log_decay.reshape(number_of_heads, line_count, block_count, block_len).transpose(2, 0, 1, 3)
    causal = jnp.arange(block_len)[:, None] >= jnp.arange(block_len)[None, :]

    def block_step(state_now, pieces):
        piece_in, piece_key, piece_query, piece_log = pieces
        running = jnp.cumsum(piece_log, axis=2)
        whole_log = running[:, :, -1]
        log_gaps = running[:, :, :, None] - running[:, :, None, :]
        decay_mat = jnp.where(causal, jnp.exp(jnp.where(causal, log_gaps, 0.0)), 0.0)
        scores = jnp.einsum('ltn,lkn->ltk', piece_query, piece_key, precision=PRECISE)
        within = jnp.einsum('gltk,lkgp->ltgp', decay_mat * scores[None], piece_in, precision=PRECISE)
        carried = jnp.einsum('ltn,lgpn->ltgp', piece_query, state_now, precision=PRECISE)
        carried = carried * jnp.exp(running).transpose(1, 2, 0)[..., None]
        to_end = jnp.exp(whole_log[:, :, None] - running)
        fresh = jnp.einsum('glk,lkgp,lkn->lgpn', to_end, piece_in, piece_key, precision=PRECISE)
        state_next = jnp.exp(whole_log).T[:, :, None, None] * state_now + fresh
        return (state_next, within + carried)
    start_state = jnp.zeros((line_count, number_of_heads, head_size, state_size), jnp.float32)
    final_state, outputs = lax.scan(block_step, start_state, (pieces_in, pieces_key, pieces_query, pieces_log))
    return outputs.transpose(1, 0, 2, 3, 4).reshape(line_count, length, number_of_heads, head_size)

def layer_forward(model_in, in_weight, out_weight, row_decay, col_decay):
    grid_rows, grid_cols, feat_width = model_in.shape
    tok_count = grid_rows * grid_cols
    inner_width = out_weight.shape[1]
    half_width = inner_width // 2
    state_size = (in_weight.shape[0] - 2 * inner_width) // 4
    number_of_heads = HEADS // 2
    head_size = inner_width // HEADS
    projected = jnp.dot(model_in.reshape(tok_count, feat_width), in_weight.T, preferred_element_type=jnp.float32)
    proj_bf = projected.astype(jnp.bfloat16)
    pre_values = proj_bf[:, :inner_width].astype(jnp.float32)
    gate_pre = proj_bf[:, inner_width:2 * inner_width].astype(jnp.float32)
    offset = 2 * inner_width
    key_rows = proj_bf[:, offset:offset + state_size].astype(jnp.float32).reshape(grid_rows, grid_cols, state_size)
    query_rows = proj_bf[:, offset + state_size:offset + 2 * state_size].astype(jnp.float32).reshape(grid_rows, grid_cols, state_size)
    key_cols = proj_bf[:, offset + 2 * state_size:offset + 3 * state_size].astype(jnp.float32).reshape(grid_rows, grid_cols, state_size).transpose(1, 0, 2)
    query_cols = proj_bf[:, offset + 3 * state_size:offset + 4 * state_size].astype(jnp.float32).reshape(grid_rows, grid_cols, state_size).transpose(1, 0, 2)
    values = jax.nn.silu(pre_values)
    row_inputs = values[:, :half_width].reshape(grid_rows, grid_cols, number_of_heads, head_size)
    col_inputs = values[:, half_width:].reshape(grid_rows, grid_cols, number_of_heads, head_size).transpose(1, 0, 2, 3)
    row_out = scan_lines(row_inputs, key_rows, query_rows, row_decay)
    col_out = scan_lines(col_inputs, key_cols, query_cols, col_decay.transpose(0, 2, 1)).transpose(1, 0, 2, 3)
    mixed = jnp.concatenate([row_out.reshape(tok_count, half_width), col_out.reshape(tok_count, half_width)], axis=1)
    gated = (mixed * jax.nn.silu(gate_pre)).reshape(tok_count, HEADS, head_size)
    normed = gated * lax.rsqrt(lax.optimization_barrier(jnp.mean(gated * gated, axis=2, keepdims=True)) + EPSILON)
    normed_bf = normed.reshape(tok_count, inner_width).astype(jnp.bfloat16)
    layer_out = jnp.dot(normed_bf, out_weight.T, preferred_element_type=jnp.float32)
    return (layer_out, normed_bf)

def reference(patches, mask_token, masked, tissue, in_weight, out_weight, row_decay, col_decay, cotangent):
    grid_rows, grid_cols, feat_width = patches.shape
    tok_count = grid_rows * grid_cols
    chosen = (masked == 1)[:, :, None]
    present = tissue.astype(jnp.bfloat16)[:, :, None]
    model_in = jnp.where(chosen, mask_token[None, None, :], patches) * present
    grad_out = cotangent * masked.astype(jnp.bfloat16)[:, :, None]
    grad_flat = grad_out.reshape(tok_count, feat_width)

    def forward(value):
        return layer_forward(value, in_weight, out_weight, row_decay, col_decay)
    layer_out, pullback, normed_bf = jax.vjp(forward, model_in, has_aux=True)
    grad_model_in, = pullback(grad_flat.astype(jnp.float32))
    keep_mask = present * (1 - masked).astype(jnp.bfloat16)[:, :, None]
    patch_grad = grad_model_in.astype(jnp.bfloat16) * keep_mask
    weight_sum = jnp.dot(grad_flat.T, normed_bf, preferred_element_type=jnp.float32)
    out_weight_grad = weight_sum * (1.0 / math.sqrt(tok_count))
    return (patch_grad, out_weight_grad)
```

```python
import functools
import math

import jax
import jax.numpy as jnp
from jax import lax
from jax.experimental import pallas as pl
from jax.experimental.pallas import tpu as pltpu
from jax.sharding import PartitionSpec as P

E = 1024
HEADS = 16
N = 64


EPSILON = 1e-05
PRECISE = lax.Precision.HIGHEST


def prefix(value, axis, join, neutral):
    count, mine = (lax.axis_size(axis), lax.axis_index(axis))
    pieces = jax.tree.map(lambda part: lax.all_gather(part, axis), value)
    so_far = jax.tree.map(
        lambda part, zero: jnp.full_like(part, 0) + jnp.asarray(zero, part.dtype), value, neutral
    )

    def prefix_hop(position, so_far):
        longer = join(so_far, jax.tree.map(lambda part: part[position], pieces))
        return jax.tree.map(lambda new, old: jnp.where(position < mine, new, old), longer, so_far)

    return lax.fori_loop(0, count - 1, prefix_hop, so_far)


def carried_in(shard, axis, combine, identity):
    length, position = (lax.axis_size(axis), lax.axis_index(axis))
    everything = jax.tree.map(
        lambda part, kind: lax.all_gather(part.astype(kind), axis),
        shard,
        jax.tree.map(lambda a: jnp.bfloat16 if a.dtype == jnp.float32 else a.dtype, shard),
    )
    start = jax.tree.map(
        lambda part, zero: jnp.broadcast_to(jnp.asarray(zero, part.dtype), part.shape),
        shard,
        identity,
    )

    def carried_hop(k, before):
        at = length - 1 - k
        reached = at > position
        new = combine(
            before, jax.tree.map(lambda part, own: part[at].astype(own.dtype), everything, shard)
        )
        return jax.tree.map(lambda a, b: jnp.where(reached, a, b), new, before)

    return lax.fori_loop(0, length, carried_hop, start)


def shortened(shard):

    def short(part):
        return part.astype(jnp.bfloat16) if part.dtype == jnp.float32 else part

    return jax.tree.map(short, shard)


def silu_grad(pre_act):
    sigmoid_v = jax.nn.sigmoid(pre_act)
    return sigmoid_v * (1.0 + pre_act * (1.0 - sigmoid_v))


def per_channel(head_part, channels):
    return jnp.repeat(head_part, channels // head_part.shape[-1], axis=-1)


def line_form(head_lines, channels):
    return per_channel(head_lines.transpose(1, 2, 0), channels)


def carry_on(log_lines, state):
    return per_channel(jnp.exp(log_lines), state.shape[2])[:, None, :] * state


def prepare(log_decay):
    length = log_decay.shape[2]
    causal = jnp.arange(length)[:, None] >= jnp.arange(length)[None, :]
    running = jnp.einsum(
        "glk,tk->glt", log_decay, causal.astype(log_decay.dtype), precision=PRECISE
    )
    whole_log = running[:, :, -1]
    log_gaps = running[:, :, :, None] - running[:, :, None, :]
    decay_mat = jnp.where(causal, jnp.exp(jnp.where(causal, log_gaps, 0.0)), 0.0)
    return (running, whole_log, decay_mat)


def chain_link(earlier, later):
    return (earlier[0] + later[0], carry_on(later[0], earlier[1]) + later[1])


def split_heads(lines, head_count):
    line_count, length, channels = lines.shape
    return lines.reshape(line_count, length, head_count, channels // head_count)


def local_summary(inputs, key_vecs, prepared):
    running, whole_log, decay_mat = prepared
    to_end = line_form(jnp.exp(whole_log[:, :, None] - running), inputs.shape[2])
    fresh = jnp.einsum("ltc,ltn->lnc", inputs * to_end, key_vecs, precision=PRECISE)
    return (whole_log.T, fresh)


def local_return(query_vecs, prepared, upstream):
    running, whole_log, decay_mat = prepared
    from_start = line_form(jnp.exp(running), upstream.shape[2])
    backward = jnp.einsum("ltc,ltn->lnc", upstream * from_start, query_vecs, precision=PRECISE)
    return (whole_log.T, backward)


def local_outputs(inputs, key_vecs, query_vecs, prepared, incoming):
    running, whole_log, decay_mat = prepared
    head_count = decay_mat.shape[0]
    line_count, length, channels = inputs.shape
    scores = jnp.einsum("ltn,lkn->ltk", query_vecs, key_vecs, precision=PRECISE)
    within = jnp.einsum(
        "gltk,lkgp->ltgp",
        decay_mat * scores[None],
        split_heads(inputs, head_count),
        precision=PRECISE,
    )
    within = within.reshape(line_count, length, channels)
    carried = jnp.einsum("ltn,lnc->ltc", query_vecs, incoming, precision=PRECISE)
    return within + carried * line_form(jnp.exp(running), channels)


def local_grads(inputs, key_vecs, query_vecs, prepared, incoming, returning, upstream):
    running, whole_log, decay_mat = prepared
    head_count = decay_mat.shape[0]
    line_count, length, channels = inputs.shape
    from_start = line_form(jnp.exp(running), channels)
    to_end = line_form(jnp.exp(whole_log[:, :, None] - running), channels)
    scores = jnp.einsum("ltn,lkn->ltk", query_vecs, key_vecs, precision=PRECISE)
    heads_up = split_heads(upstream, head_count)
    heads_in = split_heads(inputs, head_count)
    grad_inputs = jnp.einsum(
        "gltk,ltgp->lkgp", decay_mat * scores[None], heads_up, precision=PRECISE
    ).reshape(line_count, length, channels)
    grad_inputs = (
        grad_inputs + jnp.einsum("lnc,lkn->lkc", returning, key_vecs, precision=PRECISE) * to_end
    )
    mixed = jnp.einsum("ltgp,lkgp->gltk", heads_up, heads_in, precision=PRECISE) * decay_mat
    grad_keys = jnp.einsum("gltk,ltn->lkn", mixed, query_vecs, precision=PRECISE)
    grad_keys = grad_keys + jnp.einsum(
        "lkc,lnc->lkn", inputs * to_end, returning, precision=PRECISE
    )
    grad_queries = jnp.einsum("gltk,lkn->ltn", mixed, key_vecs, precision=PRECISE)
    grad_queries = grad_queries + jnp.einsum(
        "ltc,lnc->ltn", upstream * from_start, incoming, precision=PRECISE
    )
    return (grad_inputs, grad_keys, grad_queries)


def shards(
    patches, mask_token, masked, tissue, in_weight, out_weight, row_decay, col_decay, cotangent
):
    grid_rows, grid_cols, feat_width = patches.shape
    tok_count = grid_rows * grid_cols
    chosen = (masked == 1)[:, :, None]
    present = tissue.astype(jnp.bfloat16)[:, :, None]
    model_in = jnp.where(chosen, mask_token[None, None, :], patches) * present
    flat_in = model_in.reshape(tok_count, feat_width)
    inner_width = E
    half_width = inner_width // 2
    state_size = N
    number_of_heads = HEADS // 2
    offset = 2 * inner_width
    full_in, full_out = (
        lax.all_gather(in_weight, "grow", axis=1, tiled=True),
        lax.all_gather(out_weight, "grow", axis=1, tiled=True),
    )
    projected = lax.dot_general(
        flat_in, full_in, (((1,), (1,)), ((), ())), preferred_element_type=jnp.float32
    )
    proj_bf = projected.astype(jnp.bfloat16)
    pre_values = proj_bf[:, :inner_width].astype(jnp.float32)
    gate_pre = proj_bf[:, inner_width:offset].astype(jnp.float32)
    key_rows = (
        proj_bf[:, offset : offset + state_size]
        .astype(jnp.float32)
        .reshape(grid_rows, grid_cols, state_size)
    )
    query_rows = (
        proj_bf[:, offset + state_size : offset + 2 * state_size]
        .astype(jnp.float32)
        .reshape(grid_rows, grid_cols, state_size)
    )
    key_cols = (
        proj_bf[:, offset + 2 * state_size : offset + 3 * state_size]
        .astype(jnp.float32)
        .reshape(grid_rows, grid_cols, state_size)
        .transpose(1, 0, 2)
    )
    query_cols = (
        proj_bf[:, offset + 3 * state_size : offset + 4 * state_size]
        .astype(jnp.float32)
        .reshape(grid_rows, grid_cols, state_size)
        .transpose(1, 0, 2)
    )
    values = jax.nn.silu(pre_values)
    row_inputs = values[:, :half_width].reshape(grid_rows, grid_cols, half_width)
    col_inputs = values[:, half_width:].reshape(grid_rows, grid_cols, half_width).transpose(1, 0, 2)
    row_prep = prepare(row_decay)
    col_prep = prepare(col_decay.transpose(0, 2, 1))
    row_zero = (
        jnp.zeros((grid_rows, number_of_heads), jnp.float32),
        jnp.zeros((grid_rows, state_size, half_width), jnp.float32),
    )
    col_zero = (
        jnp.zeros((grid_cols, number_of_heads), jnp.float32),
        jnp.zeros((grid_cols, state_size, half_width), jnp.float32),
    )
    row_entry = prefix(local_summary(row_inputs, key_rows, row_prep), "gcol", chain_link, row_zero)[
        1
    ]
    grow_size = lax.axis_size("grow")
    my_block = lax.axis_index("grow")
    parts_in, parts_key, parts_log = (
        lax.all_gather(
            proj_bf[:, half_width:inner_width].reshape(grid_rows, grid_cols, half_width),
            "grow",
            axis=0,
            tiled=True,
        ),
        lax.all_gather(
            proj_bf[:, offset + 2 * state_size : offset + 3 * state_size].reshape(
                grid_rows, grid_cols, state_size
            ),
            "grow",
            axis=0,
            tiled=True,
        ),
        lax.all_gather(
            col_decay.transpose(1, 0, 2).astype(jnp.bfloat16), "grow", axis=0, tiled=True
        ).astype(jnp.float32),
    )
    col_entry = col_zero[1]
    for block_idx in range(grow_size):
        lower_row = block_idx * grid_rows
        piece_in = jax.nn.silu(
            parts_in[lower_row : lower_row + grid_rows].astype(jnp.float32)
        ).transpose(1, 0, 2)
        piece_keys = (
            parts_key[lower_row : lower_row + grid_rows].astype(jnp.float32).transpose(1, 0, 2)
        )
        piece_log = parts_log[lower_row : lower_row + grid_rows].transpose(1, 2, 0)
        whole_log, piece_state = local_summary(piece_in, piece_keys, prepare(piece_log))
        moved = carry_on(whole_log, col_entry) + piece_state
        col_entry = jnp.where(block_idx < my_block, moved, col_entry)
    row_out = local_outputs(row_inputs, key_rows, query_rows, row_prep, row_entry)
    col_out = local_outputs(col_inputs, key_cols, query_cols, col_prep, col_entry).transpose(
        1, 0, 2
    )
    mixed = jnp.concatenate(
        [row_out.reshape(tok_count, half_width), col_out.reshape(tok_count, half_width)], axis=1
    )
    gate_act = jax.nn.silu(gate_pre)
    head_size = inner_width // HEADS
    gated = (mixed * gate_act).reshape(tok_count, HEADS, head_size)
    inv_rms = lax.rsqrt(jnp.mean(gated * gated, axis=2, keepdims=True) + EPSILON)
    normed = gated * inv_rms
    normed_bf = normed.reshape(tok_count, inner_width).astype(jnp.bfloat16)
    grad_out = (cotangent * masked.astype(jnp.bfloat16)[:, :, None]).reshape(tok_count, feat_width)
    total_patches = tok_count * lax.axis_size("gcol") * lax.axis_size("grow")
    weight_sum = lax.psum_scatter(
        lax.dot_general(
            grad_out, normed_bf, (((0,), (0,)), ((), ())), preferred_element_type=jnp.float32
        ),
        ("gcol", "grow"),
        scatter_dimension=0,
        tiled=True,
    )
    out_weight_grad = weight_sum * (1.0 / math.sqrt(total_patches))
    grad_normed_bf = jnp.dot(grad_out, full_out, preferred_element_type=jnp.float32).astype(
        jnp.bfloat16
    )
    grad_normed = lax.optimization_barrier(grad_normed_bf).astype(jnp.float32)
    grad_normed = grad_normed.reshape(tok_count, HEADS, head_size)
    grad_gated = inv_rms * (
        grad_normed - normed * jnp.mean(grad_normed * normed, axis=2, keepdims=True)
    )
    grad_gated = grad_gated.reshape(tok_count, inner_width)
    grad_mixed = grad_gated * gate_act
    grad_gate = grad_gated * mixed * silu_grad(gate_pre)
    row_up = grad_mixed[:, :half_width].reshape(grid_rows, grid_cols, half_width)
    col_up = grad_mixed[:, half_width:].reshape(grid_rows, grid_cols, half_width).transpose(1, 0, 2)
    row_exit = carried_in(local_return(query_rows, row_prep, row_up), "gcol", chain_link, row_zero)[
        1
    ]
    parts_up, parts_query = (
        lax.all_gather(
            shortened(grad_mixed[:, half_width:].reshape(grid_rows, grid_cols, half_width)),
            "grow",
            axis=0,
            tiled=True,
        ),
        lax.all_gather(
            proj_bf[:, offset + 3 * state_size : offset + 4 * state_size].reshape(
                grid_rows, grid_cols, state_size
            ),
            "grow",
            axis=0,
            tiled=True,
        ),
    )
    col_exit = col_zero[1]
    for block_idx in reversed(range(grow_size)):
        lower_row = block_idx * grid_rows
        piece_up = parts_up[lower_row : lower_row + grid_rows].transpose(1, 0, 2)
        piece_queries = (
            parts_query[lower_row : lower_row + grid_rows].astype(jnp.float32).transpose(1, 0, 2)
        )
        piece_log = parts_log[lower_row : lower_row + grid_rows].transpose(1, 2, 0)
        whole_log, piece_back = local_return(piece_queries, prepare(piece_log), piece_up)
        moved = carry_on(whole_log, col_exit) + piece_back
        col_exit = jnp.where(block_idx > my_block, moved, col_exit)
    grad_row_in, grad_row_key, grad_row_query = local_grads(
        row_inputs, key_rows, query_rows, row_prep, row_entry, row_exit, row_up
    )
    grad_col_in, grad_col_key, grad_col_query = local_grads(
        col_inputs, key_cols, query_cols, col_prep, col_entry, col_exit, col_up
    )
    grad_values = jnp.concatenate(
        [
            grad_row_in.reshape(tok_count, half_width),
            grad_col_in.transpose(1, 0, 2).reshape(tok_count, half_width),
        ],
        axis=1,
    )
    grad_proj = jnp.concatenate(
        [
            grad_values * silu_grad(pre_values),
            grad_gate,
            grad_row_key.reshape(tok_count, state_size),
            grad_row_query.reshape(tok_count, state_size),
            grad_col_key.transpose(1, 0, 2).reshape(tok_count, state_size),
            grad_col_query.transpose(1, 0, 2).reshape(tok_count, state_size),
        ],
        axis=1,
    ).astype(jnp.bfloat16)
    keep_mask = present * (1 - masked).astype(jnp.bfloat16)[:, :, None]
    grad_model_in = jnp.dot(grad_proj, full_in, preferred_element_type=jnp.float32).reshape(
        grid_rows, grid_cols, feat_width
    )
    patch_grad = (grad_model_in * keep_mask).astype(jnp.bfloat16)
    return (patch_grad, out_weight_grad)


MESH = pl.DeviceIdType.MESH
NT = (((1,), (1,)), ((), ()))
NN = (((1,), (0,)), ((), ()))
TN = (((0,), (0,)), ((), ()))


def mm(a, b, dims):
    return lax.dot_general(a, b, dims, preferred_element_type=jnp.float32)


def layer_kernel(
    chips, rows, scale,
    patch_hbm, token_hbm, cot_hbm, hidden_hbm, present_hbm, rdec_hbm, cdec_hbm, w_hbm, wout_hbm,
    pg_ref, out_ref,
    patch_ref, token_ref, cot_ref, hidden_ref, present_ref, rdec_ref, cdec_ref, in_sem,
    xs, gs, rd, cd, xb, gb, db, wa, wb, wout, u_s, z_s, gn_s, bc_s, normed_s, y_s, mat_s, dec_s, gp, grow, gcol,
    xsend, wgo, xr, zs, zr,
    x_send, x_recv, g_send, g_recv, d_send, d_recv, w_sem, l_sem,
    gp_send, gp_recv, xr_send, xr_recv, z_send, z_recv,
):
    k, c = lax.axis_index("gcol"), lax.axis_index("grow")
    depth = chips // 2
    zi, xi = k // 2, lax.rem(k, 2)
    cols, feat = xs.shape[1], xs.shape[2]
    toks = chips * cols
    half, part = wout.shape[1], wa.shape[1]
    total = 2 * chips

    load_w = pltpu.make_async_copy(w_hbm, wa, l_sem.at[0])
    load_o = pltpu.make_async_copy(wout_hbm, wout, l_sem.at[1])
    loads = [
        pltpu.make_async_copy(src, dst, in_sem.at[i])
        for i, (src, dst) in enumerate(
            (
                (hidden_hbm, hidden_ref), (present_hbm, present_ref), (token_hbm, token_ref),
                (patch_hbm, patch_ref), (rdec_hbm, rdec_ref), (cdec_hbm, cdec_ref), (cot_hbm, cot_ref),
            )
        )
    ]
    for copy in loads:
        copy.start()
    load_w.start()
    load_o.start()

    me = 2 * k + c
    barrier = pltpu.get_barrier_semaphore()
    for d in range(1, total):
        to = lax.rem(me + d, total)
        pl.semaphore_signal(
            barrier, inc=1, device_id={"gcol": to // 2, "grow": lax.rem(to, 2)}, device_id_type=MESH
        )

    def remote(src, dst, s, r, chip, core):
        return pltpu.make_async_remote_copy(
            src_ref=src, dst_ref=dst, send_sem=s, recv_sem=r,
            device_id={"gcol": chip, "grow": core}, device_id_type=MESH,
        )

    for copy in loads[:-1]:
        copy.wait()
    square = (cols, cols)
    eye = lax.broadcasted_iota(jnp.int32, square, 0) == lax.broadcasted_iota(jnp.int32, square, 1)
    eye = eye.astype(jnp.float32)
    hidden_t = mm(eye, hidden_ref[...].astype(jnp.float32), NT)
    present_t = mm(eye, present_ref[...].astype(jnp.float32), NT)
    token = token_ref[...].reshape(1, feat).astype(jnp.float32)
    for i in range(rows):
        hidden, present = hidden_t[:, i : i + 1], present_t[:, i : i + 1]
        chosen = jnp.where(hidden > 0.5, token, patch_ref[i].astype(jnp.float32))
        xs[i] = (chosen * present).astype(jnp.bfloat16)
        rd[i] = rdec_ref[:, i, :]
        cd[i] = cdec_ref[:, i, :]

    streams = (
        (xs, xs, xb, x_send, x_recv),
        (rd, cd, db, d_send, d_recv),
        (gs, gs, gb, g_send, g_recv),
    )

    def row_out(stream, i):
        row_src, _, dst, s, r = stream
        return remote(row_src.at[i], dst.at[k], s.at[i], r.at[k], rows * c + i, 0)

    def col_out(stream):
        _, col_src, dst, s, r = stream
        return remote(col_src, dst.at[pl.ds(0, rows)], s.at[rows], r.at[chips], k, 1)

    def row_in(stream, src):
        row_src, _, dst, s, r = stream
        return remote(row_src.at[0], dst.at[src], s.at[0], r.at[src], k, 1 - c)

    def col_in(stream):
        _, col_src, dst, s, r = stream
        return remote(col_src, dst.at[pl.ds(0, rows)], s.at[rows], r.at[chips], k, 1 - c)

    def launch(stream):
        for i in range(rows):

            @pl.when(jnp.logical_or(c == 1, k != i))
            def _():
                row_out(stream, i).start()

        @pl.when(c == 0)
        def _():
            col_out(stream).start()

    def arrive(stream):
        @pl.when(c == 0)
        def _():
            for d in range(1, chips):
                row_in(stream, lax.rem(k + d, chips)).wait_recv()

            @pl.when(k >= rows)
            def _():
                row_in(stream, k).wait_recv()

        @pl.when(c == 1)
        def _():
            col_in(stream).wait_recv()

    def drain(stream):
        for i in range(rows):

            @pl.when(jnp.logical_or(c == 1, k != i))
            def _():
                row_out(stream, i).wait_send()

        @pl.when(c == 0)
        def _():
            col_out(stream).wait_send()

    pl.semaphore_wait(barrier, total - 1)
    weights = remote(w_hbm, wb, w_sem.at[0], w_sem.at[1], k, 1 - c)
    launch(streams[0])
    launch(streams[1])
    weights.start()
    loads[-1].wait()
    for i in range(rows):
        gs[i] = (cot_ref[i].astype(jnp.float32) * hidden_t[:, i : i + 1]).astype(jnp.bfloat16)
    launch(streams[2])

    for row_src, col_src, dst, _, _ in streams:

        @pl.when(c == 1)
        def _():
            dst[pl.ds(rows, rows)] = col_src[...]

        for i in range(rows):

            @pl.when(jnp.logical_and(c == 0, k == i))
            def _():
                dst[i] = row_src[i]

    t_at = lax.broadcasted_iota(jnp.int32, (toks, toks), 0)
    k_at = lax.broadcasted_iota(jnp.int32, (toks, toks), 1)
    step = jnp.where(c == 0, 1, cols)
    mask = jnp.logical_and(t_at >= k_at, lax.rem(t_at, step) == lax.rem(k_at, step))
    low = lax.broadcasted_iota(jnp.int32, (toks, 128), 1) < N

    arrive(streams[1])
    ones = mask.astype(jnp.float32)
    dec = jnp.concatenate([db[i] for i in range(chips)], axis=1)
    run_s = lax.dot_general(ones, dec, NT, precision=PRECISE, preferred_element_type=jnp.float32)
    run_l = lax.dot_general(dec, ones, NT, precision=PRECISE, preferred_element_type=jnp.float32)
    heads = dec.shape[0]
    for h in range(heads):
        gap = run_s[:, h : h + 1] - run_l[h : h + 1, :]
        dec_s[h] = jnp.where(mask, jnp.exp(jnp.minimum(gap, 0.0)), 0.0)

    load_w.wait()
    arrive(streams[0])
    mine, rest = pl.multiple_of(c * part, part), pl.multiple_of((1 - c) * part, part)
    own = xb[:, :, pl.ds(mine, part)].reshape(toks, part)
    oth = xb[:, :, pl.ds(rest, part)].reshape(toks, part)
    pieces = ((u_s, c * half, half), (z_s, 2 * half + c * half, half), (bc_s, 4 * half + c * 2 * N, 2 * N))
    partial = [
        mm(own, wa[pl.ds(pl.multiple_of(start, 128), size), :], NT) for _, start, size in pieces
    ]
    weights.wait_recv()
    for (dst, start, size), first in zip(pieces, partial):
        second = mm(oth, wb[pl.ds(pl.multiple_of(start, 128), size), :], NT)
        dst[...] = (first + second).astype(jnp.bfloat16)

    b_bf, c_bf = bc_s[:, :N], bc_s[:, N:]
    scores = mm(c_bf, b_bf, NT)

    def per_head(x):
        first = jnp.sum(jnp.where(low, x, 0.0), axis=1, keepdims=True)
        second = jnp.sum(jnp.where(low, 0.0, x), axis=1, keepdims=True)
        return jnp.where(low, first, second) * (1.0 / N)

    def norm(p):
        cols_p = slice(p * 128, (p + 1) * 128)
        z = z_s[:, cols_p].astype(jnp.float32)
        sig_z = 1.0 / (1.0 + jnp.exp(-z))
        y = y_s[:, cols_p]
        gated = y * (z * sig_z)
        inv = lax.rsqrt(per_head(gated * gated) + EPSILON)
        return cols_p, z, sig_z, y, inv, gated * inv

    for p in range(half // 128):
        cols_p = slice(p * 128, (p + 1) * 128)
        u = u_s[:, cols_p].astype(jnp.float32)
        val_bf = (u / (1.0 + jnp.exp(-u))).astype(jnp.bfloat16)
        for h in (2 * p, 2 * p + 1):
            mat_s[h] = (dec_s[h] * scores).astype(jnp.bfloat16)
        y_s[:, cols_p] = jnp.where(
            low, mm(mat_s[2 * p], val_bf, NN), mm(mat_s[2 * p + 1], val_bf, NN)
        )
        normed_s[:, cols_p] = norm(p)[-1].astype(jnp.bfloat16)

    load_o.wait()
    arrive(streams[2])

    def weight_block(chip):
        at = pl.ds(pl.multiple_of(chip * 128, 128), 128)
        return mm(gb[:, :, at].reshape(toks, 128), normed_s[...], TN)

    def across(q):
        return remote(xsend.at[q], xr.at[q], xr_send.at[q], xr_recv.at[q], 2 * zi + 1 - xi, c)

    far = sorted(range(1, depth), key=lambda j: -min(j, depth - j)) + [0]
    order = [lax.rem(zi + j, depth) for j in far]
    for q in order:
        xsend[q] = weight_block(2 * q + 1 - xi).astype(jnp.bfloat16)
        across(q).start()

    grads = gb[...].reshape(toks, feat)
    gn_s[...] = mm(grads, wout[...], NN).astype(jnp.bfloat16)
    d_scores = jnp.zeros((toks, toks), jnp.float32)
    for p in range(half // 128):
        cols_p, z, sig_z, y, inv, normed = norm(p)
        u = u_s[:, cols_p].astype(jnp.float32)
        sig_u = 1.0 / (1.0 + jnp.exp(-u))
        val_bf = (u * sig_u).astype(jnp.bfloat16)
        gn = gn_s[:, cols_p].astype(jnp.float32)
        gg = inv * (gn - normed * per_head(gn * normed))
        dy = gg * (z * sig_z)
        dz = gg * y * (sig_z * (1.0 + z * (1.0 - sig_z)))
        dy_bf = dy.astype(jnp.bfloat16)
        dv = jnp.where(low, mm(mat_s[2 * p], dy_bf, TN), mm(mat_s[2 * p + 1], dy_bf, TN))
        du = dv * (sig_u * (1.0 + u * (1.0 - sig_u)))
        gp[:, :, cols_p] = du.astype(jnp.bfloat16).reshape(chips, cols, 128)
        gp[:, :, half + p * 128 : half + (p + 1) * 128] = dz.astype(jnp.bfloat16).reshape(
            chips, cols, 128
        )
        zero = jnp.zeros_like(dy)
        d_scores += dec_s[2 * p] * mm(jnp.where(low, dy, zero).astype(jnp.bfloat16), val_bf, NT)
        d_scores += dec_s[2 * p + 1] * mm(jnp.where(low, zero, dy).astype(jnp.bfloat16), val_bf, NT)
    ds_bf = d_scores.astype(jnp.bfloat16)
    d_bc = jnp.concatenate([mm(ds_bf, c_bf, TN), mm(ds_bf, b_bf, NN)], axis=1)
    gp[:, :, 2 * half :] = d_bc.astype(jnp.bfloat16).reshape(chips, cols, 2 * N)

    home, slot = k // rows, lax.rem(k, rows)

    def row_back(chip):
        return remote(gp.at[chip], grow.at[slot], gp_send.at[chip], gp_recv.at[slot], chip, home)

    def col_back(core):
        lo = pl.ds(0, rows)
        return remote(gp.at[lo], gcol, gp_send.at[chips], gp_recv.at[rows], k, core)

    @pl.when(c == 0)
    def _():
        for d in sorted(range(1, chips), key=lambda j: -min(j, chips - j)):
            row_back(lax.rem(k + d, chips)).start()

        @pl.when(home == 1)
        def _():
            row_back(k).start()

        for i in range(rows):

            @pl.when(k == i)
            def _():
                grow[i] = gp[i]

    @pl.when(c == 1)
    def _():
        col_back(0).start()
        gcol[...] = gp[pl.ds(rows, rows)]

    for q in range(depth):
        wgo[q] = weight_block(2 * q + xi)

    def along(q, core):
        return remote(
            zs.at[q, core], zr.at[zi, c], z_send.at[2 * q + core], z_recv.at[2 * zi + c], 2 * q + xi, core
        )

    def forward(q):
        across(q).wait_recv()
        both = wgo[q] + xr[q].astype(jnp.float32)
        wgo[q] = both
        zs[q] = both.astype(jnp.bfloat16).reshape(2, both.shape[0] // 2, both.shape[1])

    def forward_far(q):
        forward(q)
        for core in range(2):
            along(q, core).start()

    def back_project(src, g, w_ref):
        flat = src[...].reshape(rows * cols, 2 * half + 2 * N)
        acc = mm(flat[:, :half], w_ref[g * half : (g + 1) * half, :], NN)
        acc += mm(flat[:, half : 2 * half], w_ref[(2 + g) * half : (3 + g) * half, :], NN)
        at = 4 * half + g * 2 * N
        return acc + mm(flat[:, 2 * half :], w_ref[at : at + 2 * N, :], NN)

    forward_far(order[0])

    @pl.when(c == 0)
    def _():
        col_back(1).wait_recv()

    col_part = [back_project(gcol, 1, w_ref) for w_ref in (wa, wb)]
    for q in order[1:-1]:
        forward_far(q)
    forward(zi)
    along(zi, 1 - c).start()

    for i in range(rows):

        @pl.when(jnp.logical_or(c == 1, k != i))
        def _():
            remote(gp.at[0], grow.at[i], gp_send.at[0], gp_recv.at[i], k, 1 - c).wait_recv()

    for w_ref, at, first in ((wa, mine, col_part[0]), (wb, rest, col_part[1])):
        acc = (first + back_project(grow, 0, w_ref)).reshape(rows, cols, part)
        for i in range(rows):
            keep = present_t[:, i : i + 1] * (1.0 - hidden_t[:, i : i + 1])
            pg_ref[i, :, pl.ds(at, part)] = (acc[i] * keep).astype(pg_ref.dtype)

    for q in order[:-1]:
        for core in range(2):
            remote(zs.at[0, 0], zr.at[q, core], z_send.at[0], z_recv.at[2 * q + core], k, 1 - c).wait_recv()
    remote(zs.at[0, 0], zr.at[zi, 1 - c], z_send.at[0], z_recv.at[2 * zi + 1 - c], k, 1 - c).wait_recv()
    zr[zi, c] = zs[zi, c]
    for core in range(2):
        acc = zr[0, core].astype(jnp.float32)
        for q in range(1, depth):
            acc += zr[q, core].astype(jnp.float32)
        out_ref[:, core * half : (core + 1) * half] = acc * scale

    for stream in streams:
        drain(stream)
    weights.wait_send()
    for q in order:
        across(q).wait_send()
    for q in order[:-1]:
        for core in range(2):
            along(q, core).wait_send()
    along(zi, 1 - c).wait_send()

    @pl.when(c == 0)
    def _():
        for d in range(1, chips):
            row_back(lax.rem(k + d, chips)).wait_send()

        @pl.when(home == 1)
        def _():
            row_back(k).wait_send()

    @pl.when(c == 1)
    def _():
        col_back(0).wait_send()


def store_kernel(a_ref, b_ref, a_hbm, b_hbm, sem):
    copies = [
        pltpu.make_async_copy(a_ref, a_hbm, sem.at[0]),
        pltpu.make_async_copy(b_ref, b_hbm, sem.at[1]),
    ]
    for copy in copies:
        copy.start()
    for copy in copies:
        copy.wait()


def owned(
    patches, mask_token, masked, tissue, in_weight, out_weight, row_decay, col_decay, cotangent
):
    rows, cols, feat = patches.shape
    chips = lax.axis_size("gcol")
    toks, heads = chips * cols, row_decay.shape[0]
    half, part = out_weight.shape[1], in_weight.shape[1]
    width = 2 * half + 2 * N
    slab = feat // (2 * chips)
    depth = chips // 2
    bf, fl = jnp.bfloat16, jnp.float32
    vmem, dma = pltpu.VMEM, pltpu.SemaphoreType.DMA
    in_vmem, anywhere = pl.BlockSpec(memory_space=pltpu.VMEM), pl.BlockSpec(memory_space=pltpu.HBM)
    scale = 1.0 / math.sqrt(2 * rows * cols * chips)
    results = pl.pallas_call(
        functools.partial(layer_kernel, chips, rows, scale),
        name="layer",
        out_shape=(vmem(patches.shape, bf), vmem((slab, 2 * half), fl)),
        in_specs=[anywhere] * 9,
        out_specs=(in_vmem, in_vmem),
        scratch_shapes=[
            vmem(patches.shape, bf), vmem(mask_token.shape, bf), vmem(patches.shape, bf),
            vmem(masked.shape, masked.dtype), vmem(tissue.shape, tissue.dtype),
            vmem(row_decay.shape, fl), vmem(col_decay.shape, fl), dma((7,)),
            vmem((rows, cols, feat), bf), vmem((rows, cols, feat), bf),
            vmem((rows, heads, cols), fl), vmem((rows, heads, cols), fl),
            vmem((chips, cols, feat), bf), vmem((chips, cols, feat), bf), vmem((chips, heads, cols), fl),
            vmem(in_weight.shape, bf), vmem(in_weight.shape, bf), vmem(out_weight.shape, bf),
            vmem((toks, half), bf), vmem((toks, half), bf), vmem((toks, half), bf),
            vmem((toks, 2 * N), bf), vmem((toks, half), bf), vmem((toks, half), fl),
            vmem((heads, toks, toks), bf), vmem((heads, toks, toks), fl),
            vmem((chips, cols, width), bf), vmem((rows, cols, width), bf), vmem((rows, cols, width), bf),
            vmem((depth, 2 * slab, half), bf), vmem((depth, 2 * slab, half), fl),
            vmem((depth, 2 * slab, half), bf), vmem((depth, 2, slab, half), bf),
            vmem((depth, 2, slab, half), bf),
            dma((rows + 1,)), dma((chips + 1,)), dma((rows + 1,)), dma((chips + 1,)),
            dma((rows + 1,)), dma((chips + 1,)), dma((2,)), dma((2,)),
            dma((chips + 1,)), dma((rows + 1,)), dma((depth,)), dma((depth,)),
            dma((2 * depth,)), dma((2 * depth,)),
        ],
        compiler_params=pltpu.CompilerParams(
            collective_id=0, has_side_effects=True, vmem_limit_bytes=60 << 20
        ),
    )(
        patches, mask_token, cotangent, masked, tissue, row_decay, col_decay,
        in_weight, out_weight,
    )
    return pl.pallas_call(
        store_kernel,
        name="store",
        out_shape=tuple(jax.ShapeDtypeStruct(r.shape, r.dtype) for r in results),
        in_specs=[in_vmem] * 2,
        out_specs=[anywhere] * 2,
        scratch_shapes=[dma((2,))],
        compiler_params=pltpu.CompilerParams(vmem_limit_bytes=1 << 20),
    )(*results)


def body(*args):
    rows = args[0].shape[0]
    if lax.axis_size("grow") == 2 and lax.axis_size("gcol") == 2 * rows:
        return owned(*args)
    return shards(*args)


def solution(mesh):
    return jax.shard_map(
        body,
        mesh=mesh,
        in_specs=(
            P(("groups", "grow"), "gcol", None),
            P(),
            P(("groups", "grow"), "gcol"),
            P(("groups", "grow"), "gcol"),
            P(None, "grow"),
            P(None, "grow"),
            P(None, ("groups", "grow"), "gcol"),
            P(None, ("groups", "grow"), "gcol"),
            P(("groups", "grow"), "gcol", None),
        ),
        out_specs=(P(("groups", "grow"), "gcol", None), P(("groups", "gcol", "grow"), None)),
        check_vma=False,
    )
```

```python
import functools
import math

import jax
import jax.numpy as jnp
from jax import lax
from jax.experimental import pallas as pl
from jax.experimental.pallas import tpu as pltpu
from jax.sharding import PartitionSpec as P

E = 1024
HEADS = 16
N = 64


EPSILON = 1e-05
PRECISE = lax.Precision.HIGHEST


def prefix(value, axis, join, neutral):
    count, mine = (lax.axis_size(axis), lax.axis_index(axis))
    pieces = jax.tree.map(lambda part: lax.all_gather(part, axis), value)
    so_far = jax.tree.map(
        lambda part, zero: jnp.full_like(part, 0) + jnp.asarray(zero, part.dtype), value, neutral
    )

    def prefix_hop(position, so_far):
        longer = join(so_far, jax.tree.map(lambda part: part[position], pieces))
        return jax.tree.map(lambda new, old: jnp.where(position < mine, new, old), longer, so_far)

    return lax.fori_loop(0, count - 1, prefix_hop, so_far)


def carried_in(shard, axis, combine, identity):
    length, position = (lax.axis_size(axis), lax.axis_index(axis))
    everything = jax.tree.map(
        lambda part, kind: lax.all_gather(part.astype(kind), axis),
        shard,
        jax.tree.map(lambda a: jnp.bfloat16 if a.dtype == jnp.float32 else a.dtype, shard),
    )
    start = jax.tree.map(
        lambda part, zero: jnp.broadcast_to(jnp.asarray(zero, part.dtype), part.shape),
        shard,
        identity,
    )

    def carried_hop(k, before):
        at = length - 1 - k
        reached = at > position
        new = combine(
            before, jax.tree.map(lambda part, own: part[at].astype(own.dtype), everything, shard)
        )
        return jax.tree.map(lambda a, b: jnp.where(reached, a, b), new, before)

    return lax.fori_loop(0, length, carried_hop, start)


def shortened(shard):

    def short(part):
        return part.astype(jnp.bfloat16) if part.dtype == jnp.float32 else part

    return jax.tree.map(short, shard)


def silu_grad(pre_act):
    sigmoid_v = jax.nn.sigmoid(pre_act)
    return sigmoid_v * (1.0 + pre_act * (1.0 - sigmoid_v))


def per_channel(head_part, channels):
    return jnp.repeat(head_part, channels // head_part.shape[-1], axis=-1)


def line_form(head_lines, channels):
    return per_channel(head_lines.transpose(1, 2, 0), channels)


def carry_on(log_lines, state):
    return per_channel(jnp.exp(log_lines), state.shape[2])[:, None, :] * state


def prepare(log_decay):
    length = log_decay.shape[2]
    causal = jnp.arange(length)[:, None] >= jnp.arange(length)[None, :]
    running = jnp.einsum(
        "glk,tk->glt", log_decay, causal.astype(log_decay.dtype), precision=PRECISE
    )
    whole_log = running[:, :, -1]
    log_gaps = running[:, :, :, None] - running[:, :, None, :]
    decay_mat = jnp.where(causal, jnp.exp(jnp.where(causal, log_gaps, 0.0)), 0.0)
    return (running, whole_log, decay_mat)


def chain_link(earlier, later):
    return (earlier[0] + later[0], carry_on(later[0], earlier[1]) + later[1])


def split_heads(lines, head_count):
    line_count, length, channels = lines.shape
    return lines.reshape(line_count, length, head_count, channels // head_count)


def local_summary(inputs, key_vecs, prepared):
    running, whole_log, decay_mat = prepared
    to_end = line_form(jnp.exp(whole_log[:, :, None] - running), inputs.shape[2])
    fresh = jnp.einsum("ltc,ltn->lnc", inputs * to_end, key_vecs, precision=PRECISE)
    return (whole_log.T, fresh)


def local_return(query_vecs, prepared, upstream):
    running, whole_log, decay_mat = prepared
    from_start = line_form(jnp.exp(running), upstream.shape[2])
    backward = jnp.einsum("ltc,ltn->lnc", upstream * from_start, query_vecs, precision=PRECISE)
    return (whole_log.T, backward)


def local_outputs(inputs, key_vecs, query_vecs, prepared, incoming):
    running, whole_log, decay_mat = prepared
    head_count = decay_mat.shape[0]
    line_count, length, channels = inputs.shape
    scores = jnp.einsum("ltn,lkn->ltk", query_vecs, key_vecs, precision=PRECISE)
    within = jnp.einsum(
        "gltk,lkgp->ltgp",
        decay_mat * scores[None],
        split_heads(inputs, head_count),
        precision=PRECISE,
    )
    within = within.reshape(line_count, length, channels)
    carried = jnp.einsum("ltn,lnc->ltc", query_vecs, incoming, precision=PRECISE)
    return within + carried * line_form(jnp.exp(running), channels)


def local_grads(inputs, key_vecs, query_vecs, prepared, incoming, returning, upstream):
    running, whole_log, decay_mat = prepared
    head_count = decay_mat.shape[0]
    line_count, length, channels = inputs.shape
    from_start = line_form(jnp.exp(running), channels)
    to_end = line_form(jnp.exp(whole_log[:, :, None] - running), channels)
    scores = jnp.einsum("ltn,lkn->ltk", query_vecs, key_vecs, precision=PRECISE)
    heads_up = split_heads(upstream, head_count)
    heads_in = split_heads(inputs, head_count)
    grad_inputs = jnp.einsum(
        "gltk,ltgp->lkgp", decay_mat * scores[None], heads_up, precision=PRECISE
    ).reshape(line_count, length, channels)
    grad_inputs = (
        grad_inputs + jnp.einsum("lnc,lkn->lkc", returning, key_vecs, precision=PRECISE) * to_end
    )
    mixed = jnp.einsum("ltgp,lkgp->gltk", heads_up, heads_in, precision=PRECISE) * decay_mat
    grad_keys = jnp.einsum("gltk,ltn->lkn", mixed, query_vecs, precision=PRECISE)
    grad_keys = grad_keys + jnp.einsum(
        "lkc,lnc->lkn", inputs * to_end, returning, precision=PRECISE
    )
    grad_queries = jnp.einsum("gltk,lkn->ltn", mixed, key_vecs, precision=PRECISE)
    grad_queries = grad_queries + jnp.einsum(
        "ltc,lnc->ltn", upstream * from_start, incoming, precision=PRECISE
    )
    return (grad_inputs, grad_keys, grad_queries)


def shards(
    patches, mask_token, masked, tissue, in_weight, out_weight, row_decay, col_decay, cotangent
):
    grid_rows, grid_cols, feat_width = patches.shape
    tok_count = grid_rows * grid_cols
    chosen = (masked == 1)[:, :, None]
    present = tissue.astype(jnp.bfloat16)[:, :, None]
    model_in = jnp.where(chosen, mask_token[None, None, :], patches) * present
    flat_in = model_in.reshape(tok_count, feat_width)
    inner_width = E
    half_width = inner_width // 2
    state_size = N
    number_of_heads = HEADS // 2
    offset = 2 * inner_width
    full_in, full_out = (
        lax.all_gather(in_weight, "grow", axis=1, tiled=True),
        lax.all_gather(out_weight, "grow", axis=1, tiled=True),
    )
    projected = lax.dot_general(
        flat_in, full_in, (((1,), (1,)), ((), ())), preferred_element_type=jnp.float32
    )
    proj_bf = projected.astype(jnp.bfloat16)
    pre_values = proj_bf[:, :inner_width].astype(jnp.float32)
    gate_pre = proj_bf[:, inner_width:offset].astype(jnp.float32)
    key_rows = (
        proj_bf[:, offset : offset + state_size]
        .astype(jnp.float32)
        .reshape(grid_rows, grid_cols, state_size)
    )
    query_rows = (
        proj_bf[:, offset + state_size : offset + 2 * state_size]
        .astype(jnp.float32)
        .reshape(grid_rows, grid_cols, state_size)
    )
    key_cols = (
        proj_bf[:, offset + 2 * state_size : offset + 3 * state_size]
        .astype(jnp.float32)
        .reshape(grid_rows, grid_cols, state_size)
        .transpose(1, 0, 2)
    )
    query_cols = (
        proj_bf[:, offset + 3 * state_size : offset + 4 * state_size]
        .astype(jnp.float32)
        .reshape(grid_rows, grid_cols, state_size)
        .transpose(1, 0, 2)
    )
    values = jax.nn.silu(pre_values)
    row_inputs = values[:, :half_width].reshape(grid_rows, grid_cols, half_width)
    col_inputs = values[:, half_width:].reshape(grid_rows, grid_cols, half_width).transpose(1, 0, 2)
    row_prep = prepare(row_decay)
    col_prep = prepare(col_decay.transpose(0, 2, 1))
    row_zero = (
        jnp.zeros((grid_rows, number_of_heads), jnp.float32),
        jnp.zeros((grid_rows, state_size, half_width), jnp.float32),
    )
    col_zero = (
        jnp.zeros((grid_cols, number_of_heads), jnp.float32),
        jnp.zeros((grid_cols, state_size, half_width), jnp.float32),
    )
    row_entry = prefix(local_summary(row_inputs, key_rows, row_prep), "gcol", chain_link, row_zero)[
        1
    ]
    grow_size = lax.axis_size("grow")
    my_block = lax.axis_index("grow")
    parts_in, parts_key, parts_log = (
        lax.all_gather(
            proj_bf[:, half_width:inner_width].reshape(grid_rows, grid_cols, half_width),
            "grow",
            axis=0,
            tiled=True,
        ),
        lax.all_gather(
            proj_bf[:, offset + 2 * state_size : offset + 3 * state_size].reshape(
                grid_rows, grid_cols, state_size
            ),
            "grow",
            axis=0,
            tiled=True,
        ),
        lax.all_gather(
            col_decay.transpose(1, 0, 2).astype(jnp.bfloat16), "grow", axis=0, tiled=True
        ).astype(jnp.float32),
    )
    col_entry = col_zero[1]
    for block_idx in range(grow_size):
        lower_row = block_idx * grid_rows
        piece_in = jax.nn.silu(
            parts_in[lower_row : lower_row + grid_rows].astype(jnp.float32)
        ).transpose(1, 0, 2)
        piece_keys = (
            parts_key[lower_row : lower_row + grid_rows].astype(jnp.float32).transpose(1, 0, 2)
        )
        piece_log = parts_log[lower_row : lower_row + grid_rows].transpose(1, 2, 0)
        whole_log, piece_state = local_summary(piece_in, piece_keys, prepare(piece_log))
        moved = carry_on(whole_log, col_entry) + piece_state
        col_entry = jnp.where(block_idx < my_block, moved, col_entry)
    row_out = local_outputs(row_inputs, key_rows, query_rows, row_prep, row_entry)
    col_out = local_outputs(col_inputs, key_cols, query_cols, col_prep, col_entry).transpose(
        1, 0, 2
    )
    mixed = jnp.concatenate(
        [row_out.reshape(tok_count, half_width), col_out.reshape(tok_count, half_width)], axis=1
    )
    gate_act = jax.nn.silu(gate_pre)
    head_size = inner_width // HEADS
    gated = (mixed * gate_act).reshape(tok_count, HEADS, head_size)
    inv_rms = lax.rsqrt(jnp.mean(gated * gated, axis=2, keepdims=True) + EPSILON)
    normed = gated * inv_rms
    normed_bf = normed.reshape(tok_count, inner_width).astype(jnp.bfloat16)
    grad_out = (cotangent * masked.astype(jnp.bfloat16)[:, :, None]).reshape(tok_count, feat_width)
    total_patches = tok_count * lax.axis_size("gcol") * lax.axis_size("grow")
    weight_sum = lax.psum_scatter(
        lax.dot_general(
            grad_out, normed_bf, (((0,), (0,)), ((), ())), preferred_element_type=jnp.float32
        ),
        ("gcol", "grow"),
        scatter_dimension=0,
        tiled=True,
    )
    out_weight_grad = weight_sum * (1.0 / math.sqrt(total_patches))
    grad_normed_bf = jnp.dot(grad_out, full_out, preferred_element_type=jnp.float32).astype(
        jnp.bfloat16
    )
    grad_normed = lax.optimization_barrier(grad_normed_bf).astype(jnp.float32)
    grad_normed = grad_normed.reshape(tok_count, HEADS, head_size)
    grad_gated = inv_rms * (
        grad_normed - normed * jnp.mean(grad_normed * normed, axis=2, keepdims=True)
    )
    grad_gated = grad_gated.reshape(tok_count, inner_width)
    grad_mixed = grad_gated * gate_act
    grad_gate = grad_gated * mixed * silu_grad(gate_pre)
    row_up = grad_mixed[:, :half_width].reshape(grid_rows, grid_cols, half_width)
    col_up = grad_mixed[:, half_width:].reshape(grid_rows, grid_cols, half_width).transpose(1, 0, 2)
    row_exit = carried_in(local_return(query_rows, row_prep, row_up), "gcol", chain_link, row_zero)[
        1
    ]
    parts_up, parts_query = (
        lax.all_gather(
            shortened(grad_mixed[:, half_width:].reshape(grid_rows, grid_cols, half_width)),
            "grow",
            axis=0,
            tiled=True,
        ),
        lax.all_gather(
            proj_bf[:, offset + 3 * state_size : offset + 4 * state_size].reshape(
                grid_rows, grid_cols, state_size
            ),
            "grow",
            axis=0,
            tiled=True,
        ),
    )
    col_exit = col_zero[1]
    for block_idx in reversed(range(grow_size)):
        lower_row = block_idx * grid_rows
        piece_up = parts_up[lower_row : lower_row + grid_rows].transpose(1, 0, 2)
        piece_queries = (
            parts_query[lower_row : lower_row + grid_rows].astype(jnp.float32).transpose(1, 0, 2)
        )
        piece_log = parts_log[lower_row : lower_row + grid_rows].transpose(1, 2, 0)
        whole_log, piece_back = local_return(piece_queries, prepare(piece_log), piece_up)
        moved = carry_on(whole_log, col_exit) + piece_back
        col_exit = jnp.where(block_idx > my_block, moved, col_exit)
    grad_row_in, grad_row_key, grad_row_query = local_grads(
        row_inputs, key_rows, query_rows, row_prep, row_entry, row_exit, row_up
    )
    grad_col_in, grad_col_key, grad_col_query = local_grads(
        col_inputs, key_cols, query_cols, col_prep, col_entry, col_exit, col_up
    )
    grad_values = jnp.concatenate(
        [
            grad_row_in.reshape(tok_count, half_width),
            grad_col_in.transpose(1, 0, 2).reshape(tok_count, half_width),
        ],
        axis=1,
    )
    grad_proj = jnp.concatenate(
        [
            grad_values * silu_grad(pre_values),
            grad_gate,
            grad_row_key.reshape(tok_count, state_size),
            grad_row_query.reshape(tok_count, state_size),
            grad_col_key.transpose(1, 0, 2).reshape(tok_count, state_size),
            grad_col_query.transpose(1, 0, 2).reshape(tok_count, state_size),
        ],
        axis=1,
    ).astype(jnp.bfloat16)
    keep_mask = present * (1 - masked).astype(jnp.bfloat16)[:, :, None]
    grad_model_in = jnp.dot(grad_proj, full_in, preferred_element_type=jnp.float32).reshape(
        grid_rows, grid_cols, feat_width
    )
    patch_grad = (grad_model_in * keep_mask).astype(jnp.bfloat16)
    return (patch_grad, out_weight_grad)


MESH = pl.DeviceIdType.MESH
NT = (((1,), (1,)), ((), ()))
NN = (((1,), (0,)), ((), ()))
TN = (((0,), (0,)), ((), ()))


def mm(a, b, dims):
    return lax.dot_general(a, b, dims, preferred_element_type=jnp.float32)


def layer_kernel(
    chips, rows, scale,
    patch_hbm, token_hbm, cot_hbm, hidden_hbm, present_hbm, rdec_hbm, cdec_hbm, w_hbm, wout_hbm,
    pg_ref, out_ref,
    patch_ref, token_ref, cot_ref, hidden_ref, present_ref, rdec_ref, cdec_ref, in_sem,
    ms, mb, rd, cd, db, wa, wb, wout, gb, u_s, z_s, su_s, sz_s, gn_s, bc_s, normed_s, y_s, inv_s, mat_s, dec_s,
    gp, pgs, prow, pcol, xsend, wgo, xr, zs, zc, zr,
    m_send, m_recv, d_send, d_recv, w_send, w_recv, l_sem,
    p_send, p_recv, xr_send, xr_recv, z_send, zc_recv, zr_recv,
):
    k, c = lax.axis_index("gcol"), lax.axis_index("grow")
    depth = chips // 2
    zi, xi = k // 2, lax.rem(k, 2)
    cols = ms.shape[2]
    toks = chips * cols
    feat, half, part = token_ref.shape[0], wout.shape[1], wa.shape[1]
    heads, width = rdec_ref.shape[0], wa.shape[0]
    total = 2 * chips
    slab = feat // chips
    scope = jax.named_scope

    pieces = ((0, 0, half), (2 * half, half, half), (4 * half, 2 * half, 2 * N))

    def packed(ref, core):
        return [
            (ref.at[pl.ds(pl.multiple_of(base + core * size, 128), size)], pl.ds(at, size))
            for base, at, size in pieces
        ]

    loads = [
        pltpu.make_async_copy(src, dst, in_sem.at[i])
        for i, (src, dst) in enumerate(
            (
                (hidden_hbm, hidden_ref), (present_hbm, present_ref), (token_hbm, token_ref),
                (rdec_hbm, rdec_ref), (cdec_hbm, cdec_ref), (patch_hbm, patch_ref), (cot_hbm, cot_ref),
            )
        )
    ]
    for copy in loads:
        copy.start()
    load_w = [
        pltpu.make_async_copy(src, wa.at[at], l_sem.at[i]) for i, (src, at) in enumerate(packed(w_hbm, c))
    ]
    load_o = pltpu.make_async_copy(wout_hbm, wout, l_sem.at[3])
    for copy in load_w:
        copy.start()
    load_o.start()

    me = 2 * k + c
    barrier = pltpu.get_barrier_semaphore()
    for d in range(1, total):
        to = lax.rem(me + d, total)
        pl.semaphore_signal(
            barrier, inc=1, device_id={"gcol": to // 2, "grow": lax.rem(to, 2)}, device_id_type=MESH
        )

    def remote(src, dst, s, r, chip, core):
        return pltpu.make_async_remote_copy(
            src_ref=src, dst_ref=dst, send_sem=s, recv_sem=r,
            device_id={"gcol": chip, "grow": core}, device_id_type=MESH,
        )

    with scope("prep"):
        for copy in loads:
            copy.wait()
        square = (cols, cols)
        eye = lax.broadcasted_iota(jnp.int32, square, 0) == lax.broadcasted_iota(jnp.int32, square, 1)
        eye = eye.astype(jnp.float32)
        hidden_f, present_f = hidden_ref[...].astype(jnp.float32), present_ref[...].astype(jnp.float32)
        hidden_t, present_t = mm(eye, hidden_f, NT), mm(eye, present_f, NT)
        for i in range(rows):
            hidden, present = hidden_t[:, i : i + 1], present_t[:, i : i + 1]
            for f in range(2):
                at = slice(f * part, (f + 1) * part)
                visible = patch_ref[i, :, at].astype(jnp.float32) * present
                either = jnp.where(hidden > 0.5, cot_ref[i, :, at].astype(jnp.float32), visible)
                ms[f, i] = either.astype(jnp.bfloat16)
            blank = jnp.zeros((rd.shape[1] - heads - 2, cols), jnp.float32)
            flags = jnp.concatenate([hidden_f[i : i + 1], present_f[i : i + 1], blank], axis=0)
            for dst, src in ((rd, rdec_ref), (cd, cdec_ref)):
                dst[i, :heads] = src[:, i, :]
                dst[i, heads:] = flags

    def m_row(f, j):
        i = lax.rem(0*k + j, rows)
        return i, remote(
            ms.at[f, i], mb.at[f, k], m_send.at[f, j], m_recv.at[f, k], rows * c + i, 0
        )

    def m_col(f):
        return remote(
            ms.at[f], mb.at[f, pl.ds(0, rows)], m_send.at[f, rows], m_recv.at[f, chips], k, 1
        )

    def d_row(j):
        i = lax.rem(0*k + j, rows)
        return i, remote(rd.at[i], db.at[k], d_send.at[j], d_recv.at[k], rows * c + i, 0)

    def d_col():
        return remote(cd, db.at[pl.ds(0, rows)], d_send.at[rows], d_recv.at[chips], k, 1)

    def not_me(i):
        return jnp.logical_or(c == 1, k != i)

    def each_row(send, act):
        for j in range(rows):
            i, copy = send(j)

            @pl.when(not_me(i))
            def _():
                act(copy)

    def arrive(row_from, from_core_0):
        @pl.when(c == 0)
        def _():
            for d in range(1, chips):
                row_from(lax.rem(k + d, chips)).wait_recv()

            @pl.when(k >= rows)
            def _():
                row_from(k).wait_recv()

        @pl.when(c == 1)
        def _():
            from_core_0.wait_recv()

    def start(copy):
        copy.start()

    def wait_send(copy):
        copy.wait_send()

    w_out = [
        remote(src, wb.at[at], w_send.at[i], w_recv.at[i], k, 1 - c)
        for i, (src, at) in enumerate(packed(w_hbm, 1 - c))
    ]
    t_at = lax.broadcasted_iota(jnp.int32, (toks, toks), 0)
    k_at = lax.broadcasted_iota(jnp.int32, (toks, toks), 1)
    step = jnp.where(c == 0, 1, cols)
    mask = jnp.logical_and(t_at >= k_at, lax.rem(t_at, step) == lax.rem(k_at, step))
    low = lax.broadcasted_iota(jnp.int32, (toks, 128), 1) < N
    same = (128, 128)
    head_of = [lax.broadcasted_iota(jnp.int32, same, d) // N for d in range(2)]
    averages = jnp.where(head_of[0] == head_of[1], 1.0 / N, 0.0).astype(jnp.bfloat16)

    with scope("barrier_wait"):
        pl.semaphore_wait(barrier, total - 1)
    with scope("launch"):
        each_row(d_row, start)

        @pl.when(c == 0)
        def _():
            d_col().start()

        for f in range(2):
            each_row(functools.partial(m_row, f), start)

        @pl.when(c == 0)
        def _():
            m_col(1).start()
            m_col(0).start()

        for copy in w_out:
            copy.start()

        @pl.when(c == 1)
        def _():
            db[pl.ds(rows, rows)] = cd[...]
            for f in range(2):
                mb[f, pl.ds(rows, rows)] = ms[f]

        for i in range(rows):

            @pl.when(jnp.logical_and(c == 0, k == i))
            def _():
                db[i] = rd[i]
                for f in range(2):
                    mb[f, i] = ms[f, i]

    with scope("arrive_decay"):
        arrive(lambda src: remote(rd.at[0], db.at[src], d_send.at[0], d_recv.at[src], k, 1 - c), d_col())
    with scope("decay"):
        ones = mask.astype(jnp.float32)
        dec = jnp.concatenate([db[i] for i in range(chips)], axis=1)
        run_s = lax.dot_general(ones, dec, NT, precision=PRECISE, preferred_element_type=jnp.float32)
        run_l = lax.dot_general(dec, ones, NT, precision=PRECISE, preferred_element_type=jnp.float32)
        for h in range(heads):
            gap = run_s[:, h : h + 1] - run_l[h : h + 1, :]
            dec_s[h] = jnp.where(mask, jnp.exp(jnp.minimum(gap, 0.0)), 0.0)
        unit = (t_at == k_at).astype(jnp.float32)
        flags_t = mm(unit, dec[heads:], NT)
        tok_hidden, tok_present = flags_t[:, 0:1] > 0.5, flags_t[:, 1:2]

    with scope("load_w"):
        for copy in load_w:
            copy.wait()
        load_o.wait()

    def unpack(f):
        at = pl.ds(pl.multiple_of(f * part, part), part)
        either = mb[f].reshape(toks, part)
        token = token_ref[at].reshape(1, part).astype(jnp.float32)
        hidden_in = token * tok_present
        wide = either.astype(jnp.float32)
        gb[:, at] = jnp.where(tok_hidden, wide, 0.0).astype(jnp.bfloat16)
        return jnp.where(tok_hidden, hidden_in, wide).astype(jnp.bfloat16)

    def arrive_m(f):
        arrive(
            lambda src: remote(ms.at[0, 0], mb.at[f, src], m_send.at[0, 0], m_recv.at[f, src], k, 1 - c),
            m_col(f),
        )

    with scope("arrive_first"):
        arrive_m(c)
    with scope("proj_first"):
        own = unpack(c)
        firsts = [mm(own, wa[at : at + size], NT) for _, at, size in pieces]
    with scope("arrive_second"):
        arrive_m(1 - c)
    with scope("weights_wait"):
        for copy in w_out:
            copy.wait_recv()
    with scope("proj_second"):
        oth = unpack(1 - c)
        for dst, (_, at, size), first in zip((u_s, z_s, bc_s), pieces, firsts):
            dst[...] = (first + mm(oth, wb[at : at + size], NT)).astype(jnp.bfloat16)

    def per_head(x):
        high = x.astype(jnp.bfloat16)
        rest = (x - high.astype(jnp.float32)).astype(jnp.bfloat16)
        return mm(high, averages, NN) + mm(rest, averages, NN)

    with scope("forward"):
        b_bf, c_bf = bc_s[:, :N], bc_s[:, N:]
        scores = mm(c_bf, b_bf, NT)
        for p in range(half // 128):
            cols_p = slice(p * 128, (p + 1) * 128)
            u = u_s[:, cols_p].astype(jnp.float32)
            sig_u = 1.0 / (1.0 + jnp.exp(-u))
            su_s[:, cols_p] = sig_u
            val_bf = (u * sig_u).astype(jnp.bfloat16)
            for h in (2 * p, 2 * p + 1):
                mat_s[h] = (dec_s[h] * scores).astype(jnp.bfloat16)
            y = jnp.where(low, mm(mat_s[2 * p], val_bf, NN), mm(mat_s[2 * p + 1], val_bf, NN))
            y_s[:, cols_p] = y
            z = z_s[:, cols_p].astype(jnp.float32)
            sig_z = 1.0 / (1.0 + jnp.exp(-z))
            sz_s[:, cols_p] = sig_z
            gated = y * (z * sig_z)
            inv = lax.rsqrt(per_head(gated * gated) + EPSILON)
            inv_s[:, cols_p] = inv
            normed_s[:, cols_p] = (gated * inv).astype(jnp.bfloat16)

    side = zi // 2
    mate = zi + 1 - 2 * lax.rem(zi, 2)
    near_far, end_far = 2 - side, 3 - 3 * side
    order = (end_far, near_far, mate, zi)
    outer = zi == 3 * side

    def weight_block(chip):
        at = pl.ds(pl.multiple_of(chip * slab, slab), slab)
        return mm(gb[:, at], normed_s[...], TN)

    def across(j):
        return remote(xsend.at[j], xr.at[j], xr_send.at[j], xr_recv.at[j], 2 * zi + 1 - xi, c)

    with scope("weight_blocks"):
        for j, q in enumerate(order):
            xsend[j] = weight_block(2 * q + 1 - xi).astype(jnp.bfloat16)
            across(j).start()

    with scope("grad_normed"):
        gn_s[...] = mm(gb[...], wout[...], NN).astype(jnp.bfloat16)
    with scope("backward"):
        d_scores = jnp.zeros((toks, toks), jnp.float32)
        for p in range(half // 128):
            cols_p = slice(p * 128, (p + 1) * 128)
            z, sig_z, y, inv = z_s[:, cols_p].astype(jnp.float32), sz_s[:, cols_p], y_s[:, cols_p], inv_s[:, cols_p]
            act = z * sig_z
            normed = y * act * inv
            u, sig_u = u_s[:, cols_p].astype(jnp.float32), su_s[:, cols_p]
            val = u * sig_u
            val_bf = val.astype(jnp.bfloat16)
            gn = gn_s[:, cols_p].astype(jnp.float32)
            gg = inv * (gn - normed * per_head(gn * normed))
            dy = gg * act
            dz = gg * y * (sig_z + act * (1.0 - sig_z))
            dy_bf = dy.astype(jnp.bfloat16)
            dv = jnp.where(low, mm(mat_s[2 * p], dy_bf, TN), mm(mat_s[2 * p + 1], dy_bf, TN))
            du = dv * (sig_u + val * (1.0 - sig_u))
            gp[:, cols_p] = du.astype(jnp.bfloat16)
            gp[:, half + p * 128 : half + (p + 1) * 128] = dz.astype(jnp.bfloat16)
            zero = jnp.zeros_like(dy)
            d_scores += dec_s[2 * p] * mm(jnp.where(low, dy, zero).astype(jnp.bfloat16), val_bf, NT)
            d_scores += dec_s[2 * p + 1] * mm(jnp.where(low, zero, dy).astype(jnp.bfloat16), val_bf, NT)
        ds_bf = d_scores.astype(jnp.bfloat16)
        d_bc = jnp.concatenate([mm(ds_bf, c_bf, TN), mm(ds_bf, b_bf, NN)], axis=1)
        gp[:, 2 * half :] = d_bc.astype(jnp.bfloat16)

    home, slot = k // rows, lax.rem(k, rows)

    def row_back(n, chip):
        return remote(
            pgs.at[n, chip], prow.at[n, slot], p_send.at[n, chip], p_recv.at[n, slot], chip, home
        )

    def col_back(n):
        return remote(
            pgs.at[n, pl.ds(0, rows)], pcol.at[n], p_send.at[n, chips], p_recv.at[n, rows], k, 0
        )

    others = [
        2 * z + x
        for z in (3 - zi, lax.rem(zi + 2, depth), mate)
        for x in (1 - xi, xi)
    ] + [2 * zi + 1 - xi]

    for n, w_ref in enumerate((wa, wb)):
        with scope("back_project"):
            pgs[n] = mm(gp[...], w_ref[...], NN).astype(jnp.bfloat16).reshape(chips, cols, part)

            @pl.when(c == 0)
            def _():
                for chip in others:
                    row_back(n, chip).start()

                @pl.when(home == 1)
                def _():
                    row_back(n, k).start()

                for i in range(rows):

                    @pl.when(k == i)
                    def _():
                        prow[n, i] = pgs[n, i]

            @pl.when(c == 1)
            def _():
                col_back(n).start()
                pcol[n] = pgs[n, pl.ds(rows, rows)]

    with scope("own_blocks"):
        for j, q in enumerate(order):
            wgo[j] = weight_block(2 * q + xi)

    def to_target(j, kind, chip, core):
        return remote(
            zs.at[j, core], zr.at[kind, c], z_send.at[j, core], zr_recv.at[kind, c], chip, core
        )

    def to_mate(j):
        return remote(zs.at[j], zc.at[j], z_send.at[j, 0], zc_recv.at[j], 2 * mate + xi, c)

    def ready(j, value):
        zs[j] = value.astype(jnp.bfloat16).reshape(2, slab // 2, half)

    def from_across(j):
        across(j).wait_recv()
        return wgo[j] + xr[j].astype(jnp.float32)

    def combine(j):
        @pl.when(jnp.logical_not(outer))
        def _():
            to_mate(j).wait_recv()
            ready(j, wgo[j] + zc[j].astype(jnp.float32).reshape(slab, half))
            for core in range(2):
                to_target(j, 1, 2 * order[j] + xi, core).start()

    with scope("far_0"):
        for j in range(2):
            both = from_across(j)

            @pl.when(outer)
            def _():
                ready(j, both)
                to_mate(j).start()

            @pl.when(jnp.logical_not(outer))
            def _():
                wgo[j] = both

    with scope("far_1"):
        combine(0)
    with scope("to_mate"):
        ready(2, from_across(2))
        for core in range(2):
            to_target(2, 0, 2 * mate + xi, core).start()
    with scope("far_2"):
        combine(1)
    with scope("own"):
        both = from_across(3)
        wgo[3] = both
        ready(3, both)
        to_target(3, 2, k, 1 - c).start()

    with scope("parts_wait"):
        for n in range(2):

            @pl.when(c == 0)
            def _():
                col_back(n).wait_recv()

            for i in range(rows):

                @pl.when(jnp.logical_or(c == 1, k != i))
                def _():
                    remote(
                        pgs.at[n, 0], prow.at[n, i], p_send.at[n, 0], p_recv.at[n, i], k, 1 - c
                    ).wait_recv()

    with scope("patch_grad"):
        for f in range(2):
            by_row, by_col = prow.at[f], pcol.at[1 - f]
            for i in range(rows):
                keep = present_t[:, i : i + 1] * (1.0 - hidden_t[:, i : i + 1])
                both = by_row[i].astype(jnp.float32) + by_col[i].astype(jnp.float32)
                pg_ref[i, :, f * part : (f + 1) * part] = (both * keep).astype(pg_ref.dtype)

    def landed(kind, core):
        return remote(
            zs.at[0, 0], zr.at[kind, core], z_send.at[0, 0], zr_recv.at[kind, core], k, 1 - c
        )

    with scope("sums_wait"):
        for kind in range(2):
            for core in range(2):
                landed(kind, core).wait_recv()
        landed(2, 1 - c).wait_recv()
    with scope("weight_sum"):
        here = pl.ds(pl.multiple_of(c * (slab // 2), slab // 2), slab // 2)
        zr[2, c] = wgo[3, here].astype(jnp.bfloat16)
        for core in range(2):
            acc = zr[0, core].astype(jnp.float32) + zr[1, core].astype(jnp.float32)
            acc += zr[2, core].astype(jnp.float32)
            out_ref[:, core * half : (core + 1) * half] = acc * scale

    with scope("drain"):
        each_row(d_row, wait_send)
        for f in range(2):
            each_row(functools.partial(m_row, f), wait_send)
        for copy in w_out:
            copy.wait_send()
        for j in range(len(order)):
            across(j).wait_send()
        for j in range(2):

            @pl.when(outer)
            def _():
                to_mate(j).wait_send()

            @pl.when(jnp.logical_not(outer))
            def _():
                for core in range(2):
                    to_target(j, 1, 2 * order[j] + xi, core).wait_send()

        for core in range(2):
            to_target(2, 0, 2 * mate + xi, core).wait_send()
        to_target(3, 2, k, 1 - c).wait_send()

        @pl.when(c == 0)
        def _():
            d_col().wait_send()
            for f in range(2):
                m_col(f).wait_send()
            for n in range(2):
                for chip in others:
                    row_back(n, chip).wait_send()

                @pl.when(home == 1)
                def _():
                    row_back(n, k).wait_send()

        @pl.when(c == 1)
        def _():
            for n in range(2):
                col_back(n).wait_send()


def store_kernel(a_ref, b_ref, a_hbm, b_hbm, sem):
    copies = [
        pltpu.make_async_copy(a_ref, a_hbm, sem.at[0]),
        pltpu.make_async_copy(b_ref, b_hbm, sem.at[1]),
    ]
    for copy in copies:
        copy.start()
    for copy in copies:
        copy.wait()


def owned(
    patches, mask_token, masked, tissue, in_weight, out_weight, row_decay, col_decay, cotangent
):
    rows, cols, feat = patches.shape
    chips = lax.axis_size("gcol")
    toks, heads = chips * cols, row_decay.shape[0]
    half, part = out_weight.shape[1], in_weight.shape[1]
    width = 2 * half + 2 * N
    slab = feat // chips
    depth = chips // 2
    bf, fl = jnp.bfloat16, jnp.float32
    vmem, dma = pltpu.VMEM, pltpu.SemaphoreType.DMA
    in_vmem, anywhere = pl.BlockSpec(memory_space=pltpu.VMEM), pl.BlockSpec(memory_space=pltpu.HBM)
    scale = 1.0 / math.sqrt(2 * rows * cols * chips)
    aux = heads + 8
    results = pl.pallas_call(
        functools.partial(layer_kernel, chips, rows, scale),
        name="layer",
        out_shape=(vmem(patches.shape, bf), vmem((slab // 2, 2 * half), fl)),
        in_specs=[anywhere] * 9,
        out_specs=(in_vmem, in_vmem),
        scratch_shapes=[
            vmem(patches.shape, bf), vmem(mask_token.shape, bf), vmem(patches.shape, bf),
            vmem(masked.shape, masked.dtype), vmem(tissue.shape, tissue.dtype),
            vmem(row_decay.shape, fl), vmem(col_decay.shape, fl), dma((7,)),
            vmem((2, rows, cols, part), bf), vmem((2, chips, cols, part), bf),
            vmem((rows, aux, cols), fl), vmem((rows, aux, cols), fl), vmem((chips, aux, cols), fl),
            vmem((width, part), bf), vmem((width, part), bf), vmem(out_weight.shape, bf),
            vmem((toks, feat), bf),
            vmem((toks, half), bf), vmem((toks, half), bf), vmem((toks, half), fl), vmem((toks, half), fl),
            vmem((toks, half), bf), vmem((toks, 2 * N), bf), vmem((toks, half), bf),
            vmem((toks, half), fl), vmem((toks, half), fl),
            vmem((heads, toks, toks), bf), vmem((heads, toks, toks), fl),
            vmem((toks, width), bf), vmem((2, chips, cols, part), bf),
            vmem((2, rows, cols, part), bf), vmem((2, rows, cols, part), bf),
            vmem((depth, slab, half), bf), vmem((depth, slab, half), fl), vmem((depth, slab, half), bf),
            vmem((depth, 2, slab // 2, half), bf), vmem((2, 2, slab // 2, half), bf),
            vmem((3, 2, slab // 2, half), bf),
            dma((2, rows + 1)), dma((2, chips + 1)), dma((rows + 1,)), dma((chips + 1,)),
            dma((3,)), dma((3,)), dma((4,)),
            dma((2, chips + 1)), dma((2, rows + 1)), dma((depth,)), dma((depth,)),
            dma((depth, 2)), dma((2,)), dma((3, 2)),
        ],
        compiler_params=pltpu.CompilerParams(
            collective_id=0, has_side_effects=True, vmem_limit_bytes=60 << 20
        ),
    )(
        patches, mask_token, cotangent, masked, tissue, row_decay, col_decay,
        in_weight, out_weight,
    )
    return pl.pallas_call(
        store_kernel,
        name="store",
        out_shape=tuple(jax.ShapeDtypeStruct(r.shape, r.dtype) for r in results),
        in_specs=[in_vmem] * 2,
        out_specs=[anywhere] * 2,
        scratch_shapes=[dma((2,))],
        compiler_params=pltpu.CompilerParams(vmem_limit_bytes=1 << 20),
    )(*results)


def body(*args):
    rows = args[0].shape[0]
    if lax.axis_size("grow") == 2 and rows == 4 and lax.axis_size("gcol") == 2 * rows:
        return owned(*args)
    return shards(*args)


def solution(mesh):
    return jax.shard_map(
        body,
        mesh=mesh,
        in_specs=(
            P(("groups", "grow"), "gcol", None),
            P(),
            P(("groups", "grow"), "gcol"),
            P(("groups", "grow"), "gcol"),
            P(None, "grow"),
            P(None, "grow"),
            P(None, ("groups", "grow"), "gcol"),
            P(None, ("groups", "grow"), "gcol"),
            P(("groups", "grow"), "gcol", None),
        ),
        out_specs=(P(("groups", "grow"), "gcol", None), P(("groups", "gcol", "grow"), None)),
        check_vma=False,
    )
```

```python
import functools
import itertools
import math

import jax
import jax.numpy as jnp
from jax import lax
from jax.experimental import pallas as pl
from jax.experimental.pallas import tpu as pltpu
from jax.sharding import PartitionSpec as P

E = 1024
HEADS = 16
N = 64


EPSILON = 1e-05
PRECISE = lax.Precision.HIGHEST


def prefix(value, axis, join, neutral):
    count, mine = (lax.axis_size(axis), lax.axis_index(axis))
    pieces = jax.tree.map(lambda part: lax.all_gather(part, axis), value)
    so_far = jax.tree.map(
        lambda part, zero: jnp.full_like(part, 0) + jnp.asarray(zero, part.dtype), value, neutral
    )

    def prefix_hop(position, so_far):
        longer = join(so_far, jax.tree.map(lambda part: part[position], pieces))
        return jax.tree.map(lambda new, old: jnp.where(position < mine, new, old), longer, so_far)

    return lax.fori_loop(0, count - 1, prefix_hop, so_far)


def carried_in(shard, axis, combine, identity):
    length, position = (lax.axis_size(axis), lax.axis_index(axis))
    everything = jax.tree.map(
        lambda part, kind: lax.all_gather(part.astype(kind), axis),
        shard,
        jax.tree.map(lambda a: jnp.bfloat16 if a.dtype == jnp.float32 else a.dtype, shard),
    )
    start = jax.tree.map(
        lambda part, zero: jnp.broadcast_to(jnp.asarray(zero, part.dtype), part.shape),
        shard,
        identity,
    )

    def carried_hop(k, before):
        at = length - 1 - k
        reached = at > position
        new = combine(
            before, jax.tree.map(lambda part, own: part[at].astype(own.dtype), everything, shard)
        )
        return jax.tree.map(lambda a, b: jnp.where(reached, a, b), new, before)

    return lax.fori_loop(0, length, carried_hop, start)


def shortened(shard):

    def short(part):
        return part.astype(jnp.bfloat16) if part.dtype == jnp.float32 else part

    return jax.tree.map(short, shard)


def silu_grad(pre_act):
    sigmoid_v = jax.nn.sigmoid(pre_act)
    return sigmoid_v * (1.0 + pre_act * (1.0 - sigmoid_v))


def per_channel(head_part, channels):
    return jnp.repeat(head_part, channels // head_part.shape[-1], axis=-1)


def line_form(head_lines, channels):
    return per_channel(head_lines.transpose(1, 2, 0), channels)


def carry_on(log_lines, state):
    return per_channel(jnp.exp(log_lines), state.shape[2])[:, None, :] * state


def prepare(log_decay):
    length = log_decay.shape[2]
    causal = jnp.arange(length)[:, None] >= jnp.arange(length)[None, :]
    running = jnp.einsum(
        "glk,tk->glt", log_decay, causal.astype(log_decay.dtype), precision=PRECISE
    )
    whole_log = running[:, :, -1]
    log_gaps = running[:, :, :, None] - running[:, :, None, :]
    decay_mat = jnp.where(causal, jnp.exp(jnp.where(causal, log_gaps, 0.0)), 0.0)
    return (running, whole_log, decay_mat)


def chain_link(earlier, later):
    return (earlier[0] + later[0], carry_on(later[0], earlier[1]) + later[1])


def split_heads(lines, head_count):
    line_count, length, channels = lines.shape
    return lines.reshape(line_count, length, head_count, channels // head_count)


def local_summary(inputs, key_vecs, prepared):
    running, whole_log, decay_mat = prepared
    to_end = line_form(jnp.exp(whole_log[:, :, None] - running), inputs.shape[2])
    fresh = jnp.einsum("ltc,ltn->lnc", inputs * to_end, key_vecs, precision=PRECISE)
    return (whole_log.T, fresh)


def local_return(query_vecs, prepared, upstream):
    running, whole_log, decay_mat = prepared
    from_start = line_form(jnp.exp(running), upstream.shape[2])
    backward = jnp.einsum("ltc,ltn->lnc", upstream * from_start, query_vecs, precision=PRECISE)
    return (whole_log.T, backward)


def local_outputs(inputs, key_vecs, query_vecs, prepared, incoming):
    running, whole_log, decay_mat = prepared
    head_count = decay_mat.shape[0]
    line_count, length, channels = inputs.shape
    scores = jnp.einsum("ltn,lkn->ltk", query_vecs, key_vecs, precision=PRECISE)
    within = jnp.einsum(
        "gltk,lkgp->ltgp",
        decay_mat * scores[None],
        split_heads(inputs, head_count),
        precision=PRECISE,
    )
    within = within.reshape(line_count, length, channels)
    carried = jnp.einsum("ltn,lnc->ltc", query_vecs, incoming, precision=PRECISE)
    return within + carried * line_form(jnp.exp(running), channels)


def local_grads(inputs, key_vecs, query_vecs, prepared, incoming, returning, upstream):
    running, whole_log, decay_mat = prepared
    head_count = decay_mat.shape[0]
    line_count, length, channels = inputs.shape
    from_start = line_form(jnp.exp(running), channels)
    to_end = line_form(jnp.exp(whole_log[:, :, None] - running), channels)
    scores = jnp.einsum("ltn,lkn->ltk", query_vecs, key_vecs, precision=PRECISE)
    heads_up = split_heads(upstream, head_count)
    heads_in = split_heads(inputs, head_count)
    grad_inputs = jnp.einsum(
        "gltk,ltgp->lkgp", decay_mat * scores[None], heads_up, precision=PRECISE
    ).reshape(line_count, length, channels)
    grad_inputs = (
        grad_inputs + jnp.einsum("lnc,lkn->lkc", returning, key_vecs, precision=PRECISE) * to_end
    )
    mixed = jnp.einsum("ltgp,lkgp->gltk", heads_up, heads_in, precision=PRECISE) * decay_mat
    grad_keys = jnp.einsum("gltk,ltn->lkn", mixed, query_vecs, precision=PRECISE)
    grad_keys = grad_keys + jnp.einsum(
        "lkc,lnc->lkn", inputs * to_end, returning, precision=PRECISE
    )
    grad_queries = jnp.einsum("gltk,lkn->ltn", mixed, key_vecs, precision=PRECISE)
    grad_queries = grad_queries + jnp.einsum(
        "ltc,lnc->ltn", upstream * from_start, incoming, precision=PRECISE
    )
    return (grad_inputs, grad_keys, grad_queries)


def shards(
    patches, mask_token, masked, tissue, in_weight, out_weight, row_decay, col_decay, cotangent
):
    grid_rows, grid_cols, feat_width = patches.shape
    tok_count = grid_rows * grid_cols
    chosen = (masked == 1)[:, :, None]
    present = tissue.astype(jnp.bfloat16)[:, :, None]
    model_in = jnp.where(chosen, mask_token[None, None, :], patches) * present
    flat_in = model_in.reshape(tok_count, feat_width)
    inner_width = E
    half_width = inner_width // 2
    state_size = N
    number_of_heads = HEADS // 2
    offset = 2 * inner_width
    full_in, full_out = (
        lax.all_gather(in_weight, "grow", axis=1, tiled=True),
        lax.all_gather(out_weight, "grow", axis=1, tiled=True),
    )
    projected = lax.dot_general(
        flat_in, full_in, (((1,), (1,)), ((), ())), preferred_element_type=jnp.float32
    )
    proj_bf = projected.astype(jnp.bfloat16)
    pre_values = proj_bf[:, :inner_width].astype(jnp.float32)
    gate_pre = proj_bf[:, inner_width:offset].astype(jnp.float32)
    key_rows = (
        proj_bf[:, offset : offset + state_size]
        .astype(jnp.float32)
        .reshape(grid_rows, grid_cols, state_size)
    )
    query_rows = (
        proj_bf[:, offset + state_size : offset + 2 * state_size]
        .astype(jnp.float32)
        .reshape(grid_rows, grid_cols, state_size)
    )
    key_cols = (
        proj_bf[:, offset + 2 * state_size : offset + 3 * state_size]
        .astype(jnp.float32)
        .reshape(grid_rows, grid_cols, state_size)
        .transpose(1, 0, 2)
    )
    query_cols = (
        proj_bf[:, offset + 3 * state_size : offset + 4 * state_size]
        .astype(jnp.float32)
        .reshape(grid_rows, grid_cols, state_size)
        .transpose(1, 0, 2)
    )
    values = jax.nn.silu(pre_values)
    row_inputs = values[:, :half_width].reshape(grid_rows, grid_cols, half_width)
    col_inputs = values[:, half_width:].reshape(grid_rows, grid_cols, half_width).transpose(1, 0, 2)
    row_prep = prepare(row_decay)
    col_prep = prepare(col_decay.transpose(0, 2, 1))
    row_zero = (
        jnp.zeros((grid_rows, number_of_heads), jnp.float32),
        jnp.zeros((grid_rows, state_size, half_width), jnp.float32),
    )
    col_zero = (
        jnp.zeros((grid_cols, number_of_heads), jnp.float32),
        jnp.zeros((grid_cols, state_size, half_width), jnp.float32),
    )
    row_entry = prefix(local_summary(row_inputs, key_rows, row_prep), "gcol", chain_link, row_zero)[
        1
    ]
    grow_size = lax.axis_size("grow")
    my_block = lax.axis_index("grow")
    parts_in, parts_key, parts_log = (
        lax.all_gather(
            proj_bf[:, half_width:inner_width].reshape(grid_rows, grid_cols, half_width),
            "grow",
            axis=0,
            tiled=True,
        ),
        lax.all_gather(
            proj_bf[:, offset + 2 * state_size : offset + 3 * state_size].reshape(
                grid_rows, grid_cols, state_size
            ),
            "grow",
            axis=0,
            tiled=True,
        ),
        lax.all_gather(
            col_decay.transpose(1, 0, 2).astype(jnp.bfloat16), "grow", axis=0, tiled=True
        ).astype(jnp.float32),
    )
    col_entry = col_zero[1]
    for block_idx in range(grow_size):
        lower_row = block_idx * grid_rows
        piece_in = jax.nn.silu(
            parts_in[lower_row : lower_row + grid_rows].astype(jnp.float32)
        ).transpose(1, 0, 2)
        piece_keys = (
            parts_key[lower_row : lower_row + grid_rows].astype(jnp.float32).transpose(1, 0, 2)
        )
        piece_log = parts_log[lower_row : lower_row + grid_rows].transpose(1, 2, 0)
        whole_log, piece_state = local_summary(piece_in, piece_keys, prepare(piece_log))
        moved = carry_on(whole_log, col_entry) + piece_state
        col_entry = jnp.where(block_idx < my_block, moved, col_entry)
    row_out = local_outputs(row_inputs, key_rows, query_rows, row_prep, row_entry)
    col_out = local_outputs(col_inputs, key_cols, query_cols, col_prep, col_entry).transpose(
        1, 0, 2
    )
    mixed = jnp.concatenate(
        [row_out.reshape(tok_count, half_width), col_out.reshape(tok_count, half_width)], axis=1
    )
    gate_act = jax.nn.silu(gate_pre)
    head_size = inner_width // HEADS
    gated = (mixed * gate_act).reshape(tok_count, HEADS, head_size)
    inv_rms = lax.rsqrt(jnp.mean(gated * gated, axis=2, keepdims=True) + EPSILON)
    normed = gated * inv_rms
    normed_bf = normed.reshape(tok_count, inner_width).astype(jnp.bfloat16)
    grad_out = (cotangent * masked.astype(jnp.bfloat16)[:, :, None]).reshape(tok_count, feat_width)
    total_patches = tok_count * lax.axis_size("gcol") * lax.axis_size("grow")
    weight_sum = lax.psum_scatter(
        lax.dot_general(
            grad_out, normed_bf, (((0,), (0,)), ((), ())), preferred_element_type=jnp.float32
        ),
        ("gcol", "grow"),
        scatter_dimension=0,
        tiled=True,
    )
    out_weight_grad = weight_sum * (1.0 / math.sqrt(total_patches))
    grad_normed_bf = jnp.dot(grad_out, full_out, preferred_element_type=jnp.float32).astype(
        jnp.bfloat16
    )
    grad_normed = lax.optimization_barrier(grad_normed_bf).astype(jnp.float32)
    grad_normed = grad_normed.reshape(tok_count, HEADS, head_size)
    grad_gated = inv_rms * (
        grad_normed - normed * jnp.mean(grad_normed * normed, axis=2, keepdims=True)
    )
    grad_gated = grad_gated.reshape(tok_count, inner_width)
    grad_mixed = grad_gated * gate_act
    grad_gate = grad_gated * mixed * silu_grad(gate_pre)
    row_up = grad_mixed[:, :half_width].reshape(grid_rows, grid_cols, half_width)
    col_up = grad_mixed[:, half_width:].reshape(grid_rows, grid_cols, half_width).transpose(1, 0, 2)
    row_exit = carried_in(local_return(query_rows, row_prep, row_up), "gcol", chain_link, row_zero)[
        1
    ]
    parts_up, parts_query = (
        lax.all_gather(
            shortened(grad_mixed[:, half_width:].reshape(grid_rows, grid_cols, half_width)),
            "grow",
            axis=0,
            tiled=True,
        ),
        lax.all_gather(
            proj_bf[:, offset + 3 * state_size : offset + 4 * state_size].reshape(
                grid_rows, grid_cols, state_size
            ),
            "grow",
            axis=0,
            tiled=True,
        ),
    )
    col_exit = col_zero[1]
    for block_idx in reversed(range(grow_size)):
        lower_row = block_idx * grid_rows
        piece_up = parts_up[lower_row : lower_row + grid_rows].transpose(1, 0, 2)
        piece_queries = (
            parts_query[lower_row : lower_row + grid_rows].astype(jnp.float32).transpose(1, 0, 2)
        )
        piece_log = parts_log[lower_row : lower_row + grid_rows].transpose(1, 2, 0)
        whole_log, piece_back = local_return(piece_queries, prepare(piece_log), piece_up)
        moved = carry_on(whole_log, col_exit) + piece_back
        col_exit = jnp.where(block_idx > my_block, moved, col_exit)
    grad_row_in, grad_row_key, grad_row_query = local_grads(
        row_inputs, key_rows, query_rows, row_prep, row_entry, row_exit, row_up
    )
    grad_col_in, grad_col_key, grad_col_query = local_grads(
        col_inputs, key_cols, query_cols, col_prep, col_entry, col_exit, col_up
    )
    grad_values = jnp.concatenate(
        [
            grad_row_in.reshape(tok_count, half_width),
            grad_col_in.transpose(1, 0, 2).reshape(tok_count, half_width),
        ],
        axis=1,
    )
    grad_proj = jnp.concatenate(
        [
            grad_values * silu_grad(pre_values),
            grad_gate,
            grad_row_key.reshape(tok_count, state_size),
            grad_row_query.reshape(tok_count, state_size),
            grad_col_key.transpose(1, 0, 2).reshape(tok_count, state_size),
            grad_col_query.transpose(1, 0, 2).reshape(tok_count, state_size),
        ],
        axis=1,
    ).astype(jnp.bfloat16)
    keep_mask = present * (1 - masked).astype(jnp.bfloat16)[:, :, None]
    grad_model_in = jnp.dot(grad_proj, full_in, preferred_element_type=jnp.float32).reshape(
        grid_rows, grid_cols, feat_width
    )
    patch_grad = (grad_model_in * keep_mask).astype(jnp.bfloat16)
    return (patch_grad, out_weight_grad)


MESH = pl.DeviceIdType.MESH
NT = (((1,), (1,)), ((), ()))
NN = (((1,), (0,)), ((), ()))
TN = (((0,), (0,)), ((), ()))


def mm(a, b, dims):
    return lax.dot_general(a, b, dims, preferred_element_type=jnp.float32)


def layer_kernel(
    chips, rows, scale,
    patch_hbm, token_hbm, cot_hbm, hidden_hbm, present_hbm, rdec_hbm, cdec_hbm, w_hbm, wout_hbm,
    pg_out, sum_out,
    sems, pg_ref, out_ref, pair_ref, token_ref, flag_ref, dec_ref,
    ms, mb, rd, cd, db, wa, wb, wr, wout, gb, gsr, ga, gx, gsx, gcx, nx, la, lx, ln, lnx, u_s, z_s, su_s, sz_s, gn_s, bc_s,
    normed_s, y_s, inv_s, mat_s, dec_s, gp, gph, prs, pcs, prow, pcol,
    wc, wq, zs, zq, zc, zcq, zr, zrq,
):
    k, c = lax.axis_index("gcol"), lax.axis_index("grow")
    depth = chips // 2
    zi, xi = k // 2, lax.rem(k, 2)
    cols = ms.shape[2]
    toks = chips * cols
    feat, half, part = token_ref.shape[0], wout.shape[1], wa.shape[1]
    heads, width = dec_ref.shape[1], wa.shape[0]
    total = 2 * chips
    slab = feat // chips
    scope = jax.named_scope
    ids = itertools.count()

    def new_sem():
        return sems.at[next(ids)]

    def landed(ref, sem):
        pltpu.make_async_copy(ref, ref, sem).wait()

    me = 2 * k + c
    barrier = pltpu.get_barrier_semaphore()
    for d in range(1, total):
        to = lax.rem(me + d, total)
        pl.semaphore_signal(
            barrier, inc=1, device_id={"gcol": to // 2, "grow": lax.rem(to, 2)}, device_id_type=MESH
        )

    side = zi // 2
    mate = zi + 1 - 2 * lax.rem(zi, 2)
    near_far, end_far = 2 - side, 3 - 3 * side
    order = (end_far, near_far, mate, zi)
    outer = zi == 3 * side
    inner = jnp.logical_not(outer)
    beside = 2 * zi + 1 - xi

    def block(q):
        return pl.ds(pl.multiple_of(q * slab, slab), slab)

    pieces = ((0, 0, half), (2 * half, half, half), (4 * half, 2 * half, 2 * N))

    def packed(ref, core):
        return [
            (ref.at[pl.ds(pl.multiple_of(base + core * size, 128), size)], pl.ds(at, size))
            for base, at, size in pieces
        ]

    in_sem = [new_sem() for _ in range(4)]
    loads = [
        pltpu.make_async_copy(src, dst, s)
        for src, dst, s in (
            (hidden_hbm, flag_ref.at[0], in_sem[0]), (present_hbm, flag_ref.at[1], in_sem[0]),
            (token_hbm, token_ref, in_sem[1]),
            (rdec_hbm, dec_ref.at[0], in_sem[2]), (cdec_hbm, dec_ref.at[1], in_sem[2]),
            (patch_hbm, pair_ref.at[0], in_sem[3]), (cot_hbm, pair_ref.at[1], in_sem[3]),
        )
    ]
    for copy in loads:
        copy.start()
    load_w = [pltpu.make_async_copy(src, wa.at[at], in_sem[0]) for src, at in packed(w_hbm, c)]
    load_o = pltpu.make_async_copy(wout_hbm, wout, in_sem[1])
    load_r = [pltpu.make_async_copy(src, wr.at[at], in_sem[2]) for src, at in packed(w_hbm, 1 - c)]
    patch_ref, cot_ref = pair_ref.at[0], pair_ref.at[1]

    def remote(src, dst, s, r, chip, core):
        return pltpu.make_async_remote_copy(
            src_ref=src, dst_ref=dst, send_sem=s, recv_sem=r,
            device_id={"gcol": chip, "grow": core}, device_id_type=MESH,
        )

    def across_lanes(column):
        one = jnp.broadcast_to(column, (column.shape[0], 128)).astype(jnp.bfloat16)
        return jnp.concatenate([one] * (part // 128), axis=1)

    with scope("prep"):
        for ref, sem in zip((flag_ref, token_ref, dec_ref, pair_ref), in_sem):
            landed(ref, sem)
        for copy in load_w:
            copy.start()
        load_o.start()
        for copy in load_r:
            copy.start()
        square = (cols, cols)
        eye = lax.broadcasted_iota(jnp.int32, square, 0) == lax.broadcasted_iota(jnp.int32, square, 1)
        eye = eye.astype(jnp.float32)
        hidden_f, present_f = flag_ref[0].astype(jnp.float32), flag_ref[1].astype(jnp.float32)
        hidden_t, present_t = mm(eye, hidden_f, NT), mm(eye, present_f, NT)
        visible_t = present_t * (1.0 - hidden_t)
        for i in range(rows):
            hidden, visible = across_lanes(hidden_t[:, i : i + 1]), across_lanes(visible_t[:, i : i + 1])
            for f in range(2):
                at = slice(f * part, (f + 1) * part)
                ms[f, i] = patch_ref[i, :, at] * visible + cot_ref[i, :, at] * hidden
            for q in range(depth):
                at = slice(q * slab, (q + 1) * slab)
                gsx[i, :, at] = cot_ref[i, :, block(2 * q + 1 - xi)] * hidden[:, :slab]
                turn = (2 * q + 1 - i % 2) * slab
                gsr[i, :, at] = cot_ref[i, :, turn : turn + slab] * hidden[:, :slab]
            blank = jnp.zeros((rd.shape[1] - heads - 2, cols), jnp.float32)
            flags = jnp.concatenate([hidden_f[i : i + 1], present_f[i : i + 1], blank], axis=0)
            for n, dst in enumerate((rd, cd)):
                dst[i, :heads] = dec_ref[n, :, i, :]
                dst[i, heads:] = flags

    m_send, d_send, g_send, gc_send, w_send, n_send, p_send, c_send = [new_sem() for _ in range(8)]
    m_recv, (d_recv, g_recv, gc_recv, w_recv, n_recv, nr_recv, p_recv, c_recv) = (
        [sems.at[next(ids)] for _ in range(2)], [new_sem() for _ in range(8)]
    )

    g_col = remote(gsx, gcx.at[pl.ds(rows * c, rows)], gc_send, gc_recv, beside, 1)

    def g_row(i):
        return remote(gsr.at[i], gx.at[k], g_send, g_recv, rows * c + (i ^ 1), 0)

    def m_row(f, i):
        return remote(ms.at[f, i], mb.at[f * chips + k], m_send, m_recv[f], rows * c + i, 0)

    def m_col(f):
        return remote(ms.at[f], mb.at[pl.ds(f * chips, rows)], m_send, m_recv[f], k, 1)

    def d_row(i):
        return remote(rd.at[i], db.at[k], d_send, d_recv, rows * c + i, 0)

    d_col = remote(cd, db.at[pl.ds(0, rows)], d_send, d_recv, k, 1)

    def not_me(i):
        return jnp.logical_or(c == 1, k != i)

    def each_row(copy_of, owner=lambda i: i):
        for i in range(rows):

            @pl.when(not_me(owner(i)))
            def _():
                copy_of(i).start()

    def each_g_row():
        each_row(g_row, lambda i: i ^ 1)

    def drained(ref, sem, count, own, extra):
        @pl.when(c == 1)
        def _():
            landed(ref.at[pl.ds(0, count)], sem)

        for mine, less in ((k < rows, own), (k >= rows, 0)):

            @pl.when(jnp.logical_and(c == 0, mine))
            def _():
                landed(ref.at[pl.ds(0, count - less + extra)], sem)

    w_out = remote(wr, wb, w_send, w_recv, k, 1 - c)
    with scope("own_rows"):
        @pl.when(c == 1)
        def _():
            pltpu.make_async_copy(cd, db.at[pl.ds(rows, rows)], d_recv).start()
            for f in range(2):
                pltpu.make_async_copy(ms.at[f], mb.at[pl.ds(f * chips + rows, rows)], m_recv[f]).start()

        for i in range(rows):

            @pl.when(jnp.logical_and(c == 0, k == i))
            def _():
                pltpu.make_async_copy(rd.at[i], db.at[i], d_recv).start()
                pltpu.make_async_copy(gsr.at[i ^ 1], gx.at[i], g_recv).start()
                for f in range(2):
                    pltpu.make_async_copy(ms.at[f, i], mb.at[f * chips + i], m_recv[f]).start()

    with scope("barrier_wait"):
        pl.semaphore_wait(barrier, total - 1)
    with scope("launch"):
        each_row(d_row)

        @pl.when(c == 0)
        def _():
            d_col.start()
            m_col(1).start()
            m_col(0).start()

        for f in range(2):
            each_row(functools.partial(m_row, f))
        landed(wr, in_sem[2])
        w_out.start()
        g_col.start()

    t_at = lax.broadcasted_iota(jnp.int32, (toks, toks), 0)
    k_at = lax.broadcasted_iota(jnp.int32, (toks, toks), 1)
    gap_at = t_at - k_at
    mask = jnp.logical_and(gap_at >= 0, (gap_at & (cols - 1)) * c == 0)
    low = lax.broadcasted_iota(jnp.int32, (toks, 128), 1) < N
    same = (128, 128)
    head_of = [lax.broadcasted_iota(jnp.int32, same, d) // N for d in range(2)]
    averages = jnp.where(head_of[0] == head_of[1], 1.0 / N, 0.0).astype(jnp.bfloat16)

    with scope("arrive_decay"):
        landed(db, d_recv)
    with scope("decay"):
        ones = mask.astype(jnp.float32)
        dec = jnp.concatenate([db[i] for i in range(chips)], axis=1)
        run_s = lax.dot_general(ones, dec, NT, precision=PRECISE, preferred_element_type=jnp.float32)
        run_l = lax.dot_general(dec, ones, NT, precision=PRECISE, preferred_element_type=jnp.float32)
        for h in range(heads):
            gap = run_s[:, h : h + 1] - run_l[h : h + 1, :]
            dec_s[h] = jnp.where(mask, jnp.exp(jnp.minimum(gap, 0.0)), 0.0)
        unit = (t_at == k_at).astype(jnp.float32)
        flags_t = mm(unit, dec[heads:], NT)
        tok_hidden, tok_filled = across_lanes(flags_t[:, 0:1]), across_lanes(flags_t[:, 0:1] * flags_t[:, 1:2])
        tok_shown = across_lanes(1.0 - flags_t[:, 0:1])

    with scope("load_w"):
        landed(wa, in_sem[0])
        landed(wout, in_sem[1])

    def halves(ref):
        return jnp.concatenate([ref[0], ref[1]], axis=1)

    def unpack(f):
        at = pl.ds(pl.multiple_of(f * part, part), part)
        either = mb[pl.ds(f * chips, chips)].reshape(toks, part)
        gb[:, at] = either * tok_hidden
        return either * tok_shown + token_ref[at].reshape(1, part) * tok_filled

    def split(f):
        for i in range(depth // 2):
            q = f * (depth // 2) + i
            at_i = slice(i * slab, (i + 1) * slab)
            ga[f, :, at_i] = gb[:, block(2 * q + xi)]

    def half_gn(f):
        at = pl.ds(pl.multiple_of(f * part, part), part)
        return mm(gb[:, at], wout[at, :], NN)

    def arrive_m(core):
        for f in range(2):

            @pl.when(core == f)
            def _():
                landed(mb.at[pl.ds(f * chips, chips)], m_recv[f])

    lend_sems = [(new_sem(), new_sem()) for _ in range(4)]

    def lend(i, src, dst):
        return remote(src, dst, *lend_sems[i], k, 1)

    pair = [pl.ds(i * 256, 256) for i in range(4)]
    lend_a = lend(0, ga, la)
    lend_x = lend(1, gx, lx)
    lend_n = lend(2, normed_s.at[:, pair[1]], ln)
    lend_p = [lend(3, gp.at[:, pair[i]], gph.at[:, pair[i]]) for i in range(4)]
    lend_p.append(lend(3, gp.at[:, pl.ds(2 * half, 2 * N)], gph.at[:, pl.ds(2 * half, 2 * N)]))

    n_first = remote(normed_s.at[:, pair[0]], nx.at[:, pair[0]], n_send, n_recv, beside, c)
    n_col = remote(normed_s.at[:, pair[1]], nx.at[:, pair[1]], n_send, n_recv, beside, 1)
    n_row = remote(normed_s.at[:, pair[1]], lnx, n_send, nr_recv, beside, 1)
    with scope("arrive_first"):
        arrive_m(c)
    with scope("proj_first"):
        own = unpack(c)
        firsts = [mm(own, wa[at : at + size], NT) for _, at, size in pieces]
        split(c)
        gn_first = half_gn(c)

        @pl.when(c == 0)
        def _():
            each_g_row()

    with scope("arrive_second"):
        arrive_m(1 - c)
    with scope("weights_wait"):
        landed(wb, w_recv)
    with scope("proj_second"):
        oth = unpack(1 - c)
        for dst, (_, at, size), first in zip((u_s, z_s, bc_s), pieces, firsts):
            dst[...] = (first + mm(oth, wb[at : at + size], NT)).astype(jnp.bfloat16)
        split(1 - c)


    def per_head(x):
        high = x.astype(jnp.bfloat16)
        rest = (x - high.astype(jnp.float32)).astype(jnp.bfloat16)
        return mm(high, averages, NN) + mm(rest, averages, NN)

    def if_core(core, copies):
        @pl.when(c == core)
        def _():
            for copy in copies:
                copy.start()

    if_core(0, [lend_a])

    with scope("forward"):
        b_bf, c_bf = bc_s[:, :N], bc_s[:, N:]
        scores = mm(c_bf, b_bf, NT)
        for p in range(half // 128):
            cols_p = slice(p * 128, (p + 1) * 128)
            u = u_s[:, cols_p].astype(jnp.float32)
            sig_u = 0.5 + 0.5 * jnp.tanh(0.5 * u)
            su_s[:, cols_p] = sig_u
            val_bf = (u * sig_u).astype(jnp.bfloat16)
            for h in (2 * p, 2 * p + 1):
                mat_s[h] = (dec_s[h] * scores).astype(jnp.bfloat16)
            y = jnp.where(low, mm(mat_s[2 * p], val_bf, NN), mm(mat_s[2 * p + 1], val_bf, NN))
            y_s[:, cols_p] = y
            z = z_s[:, cols_p].astype(jnp.float32)
            sig_z = 0.5 + 0.5 * jnp.tanh(0.5 * z)
            sz_s[:, cols_p] = sig_z
            gated = y * (z * sig_z)
            inv = lax.rsqrt(per_head(gated * gated) + EPSILON)
            inv_s[:, cols_p] = inv
            normed_s[:, cols_p] = (gated * inv).astype(jnp.bfloat16)
            if p == 1:
                n_first.start()
            if p == 3:
                if_core(1, [n_col])

                @pl.when(c == 1)
                def _():
                    each_g_row()

                if_core(0, [n_row, lend_n])

    with scope("grad_normed"):
        gn_s[...] = (gn_first + half_gn(1 - c)).astype(jnp.bfloat16)
    with scope("backward"):
        d_scores = jnp.zeros((toks, toks), jnp.float32)
        for p in range(half // 128):
            cols_p = slice(p * 128, (p + 1) * 128)
            z, sig_z, y, inv = z_s[:, cols_p].astype(jnp.float32), sz_s[:, cols_p], y_s[:, cols_p], inv_s[:, cols_p]
            act = z * sig_z
            normed = y * act * inv
            u, sig_u = u_s[:, cols_p].astype(jnp.float32), su_s[:, cols_p]
            val = u * sig_u
            val_bf = val.astype(jnp.bfloat16)
            gn = gn_s[:, cols_p].astype(jnp.float32)
            gg = inv * (gn - normed * per_head(gn * normed))
            dy = gg * act
            dz = gg * y * (sig_z + act * (1.0 - sig_z))
            dy_bf = dy.astype(jnp.bfloat16)
            dv = jnp.where(low, mm(mat_s[2 * p], dy_bf, TN), mm(mat_s[2 * p + 1], dy_bf, TN))
            du = dv * (sig_u + val * (1.0 - sig_u))
            gp[:, cols_p] = du.astype(jnp.bfloat16)
            gp[:, half + p * 128 : half + (p + 1) * 128] = dz.astype(jnp.bfloat16)
            zero = jnp.zeros_like(dy)
            d_scores += dec_s[2 * p] * mm(jnp.where(low, dy, zero).astype(jnp.bfloat16), val_bf, NT)
            d_scores += dec_s[2 * p + 1] * mm(jnp.where(low, zero, dy).astype(jnp.bfloat16), val_bf, NT)
            if p % 2 == 1:
                if_core(0, [lend_p[p // 2], lend_p[2 + p // 2]])
        ds_bf = d_scores.astype(jnp.bfloat16)
        d_bc = jnp.concatenate([mm(ds_bf, c_bf, TN), mm(ds_bf, b_bf, NN)], axis=1)
        gp[:, 2 * half :] = d_bc.astype(jnp.bfloat16)
        if_core(0, lend_p[4:])

    with scope("pass_gx"):

        @pl.when(c == 0)
        def _():
            landed(gx, g_recv)

        if_core(0, [lend_x])

    home, slot = k // rows, lax.rem(k, rows)

    def row_back(chip):
        return remote(prs.at[chip], prow.at[c, slot], p_send, p_recv, chip, home)

    def col_back(n):
        return remote(pcs.at[n, pl.ds(0, rows)], pcol.at[n], c_send, c_recv, k, 0)

    others = [
        2 * z + x
        for z in (3 - zi, lax.rem(zi + 2, depth), mate)
        for x in (1 - xi, xi)
    ] + [2 * zi + 1 - xi]

    def project_back(g_ref, w_ref):
        return mm(g_ref[...], w_ref[...], NN).astype(jnp.bfloat16).reshape(chips, cols, part)

    def return_rows():
        for chip in others:
            row_back(chip).start()

        @pl.when(home != c)
        def _():
            row_back(k).start()

        @pl.when(home == c)
        def _():
            pltpu.make_async_copy(prs.at[k], prow.at[c, slot], p_recv).start()

    class Sums:
        def __init__(self, w, z, zin, zout, slot):
            self.w, self.z, self.zin, self.zout, self.slot = w, z, zin, zout, slot
            self.send, self.in_recv, self.out_recv = [new_sem() for _ in range(3)]

        def to_target(self, j, kind, chip, core):
            return remote(
                self.z.at[2 * j + core], self.zout.at[3 * self.slot + kind], self.send, self.out_recv, chip, core
            )

        def part(self, j):
            return self.w[block(order[j]), :]

        def ready(self, j, value):
            self.z[2 * j : 2 * j + 2] = value.astype(jnp.bfloat16).reshape(2, slab // 2, value.shape[1])

        def begin(self):
            @pl.when(outer)
            def _():
                for j in range(2):
                    self.ready(j, self.part(j))
                    two = pl.ds(2 * j, 2)
                    remote(
                        self.z.at[two], self.zin.at[two], self.send, self.in_recv, 2 * mate + xi, c
                    ).start()

            self.ready(2, self.part(2))
            for core in range(2):
                self.to_target(2, 0, 2 * mate + xi, core).start()
            self.ready(3, self.part(3))
            pltpu.make_async_copy(
                self.z.at[6 + c], self.zout.at[3 * self.slot + 2], self.out_recv
            ).start()
            self.to_target(3, 2, k, 1 - c).start()

        def combine(self):
            @pl.when(inner)
            def _():
                landed(self.zin, self.in_recv)
                for j in range(2):
                    passed = self.zin[2 * j : 2 * j + 2].astype(jnp.float32).reshape(slab, self.w.shape[1])
                    self.ready(j, self.part(j) + passed)
                    for core in range(2):
                        self.to_target(j, 1, 2 * order[j] + xi, core).start()

        def drain(self):
            landed(self.z.at[pl.ds(0, 7)], self.send)

    col_sums = Sums(wc, zs, zc, zr, 0)
    row_sums = Sums(wq, zq, zcq, zrq, c)

    @pl.when(c == 0)
    def _():
        with scope("back_project_0"):
            prs[...] = project_back(gp, wa)
        with scope("wait_n0"):
            landed(nx.at[:, pair[0]], n_recv)
        with scope("row_product_0"):
            wq[...] = mm(halves(ga), normed_s[:, :256], TN) + mm(gx[...].reshape(toks, part), nx[:, :256], TN)

    @pl.when(c == 1)
    def _():
        with scope("col_back_1"):
            for n, w_ref in enumerate((wa, wb)):
                pcs[n] = project_back(gp, w_ref)
                col_back(n).start()
                pcol[n] = pcs[n, pl.ds(rows, rows)]
        with scope("wait_n1"):
            landed(gcx, gc_recv)
            landed(nx, n_recv)
        with scope("col_product"):
            wc[...] = mm(halves(ga), normed_s[...], TN) + mm(gcx[...].reshape(toks, part), nx[...], TN)
            col_sums.begin()
        with scope("lent_grad_wait"):
            landed(gph, lend_sems[3][1])
        with scope("back_project_1"):
            prs[...] = project_back(gph, wr)
        with scope("lent_wait"):
            for copy in (lend_a, lend_x, lend_n, n_row):
                copy.wait_recv()
        with scope("row_product_1"):
            wq[...] = mm(halves(la), ln[...], TN) + mm(lx[...].reshape(toks, part), lnx[...], TN)

    with scope("row_begin"):
        row_sums.begin()

    with scope("return_rows"):
        return_rows()


    @pl.when(c == 1)
    def _():
        with scope("col_combine"):
            col_sums.combine()

    with scope("row_combine"):
        row_sums.combine()

    with scope("parts_wait"):

        @pl.when(c == 0)
        def _():
            landed(pcol, c_recv)

        landed(prow, p_recv)

    with scope("patch_grad"):
        for f in range(2):
            by_row, by_col = prow.at[f], pcol.at[1 - f]
            for i in range(rows):
                keep = visible_t[:, i : i + 1]
                both = by_row[i].astype(jnp.float32) + by_col[i].astype(jnp.float32)
                pg_ref[i, :, f * part : (f + 1) * part] = (both * keep).astype(pg_ref.dtype)

    results = [
        pltpu.make_async_copy(pg_ref, pg_out, in_sem[0]),
        pltpu.make_async_copy(out_ref, sum_out, in_sem[1]),
    ]
    results[0].start()

    with scope("sums_wait"):
        landed(zr, col_sums.out_recv)
        landed(zrq, row_sums.out_recv)

    with scope("weight_sum"):
        for ref, at, size in ((zrq.at[0:3], 0, 256), (zrq.at[3:6], 256, 256), (zr, half, half)):
            acc = ref[0].astype(jnp.float32) + ref[1].astype(jnp.float32)
            acc += ref[2].astype(jnp.float32)
            out_ref[:, at : at + size] = acc * scale
    results[1].start()

    with scope("drain"):
        drained(db, d_send, rows, 1, rows)
        drained(mb, m_send, 2 * rows, 2, 2 * rows)
        drained(gx, g_send, rows, 1, 0)
        landed(gsx, gc_send)
        landed(wb, w_send)
        row_sums.drain()
        landed(normed_s, n_send)

        @pl.when(home == c)
        def _():
            landed(prs.at[pl.ds(0, chips - 1)], p_send)

        @pl.when(home != c)
        def _():
            landed(prs, p_send)

        @pl.when(c == 0)
        def _():
            for copy in (lend_a, lend_x, lend_n):
                copy.wait_send()
            landed(gp, lend_sems[3][0])

        @pl.when(c == 1)
        def _():
            col_sums.drain()
            landed(pcol, c_send)

        for copy in results:
            copy.wait()


def store_kernel(a_ref, b_ref, a_hbm, b_hbm, sem):
    copies = [
        pltpu.make_async_copy(a_ref, a_hbm, sem.at[0]),
        pltpu.make_async_copy(b_ref, b_hbm, sem.at[1]),
    ]
    for copy in copies:
        copy.start()
    for copy in copies:
        copy.wait()


def owned(
    patches, mask_token, masked, tissue, in_weight, out_weight, row_decay, col_decay, cotangent
):
    rows, cols, feat = patches.shape
    chips = lax.axis_size("gcol")
    toks, heads = chips * cols, row_decay.shape[0]
    half, part = out_weight.shape[1], in_weight.shape[1]
    width = 2 * half + 2 * N
    slab = feat // chips
    bf, fl = jnp.bfloat16, jnp.float32
    vmem, dma = pltpu.VMEM, pltpu.SemaphoreType.DMA
    anywhere = pl.BlockSpec(memory_space=pltpu.HBM)
    place = pl.BlockSpec(memory_space=pl.ANY)
    scale = 1.0 / math.sqrt(2 * rows * cols * chips)
    aux = heads + 8
    results = pl.pallas_call(
        functools.partial(layer_kernel, chips, rows, scale),
        name="layer",
        out_shape=(vmem(patches.shape, bf), vmem((slab // 2, 2 * half), fl)),
        in_specs=[anywhere] * 9,
        out_specs=(place, place),
        scratch_shapes=[
            dma((36,)), vmem(patches.shape, bf), vmem((slab // 2, 2 * half), fl),
            vmem((2,) + patches.shape, bf), vmem(mask_token.shape, bf),
            vmem((2,) + masked.shape, masked.dtype), vmem((2,) + row_decay.shape, fl),
            vmem((2, rows, cols, part), bf), vmem((2 * chips, cols, part), bf),
            vmem((rows, aux, cols), fl), vmem((rows, aux, cols), fl), vmem((chips, aux, cols), fl),
            vmem((width, part), bf), vmem((width, part), bf), vmem((width, part), bf), vmem(out_weight.shape, bf),
            vmem((toks, feat), bf), vmem((rows, cols, part), bf), vmem((2, toks, part // 2), bf),
            vmem((chips, cols, part), bf), vmem((rows, cols, part), bf), vmem((chips, cols, part), bf),
            vmem((toks, half), bf), vmem((2, toks, part // 2), bf),
            vmem((chips, cols, part), bf), vmem((toks, half // 2), bf), vmem((toks, half // 2), bf),
            vmem((toks, half), bf), vmem((toks, half), bf), vmem((toks, half), fl), vmem((toks, half), fl),
            vmem((toks, half), bf), vmem((toks, 2 * N), bf), vmem((toks, half), bf),
            vmem((toks, half), fl), vmem((toks, half), fl),
            vmem((heads, toks, toks), bf), vmem((heads, toks, toks), fl),
            vmem((toks, width), bf), vmem((toks, width), bf),
            vmem((chips, cols, part), bf), vmem((2, chips, cols, part), bf),
            vmem((2, rows, cols, part), bf), vmem((2, rows, cols, part), bf),
            vmem((half, half), fl), vmem((half, half // 2), fl),
            vmem((8, slab // 2, half), bf), vmem((8, slab // 2, half // 2), bf),
            vmem((4, slab // 2, half), bf), vmem((4, slab // 2, half // 2), bf),
            vmem((3, slab // 2, half), bf), vmem((6, slab // 2, half // 2), bf),
        ],
        compiler_params=pltpu.CompilerParams(
            collective_id=0, has_side_effects=True, vmem_limit_bytes=60 << 20
        ),
    )(
        patches, mask_token, cotangent, masked, tissue, row_decay, col_decay,
        in_weight, out_weight,
    )
    return pl.pallas_call(
        store_kernel,
        name="store",
        out_shape=tuple(jax.ShapeDtypeStruct(r.shape, r.dtype) for r in results),
        in_specs=[place] * 2,
        out_specs=[anywhere] * 2,
        scratch_shapes=[dma((2,))],
        compiler_params=pltpu.CompilerParams(vmem_limit_bytes=1 << 20),
    )(*results)


def body(*args):
    rows = args[0].shape[0]
    cols = args[0].shape[1]
    if lax.axis_size("grow") == 2 and rows == 4 and lax.axis_size("gcol") == 2 * rows and cols & (cols - 1) == 0:
        return owned(*args)
    return shards(*args)


def solution(mesh):
    return jax.shard_map(
        body,
        mesh=mesh,
        in_specs=(
            P(("groups", "grow"), "gcol", None),
            P(),
            P(("groups", "grow"), "gcol"),
            P(("groups", "grow"), "gcol"),
            P(None, "grow"),
            P(None, "grow"),
            P(None, ("groups", "grow"), "gcol"),
            P(None, ("groups", "grow"), "gcol"),
            P(("groups", "grow"), "gcol", None),
        ),
        out_specs=(P(("groups", "grow"), "gcol", None), P(("groups", "gcol", "grow"), None)),
        check_vma=False,
    )
```

```python
import functools
import itertools
import math

import jax
import jax.numpy as jnp
from jax import lax
from jax.experimental import pallas as pl
from jax.experimental.pallas import tpu as pltpu
from jax.sharding import PartitionSpec as P

E = 1024
HEADS = 16
N = 64


EPSILON = 1e-05
PRECISE = lax.Precision.HIGHEST


def prefix(value, axis, join, neutral):
    count, mine = (lax.axis_size(axis), lax.axis_index(axis))
    pieces = jax.tree.map(lambda part: lax.all_gather(part, axis), value)
    so_far = jax.tree.map(
        lambda part, zero: jnp.full_like(part, 0) + jnp.asarray(zero, part.dtype), value, neutral
    )

    def prefix_hop(position, so_far):
        longer = join(so_far, jax.tree.map(lambda part: part[position], pieces))
        return jax.tree.map(lambda new, old: jnp.where(position < mine, new, old), longer, so_far)

    return lax.fori_loop(0, count - 1, prefix_hop, so_far)


def carried_in(shard, axis, combine, identity):
    length, position = (lax.axis_size(axis), lax.axis_index(axis))
    everything = jax.tree.map(
        lambda part, kind: lax.all_gather(part.astype(kind), axis),
        shard,
        jax.tree.map(lambda a: jnp.bfloat16 if a.dtype == jnp.float32 else a.dtype, shard),
    )
    start = jax.tree.map(
        lambda part, zero: jnp.broadcast_to(jnp.asarray(zero, part.dtype), part.shape),
        shard,
        identity,
    )

    def carried_hop(k, before):
        at = length - 1 - k
        reached = at > position
        new = combine(
            before, jax.tree.map(lambda part, own: part[at].astype(own.dtype), everything, shard)
        )
        return jax.tree.map(lambda a, b: jnp.where(reached, a, b), new, before)

    return lax.fori_loop(0, length, carried_hop, start)


def shortened(shard):

    def short(part):
        return part.astype(jnp.bfloat16) if part.dtype == jnp.float32 else part

    return jax.tree.map(short, shard)


def silu_grad(pre_act):
    sigmoid_v = jax.nn.sigmoid(pre_act)
    return sigmoid_v * (1.0 + pre_act * (1.0 - sigmoid_v))


def per_channel(head_part, channels):
    return jnp.repeat(head_part, channels // head_part.shape[-1], axis=-1)


def line_form(head_lines, channels):
    return per_channel(head_lines.transpose(1, 2, 0), channels)


def carry_on(log_lines, state):
    return per_channel(jnp.exp(log_lines), state.shape[2])[:, None, :] * state


def prepare(log_decay):
    length = log_decay.shape[2]
    causal = jnp.arange(length)[:, None] >= jnp.arange(length)[None, :]
    running = jnp.einsum(
        "glk,tk->glt", log_decay, causal.astype(log_decay.dtype), precision=PRECISE
    )
    whole_log = running[:, :, -1]
    log_gaps = running[:, :, :, None] - running[:, :, None, :]
    decay_mat = jnp.where(causal, jnp.exp(jnp.where(causal, log_gaps, 0.0)), 0.0)
    return (running, whole_log, decay_mat)


def chain_link(earlier, later):
    return (earlier[0] + later[0], carry_on(later[0], earlier[1]) + later[1])


def split_heads(lines, head_count):
    line_count, length, channels = lines.shape
    return lines.reshape(line_count, length, head_count, channels // head_count)


def local_summary(inputs, key_vecs, prepared):
    running, whole_log, decay_mat = prepared
    to_end = line_form(jnp.exp(whole_log[:, :, None] - running), inputs.shape[2])
    fresh = jnp.einsum("ltc,ltn->lnc", inputs * to_end, key_vecs, precision=PRECISE)
    return (whole_log.T, fresh)


def local_return(query_vecs, prepared, upstream):
    running, whole_log, decay_mat = prepared
    from_start = line_form(jnp.exp(running), upstream.shape[2])
    backward = jnp.einsum("ltc,ltn->lnc", upstream * from_start, query_vecs, precision=PRECISE)
    return (whole_log.T, backward)


def local_outputs(inputs, key_vecs, query_vecs, prepared, incoming):
    running, whole_log, decay_mat = prepared
    head_count = decay_mat.shape[0]
    line_count, length, channels = inputs.shape
    scores = jnp.einsum("ltn,lkn->ltk", query_vecs, key_vecs, precision=PRECISE)
    within = jnp.einsum(
        "gltk,lkgp->ltgp",
        decay_mat * scores[None],
        split_heads(inputs, head_count),
        precision=PRECISE,
    )
    within = within.reshape(line_count, length, channels)
    carried = jnp.einsum("ltn,lnc->ltc", query_vecs, incoming, precision=PRECISE)
    return within + carried * line_form(jnp.exp(running), channels)


def local_grads(inputs, key_vecs, query_vecs, prepared, incoming, returning, upstream):
    running, whole_log, decay_mat = prepared
    head_count = decay_mat.shape[0]
    line_count, length, channels = inputs.shape
    from_start = line_form(jnp.exp(running), channels)
    to_end = line_form(jnp.exp(whole_log[:, :, None] - running), channels)
    scores = jnp.einsum("ltn,lkn->ltk", query_vecs, key_vecs, precision=PRECISE)
    heads_up = split_heads(upstream, head_count)
    heads_in = split_heads(inputs, head_count)
    grad_inputs = jnp.einsum(
        "gltk,ltgp->lkgp", decay_mat * scores[None], heads_up, precision=PRECISE
    ).reshape(line_count, length, channels)
    grad_inputs = (
        grad_inputs + jnp.einsum("lnc,lkn->lkc", returning, key_vecs, precision=PRECISE) * to_end
    )
    mixed = jnp.einsum("ltgp,lkgp->gltk", heads_up, heads_in, precision=PRECISE) * decay_mat
    grad_keys = jnp.einsum("gltk,ltn->lkn", mixed, query_vecs, precision=PRECISE)
    grad_keys = grad_keys + jnp.einsum(
        "lkc,lnc->lkn", inputs * to_end, returning, precision=PRECISE
    )
    grad_queries = jnp.einsum("gltk,lkn->ltn", mixed, key_vecs, precision=PRECISE)
    grad_queries = grad_queries + jnp.einsum(
        "ltc,lnc->ltn", upstream * from_start, incoming, precision=PRECISE
    )
    return (grad_inputs, grad_keys, grad_queries)


def shards(
    patches, mask_token, masked, tissue, in_weight, out_weight, row_decay, col_decay, cotangent
):
    grid_rows, grid_cols, feat_width = patches.shape
    tok_count = grid_rows * grid_cols
    chosen = (masked == 1)[:, :, None]
    present = tissue.astype(jnp.bfloat16)[:, :, None]
    model_in = jnp.where(chosen, mask_token[None, None, :], patches) * present
    flat_in = model_in.reshape(tok_count, feat_width)
    inner_width = E
    half_width = inner_width // 2
    state_size = N
    number_of_heads = HEADS // 2
    offset = 2 * inner_width
    full_in, full_out = (
        lax.all_gather(in_weight, "grow", axis=1, tiled=True),
        lax.all_gather(out_weight, "grow", axis=1, tiled=True),
    )
    projected = lax.dot_general(
        flat_in, full_in, (((1,), (1,)), ((), ())), preferred_element_type=jnp.float32
    )
    proj_bf = projected.astype(jnp.bfloat16)
    pre_values = proj_bf[:, :inner_width].astype(jnp.float32)
    gate_pre = proj_bf[:, inner_width:offset].astype(jnp.float32)
    key_rows = (
        proj_bf[:, offset : offset + state_size]
        .astype(jnp.float32)
        .reshape(grid_rows, grid_cols, state_size)
    )
    query_rows = (
        proj_bf[:, offset + state_size : offset + 2 * state_size]
        .astype(jnp.float32)
        .reshape(grid_rows, grid_cols, state_size)
    )
    key_cols = (
        proj_bf[:, offset + 2 * state_size : offset + 3 * state_size]
        .astype(jnp.float32)
        .reshape(grid_rows, grid_cols, state_size)
        .transpose(1, 0, 2)
    )
    query_cols = (
        proj_bf[:, offset + 3 * state_size : offset + 4 * state_size]
        .astype(jnp.float32)
        .reshape(grid_rows, grid_cols, state_size)
        .transpose(1, 0, 2)
    )
    values = jax.nn.silu(pre_values)
    row_inputs = values[:, :half_width].reshape(grid_rows, grid_cols, half_width)
    col_inputs = values[:, half_width:].reshape(grid_rows, grid_cols, half_width).transpose(1, 0, 2)
    row_prep = prepare(row_decay)
    col_prep = prepare(col_decay.transpose(0, 2, 1))
    row_zero = (
        jnp.zeros((grid_rows, number_of_heads), jnp.float32),
        jnp.zeros((grid_rows, state_size, half_width), jnp.float32),
    )
    col_zero = (
        jnp.zeros((grid_cols, number_of_heads), jnp.float32),
        jnp.zeros((grid_cols, state_size, half_width), jnp.float32),
    )
    row_entry = prefix(local_summary(row_inputs, key_rows, row_prep), "gcol", chain_link, row_zero)[
        1
    ]
    grow_size = lax.axis_size("grow")
    my_block = lax.axis_index("grow")
    parts_in, parts_key, parts_log = (
        lax.all_gather(
            proj_bf[:, half_width:inner_width].reshape(grid_rows, grid_cols, half_width),
            "grow",
            axis=0,
            tiled=True,
        ),
        lax.all_gather(
            proj_bf[:, offset + 2 * state_size : offset + 3 * state_size].reshape(
                grid_rows, grid_cols, state_size
            ),
            "grow",
            axis=0,
            tiled=True,
        ),
        lax.all_gather(
            col_decay.transpose(1, 0, 2).astype(jnp.bfloat16), "grow", axis=0, tiled=True
        ).astype(jnp.float32),
    )
    col_entry = col_zero[1]
    for block_idx in range(grow_size):
        lower_row = block_idx * grid_rows
        piece_in = jax.nn.silu(
            parts_in[lower_row : lower_row + grid_rows].astype(jnp.float32)
        ).transpose(1, 0, 2)
        piece_keys = (
            parts_key[lower_row : lower_row + grid_rows].astype(jnp.float32).transpose(1, 0, 2)
        )
        piece_log = parts_log[lower_row : lower_row + grid_rows].transpose(1, 2, 0)
        whole_log, piece_state = local_summary(piece_in, piece_keys, prepare(piece_log))
        moved = carry_on(whole_log, col_entry) + piece_state
        col_entry = jnp.where(block_idx < my_block, moved, col_entry)
    row_out = local_outputs(row_inputs, key_rows, query_rows, row_prep, row_entry)
    col_out = local_outputs(col_inputs, key_cols, query_cols, col_prep, col_entry).transpose(
        1, 0, 2
    )
    mixed = jnp.concatenate(
        [row_out.reshape(tok_count, half_width), col_out.reshape(tok_count, half_width)], axis=1
    )
    gate_act = jax.nn.silu(gate_pre)
    head_size = inner_width // HEADS
    gated = (mixed * gate_act).reshape(tok_count, HEADS, head_size)
    inv_rms = lax.rsqrt(jnp.mean(gated * gated, axis=2, keepdims=True) + EPSILON)
    normed = gated * inv_rms
    normed_bf = normed.reshape(tok_count, inner_width).astype(jnp.bfloat16)
    grad_out = (cotangent * masked.astype(jnp.bfloat16)[:, :, None]).reshape(tok_count, feat_width)
    total_patches = tok_count * lax.axis_size("gcol") * lax.axis_size("grow")
    weight_sum = lax.psum_scatter(
        lax.dot_general(
            grad_out, normed_bf, (((0,), (0,)), ((), ())), preferred_element_type=jnp.float32
        ),
        ("gcol", "grow"),
        scatter_dimension=0,
        tiled=True,
    )
    out_weight_grad = weight_sum * (1.0 / math.sqrt(total_patches))
    grad_normed_bf = jnp.dot(grad_out, full_out, preferred_element_type=jnp.float32).astype(
        jnp.bfloat16
    )
    grad_normed = lax.optimization_barrier(grad_normed_bf).astype(jnp.float32)
    grad_normed = grad_normed.reshape(tok_count, HEADS, head_size)
    grad_gated = inv_rms * (
        grad_normed - normed * jnp.mean(grad_normed * normed, axis=2, keepdims=True)
    )
    grad_gated = grad_gated.reshape(tok_count, inner_width)
    grad_mixed = grad_gated * gate_act
    grad_gate = grad_gated * mixed * silu_grad(gate_pre)
    row_up = grad_mixed[:, :half_width].reshape(grid_rows, grid_cols, half_width)
    col_up = grad_mixed[:, half_width:].reshape(grid_rows, grid_cols, half_width).transpose(1, 0, 2)
    row_exit = carried_in(local_return(query_rows, row_prep, row_up), "gcol", chain_link, row_zero)[
        1
    ]
    parts_up, parts_query = (
        lax.all_gather(
            shortened(grad_mixed[:, half_width:].reshape(grid_rows, grid_cols, half_width)),
            "grow",
            axis=0,
            tiled=True,
        ),
        lax.all_gather(
            proj_bf[:, offset + 3 * state_size : offset + 4 * state_size].reshape(
                grid_rows, grid_cols, state_size
            ),
            "grow",
            axis=0,
            tiled=True,
        ),
    )
    col_exit = col_zero[1]
    for block_idx in reversed(range(grow_size)):
        lower_row = block_idx * grid_rows
        piece_up = parts_up[lower_row : lower_row + grid_rows].transpose(1, 0, 2)
        piece_queries = (
            parts_query[lower_row : lower_row + grid_rows].astype(jnp.float32).transpose(1, 0, 2)
        )
        piece_log = parts_log[lower_row : lower_row + grid_rows].transpose(1, 2, 0)
        whole_log, piece_back = local_return(piece_queries, prepare(piece_log), piece_up)
        moved = carry_on(whole_log, col_exit) + piece_back
        col_exit = jnp.where(block_idx > my_block, moved, col_exit)
    grad_row_in, grad_row_key, grad_row_query = local_grads(
        row_inputs, key_rows, query_rows, row_prep, row_entry, row_exit, row_up
    )
    grad_col_in, grad_col_key, grad_col_query = local_grads(
        col_inputs, key_cols, query_cols, col_prep, col_entry, col_exit, col_up
    )
    grad_values = jnp.concatenate(
        [
            grad_row_in.reshape(tok_count, half_width),
            grad_col_in.transpose(1, 0, 2).reshape(tok_count, half_width),
        ],
        axis=1,
    )
    grad_proj = jnp.concatenate(
        [
            grad_values * silu_grad(pre_values),
            grad_gate,
            grad_row_key.reshape(tok_count, state_size),
            grad_row_query.reshape(tok_count, state_size),
            grad_col_key.transpose(1, 0, 2).reshape(tok_count, state_size),
            grad_col_query.transpose(1, 0, 2).reshape(tok_count, state_size),
        ],
        axis=1,
    ).astype(jnp.bfloat16)
    keep_mask = present * (1 - masked).astype(jnp.bfloat16)[:, :, None]
    grad_model_in = jnp.dot(grad_proj, full_in, preferred_element_type=jnp.float32).reshape(
        grid_rows, grid_cols, feat_width
    )
    patch_grad = (grad_model_in * keep_mask).astype(jnp.bfloat16)
    return (patch_grad, out_weight_grad)


MESH = pl.DeviceIdType.MESH
NT = (((1,), (1,)), ((), ()))
NN = (((1,), (0,)), ((), ()))
TN = (((0,), (0,)), ((), ()))


def mm(a, b, dims):
    return lax.dot_general(a, b, dims, preferred_element_type=jnp.float32)


def layer_kernel(
    chips, rows, scale,
    patch_hbm, token_hbm, cot_hbm, hidden_hbm, present_hbm, rdec_hbm, cdec_hbm, w_hbm, wout_hbm,
    pg_out, sum_out,
    sems, pg_ref, out_ref, pair_ref, token_ref, flag_ref, dec_ref,
    ms, mb, rd, cd, db, wa, wb, wr, wout, gb, gsr, ga, gx, gsx, gcx, nx, la, lx, ln, lnx, u_s, z_s, su_s, sz_s, gn_s, bc_s,
    normed_s, y_s, inv_s, mat_s, dec_s, turned_s, run_a, run_b, gp, prs, pcs, prow, pcol,
    wc, wq, zs, zq, zc, zcq, zr, zrq,
):
    k, c = lax.axis_index("gcol"), lax.axis_index("grow")
    depth = chips // 2
    zi, xi = k // 2, lax.rem(k, 2)
    cols = ms.shape[2]
    toks = chips * cols
    feat, half, part = token_ref.shape[0], wout.shape[1], wa.shape[1]
    heads, width = dec_ref.shape[1], wa.shape[0]
    total = 2 * chips
    slab = feat // chips
    scope = jax.named_scope
    ids = itertools.count()

    def new_sem():
        return sems.at[next(ids)]

    def landed(ref, sem):
        pltpu.make_async_copy(ref, ref, sem).wait()

    me = 2 * k + c
    barrier = pltpu.get_barrier_semaphore()
    for d in range(1, total):
        to = lax.rem(me + d, total)
        pl.semaphore_signal(
            barrier, inc=1, device_id={"gcol": to // 2, "grow": lax.rem(to, 2)}, device_id_type=MESH
        )

    side = zi // 2
    mate = zi + 1 - 2 * lax.rem(zi, 2)
    near_far, end_far = 2 - side, 3 - 3 * side
    order = (end_far, near_far, mate, zi)
    outer = zi == 3 * side
    inner = jnp.logical_not(outer)
    beside = 2 * zi + 1 - xi

    def block(q):
        return pl.ds(pl.multiple_of(q * slab, slab), slab)

    pieces = ((0, 0, half), (2 * half, half, half), (4 * half, 2 * half, 2 * N))

    def packed(ref, core):
        return [
            (ref.at[pl.ds(pl.multiple_of(base + core * size, 128), size)], pl.ds(at, size))
            for base, at, size in pieces
        ]

    in_sem = [new_sem() for _ in range(4)]
    loads = [
        pltpu.make_async_copy(src, dst, s)
        for src, dst, s in (
            (hidden_hbm, flag_ref.at[0], in_sem[0]), (present_hbm, flag_ref.at[1], in_sem[0]),
            (token_hbm, token_ref, in_sem[1]),
            (rdec_hbm, dec_ref.at[0], in_sem[2]), (cdec_hbm, dec_ref.at[1], in_sem[2]),
            (patch_hbm, pair_ref.at[0], in_sem[3]), (cot_hbm, pair_ref.at[1], in_sem[3]),
        )
    ]
    for copy in loads:
        copy.start()
    load_w = [pltpu.make_async_copy(src, wa.at[at], in_sem[0]) for src, at in packed(w_hbm, c)]
    load_o = pltpu.make_async_copy(wout_hbm, wout, in_sem[1])
    load_r = [pltpu.make_async_copy(src, wr.at[at], in_sem[2]) for src, at in packed(w_hbm, 1 - c)]
    patch_ref, cot_ref = pair_ref.at[0], pair_ref.at[1]

    def remote(src, dst, s, r, chip, core):
        return pltpu.make_async_remote_copy(
            src_ref=src, dst_ref=dst, send_sem=s, recv_sem=r,
            device_id={"gcol": chip, "grow": core}, device_id_type=MESH,
        )

    def across_lanes(column):
        one = jnp.broadcast_to(column, (column.shape[0], 128)).astype(jnp.bfloat16)
        return jnp.concatenate([one] * (part // 128), axis=1)

    with scope("prep"):
        for ref, sem in zip((flag_ref, token_ref, dec_ref, pair_ref), in_sem):
            landed(ref, sem)
        for copy in load_w:
            copy.start()
        load_o.start()
        for copy in load_r:
            copy.start()
        square = (cols, cols)
        eye = lax.broadcasted_iota(jnp.int32, square, 0) == lax.broadcasted_iota(jnp.int32, square, 1)
        eye = eye.astype(jnp.float32)
        hidden_f, present_f = flag_ref[0].astype(jnp.float32), flag_ref[1].astype(jnp.float32)
        hidden_t, present_t = mm(eye, hidden_f, NT), mm(eye, present_f, NT)
        visible_t = present_t * (1.0 - hidden_t)
        for i in range(rows):
            hidden, visible = across_lanes(hidden_t[:, i : i + 1]), across_lanes(visible_t[:, i : i + 1])
            for f in range(2):
                at = slice(f * part, (f + 1) * part)
                ms[f, i] = patch_ref[i, :, at] * visible + cot_ref[i, :, at] * hidden
            for q in range(depth):
                at = slice(q * slab, (q + 1) * slab)
                gsx[i, :, at] = cot_ref[i, :, block(2 * q + 1 - xi)] * hidden[:, :slab]
                turn = (2 * q + 1 - i % 2) * slab
                gsr[i, :, at] = cot_ref[i, :, turn : turn + slab] * hidden[:, :slab]
            blank = jnp.zeros((rd.shape[1] - heads - 2, cols), jnp.float32)
            flags = jnp.concatenate([hidden_f[i : i + 1], present_f[i : i + 1], blank], axis=0)
            for n, dst in enumerate((rd, cd)):
                dst[i, :heads] = dec_ref[n, :, i, :]
                dst[i, heads:] = flags

    m_send, d_send, g_send, gc_send, w_send, n_send, p_send, c_send = [new_sem() for _ in range(8)]
    m_recv, (d_recv, g_recv, gc_recv, w_recv, n_recv, nr_recv, p_recv, c_recv) = (
        [sems.at[next(ids)] for _ in range(2)], [new_sem() for _ in range(8)]
    )

    g_col = remote(gsx, gcx.at[pl.ds(rows * c, rows)], gc_send, gc_recv, beside, 1)

    def g_row(i):
        return remote(gsr.at[i], gx.at[k], g_send, g_recv, rows * c + (i ^ 1), 0)

    def m_row(f, i):
        return remote(ms.at[f, i], mb.at[f * chips + k], m_send, m_recv[f], rows * c + i, 0)

    def m_col(f):
        return remote(ms.at[f], mb.at[pl.ds(f * chips, rows)], m_send, m_recv[f], k, 1)

    def d_row(i):
        return remote(rd.at[i], db.at[k], d_send, d_recv, rows * c + i, 0)

    d_col = remote(cd, db.at[pl.ds(0, rows)], d_send, d_recv, k, 1)

    def not_me(i):
        return jnp.logical_or(c == 1, k != i)

    def each_row(copy_of, owner=lambda i: i):
        for i in range(rows):

            @pl.when(not_me(owner(i)))
            def _():
                copy_of(i).start()

    def each_g_row():
        each_row(g_row, lambda i: i ^ 1)

    def drained(ref, sem, count, own, extra):
        @pl.when(c == 1)
        def _():
            landed(ref.at[pl.ds(0, count)], sem)

        for mine, less in ((k < rows, own), (k >= rows, 0)):

            @pl.when(jnp.logical_and(c == 0, mine))
            def _():
                landed(ref.at[pl.ds(0, count - less + extra)], sem)

    w_out = remote(wr, wb, w_send, w_recv, k, 1 - c)
    with scope("own_rows"):
        @pl.when(c == 1)
        def _():
            pltpu.make_async_copy(cd, db.at[pl.ds(rows, rows)], d_recv).start()
            for f in range(2):
                pltpu.make_async_copy(ms.at[f], mb.at[pl.ds(f * chips + rows, rows)], m_recv[f]).start()

        for i in range(rows):

            @pl.when(jnp.logical_and(c == 0, k == i))
            def _():
                pltpu.make_async_copy(rd.at[i], db.at[i], d_recv).start()
                pltpu.make_async_copy(gsr.at[i ^ 1], gx.at[i], g_recv).start()
                for f in range(2):
                    pltpu.make_async_copy(ms.at[f, i], mb.at[f * chips + i], m_recv[f]).start()

    with scope("barrier_wait"):
        pl.semaphore_wait(barrier, total - 1)
    with scope("launch"):
        each_row(d_row)

        @pl.when(c == 0)
        def _():
            d_col.start()
            m_col(1).start()
            m_col(0).start()

        for f in range(2):
            each_row(functools.partial(m_row, f))
        landed(wr, in_sem[2])
        w_out.start()
        g_col.start()

    t_at = lax.broadcasted_iota(jnp.int32, (toks, toks), 0)
    k_at = lax.broadcasted_iota(jnp.int32, (toks, toks), 1)
    gap_at = t_at - k_at
    mask = jnp.logical_and(gap_at >= 0, (gap_at & (cols - 1)) * c == 0)
    low = lax.broadcasted_iota(jnp.int32, (toks, 128), 1) < N
    same = (128, 128)
    head_of = [lax.broadcasted_iota(jnp.int32, same, d) // N for d in range(2)]
    averages = jnp.where(head_of[0] == head_of[1], 1.0 / N, 0.0).astype(jnp.bfloat16)

    with scope("arrive_decay"):
        landed(db, d_recv)
    with scope("decay"):
        ones = mask.astype(jnp.float32)
        dec = jnp.concatenate([db[i] for i in range(chips)], axis=1)
        run_s = lax.dot_general(ones, dec, NT, precision=PRECISE, preferred_element_type=jnp.float32)
        run_l = lax.dot_general(dec, ones, NT, precision=PRECISE, preferred_element_type=jnp.float32)
        run_a[...], run_b[...] = run_s, run_l
        for h in range(heads):
            gap = run_s[:, h : h + 1] - run_l[h : h + 1, :]
            dec_s[h] = jnp.where(mask, jnp.exp(jnp.minimum(gap, 0.0)), 0.0)
        unit = (t_at == k_at).astype(jnp.float32)
        flags_t = mm(unit, dec[heads:], NT)
        tok_hidden, tok_filled = across_lanes(flags_t[:, 0:1]), across_lanes(flags_t[:, 0:1] * flags_t[:, 1:2])
        tok_shown = across_lanes(1.0 - flags_t[:, 0:1])

    with scope("load_w"):
        landed(wa, in_sem[0])
        landed(wout, in_sem[1])

    def turn_decay():
        late = k_at - t_at
        reach = jnp.logical_and(late >= 0, (late & (cols - 1)) * c == 0)
        for h in range(heads):
            gap = run_b[h : h + 1, :] - run_a[:, h : h + 1]
            turned_s[h] = jnp.where(reach, jnp.exp(jnp.minimum(gap, 0.0)), 0.0)

    def halves(ref):
        return jnp.concatenate([ref[0], ref[1]], axis=1)

    def unpack(f):
        at = pl.ds(pl.multiple_of(f * part, part), part)
        either = mb[pl.ds(f * chips, chips)].reshape(toks, part)
        gb[:, at] = either * tok_hidden
        return either * tok_shown + token_ref[at].reshape(1, part) * tok_filled

    def split(f):
        for i in range(depth // 2):
            q = f * (depth // 2) + i
            at_i = slice(i * slab, (i + 1) * slab)
            ga[f, :, at_i] = gb[:, block(2 * q + xi)]

    def half_gn(f):
        at = pl.ds(pl.multiple_of(f * part, part), part)
        return mm(gb[:, at], wout[at, :], NN)

    def arrive_m(core):
        for f in range(2):

            @pl.when(core == f)
            def _():
                landed(mb.at[pl.ds(f * chips, chips)], m_recv[f])

    lend_sems = [(new_sem(), new_sem()) for _ in range(3)]

    def lend(i, src, dst):
        return remote(src, dst, *lend_sems[i], k, 1)

    pair = [pl.ds(i * 256, 256) for i in range(4)]
    lend_a = lend(0, ga, la)
    lend_x = lend(1, gx, lx)
    lend_n = lend(2, normed_s.at[:, pair[1]], ln)
    n_first = remote(normed_s.at[:, pair[0]], nx.at[:, pair[0]], n_send, n_recv, beside, c)
    n_col = remote(normed_s.at[:, pair[1]], nx.at[:, pair[1]], n_send, n_recv, beside, 1)
    n_row = remote(normed_s.at[:, pair[1]], lnx, n_send, nr_recv, beside, 1)
    with scope("arrive_first"):
        arrive_m(c)
    with scope("proj_first"):
        own = unpack(c)
        firsts = [mm(own, wa[at : at + size], NT) for _, at, size in pieces]
        split(c)
        gn_first = half_gn(c)

        @pl.when(c == 0)
        def _():
            each_g_row()
            turn_decay()

    with scope("arrive_second"):
        arrive_m(1 - c)
    with scope("weights_wait"):
        landed(wb, w_recv)
    with scope("proj_second"):
        oth = unpack(1 - c)
        for dst, (_, at, size), first in zip((u_s, z_s, bc_s), pieces, firsts):
            dst[...] = (first + mm(oth, wb[at : at + size], NT)).astype(jnp.bfloat16)
        split(1 - c)


    def per_head(x):
        high = x.astype(jnp.bfloat16)
        rest = (x - high.astype(jnp.float32)).astype(jnp.bfloat16)
        return mm(high, averages, NN) + mm(rest, averages, NN)

    def if_core(core, copies):
        @pl.when(c == core)
        def _():
            for copy in copies:
                copy.start()

    if_core(0, [lend_a])

    with scope("forward"):
        b_bf, c_bf = bc_s[:, :N], bc_s[:, N:]
        scores = mm(c_bf, b_bf, NT)
        rest_at = pl.ds(pl.multiple_of((1 - c) * part, part), part)
        for p in range(half // 128):
            cols_p = slice(p * 128, (p + 1) * 128)
            if p >= 2:
                two = slice((p - 2) * 256, (p - 1) * 256)
                gn = gn_first[:, two] + mm(gb[:, rest_at], wout[rest_at, two], NN)
                gn_s[:, two] = gn.astype(jnp.bfloat16)
            u = u_s[:, cols_p].astype(jnp.float32)
            sig_u = 0.5 + 0.5 * jnp.tanh(0.5 * u)
            su_s[:, cols_p] = sig_u
            val_bf = (u * sig_u).astype(jnp.bfloat16)
            for h in (2 * p, 2 * p + 1):
                mat_s[h] = (dec_s[h] * scores).astype(jnp.bfloat16)
            y = jnp.where(low, mm(mat_s[2 * p], val_bf, NN), mm(mat_s[2 * p + 1], val_bf, NN))
            y_s[:, cols_p] = y
            z = z_s[:, cols_p].astype(jnp.float32)
            sig_z = 0.5 + 0.5 * jnp.tanh(0.5 * z)
            sz_s[:, cols_p] = sig_z
            gated = y * (z * sig_z)
            inv = lax.rsqrt(per_head(gated * gated) + EPSILON)
            inv_s[:, cols_p] = inv
            normed_s[:, cols_p] = (gated * inv).astype(jnp.bfloat16)
            if p == 1:
                n_first.start()
            if p == 3:
                if_core(1, [n_col])

                @pl.when(c == 1)
                def _():
                    each_g_row()

                if_core(0, [n_row, lend_n])

    with scope("turn_decay"):
        @pl.when(c == 1)
        def _():
            turn_decay()

    with scope("backward"):
        turned_scores = mm(b_bf, c_bf, NT)
        d_scores = jnp.zeros((toks, toks), jnp.float32)
        for p in range(half // 128):
            cols_p = slice(p * 128, (p + 1) * 128)
            z, sig_z, y, inv = z_s[:, cols_p].astype(jnp.float32), sz_s[:, cols_p], y_s[:, cols_p], inv_s[:, cols_p]
            act = z * sig_z
            normed = y * act * inv
            u, sig_u = u_s[:, cols_p].astype(jnp.float32), su_s[:, cols_p]
            val = u * sig_u
            val_bf = val.astype(jnp.bfloat16)
            gn = gn_s[:, cols_p].astype(jnp.float32)
            gg = inv * (gn - normed * per_head(gn * normed))
            dy = gg * act
            dz = gg * y * (sig_z + act * (1.0 - sig_z))
            dy_bf = dy.astype(jnp.bfloat16)
            dec_a, dec_b = turned_s[2 * p], turned_s[2 * p + 1]
            dv = jnp.where(
                low,
                mm((dec_a * turned_scores).astype(jnp.bfloat16), dy_bf, NN),
                mm((dec_b * turned_scores).astype(jnp.bfloat16), dy_bf, NN),
            )
            du = dv * (sig_u + val * (1.0 - sig_u))
            gp[:, cols_p] = du.astype(jnp.bfloat16)
            gp[:, half + p * 128 : half + (p + 1) * 128] = dz.astype(jnp.bfloat16)
            zero = jnp.zeros_like(dy)
            d_scores += dec_a * mm(val_bf, jnp.where(low, dy, zero).astype(jnp.bfloat16), NT)
            d_scores += dec_b * mm(val_bf, jnp.where(low, zero, dy).astype(jnp.bfloat16), NT)
        ds_bf = d_scores.astype(jnp.bfloat16)
        d_bc = jnp.concatenate([mm(ds_bf, c_bf, NN), mm(ds_bf, b_bf, TN)], axis=1)
        gp[:, 2 * half :] = d_bc.astype(jnp.bfloat16)

    with scope("pass_gx"):

        @pl.when(c == 0)
        def _():
            landed(gx, g_recv)

        if_core(0, [lend_x])

    home, slot = k // rows, lax.rem(k, rows)

    def row_back(f, chip):
        return remote(prs.at[f, chip], prow.at[f, slot], p_send, p_recv, chip, home)

    def col_back(n):
        return remote(pcs.at[pl.ds(n * chips, rows)], pcol.at[n], c_send, c_recv, k, 0)

    others = [
        2 * z + x
        for z in (3 - zi, lax.rem(zi + 2, depth), mate)
        for x in (1 - xi, xi)
    ] + [2 * zi + 1 - xi]

    def project_back(g_ref, w_ref):
        return mm(g_ref[...], w_ref[...], NN).astype(jnp.bfloat16).reshape(chips, cols, part)

    def return_rows(f):
        for chip in others:
            row_back(f, chip).start()

        @pl.when(home == 1)
        def _():
            row_back(f, k).start()

        @pl.when(home == 0)
        def _():
            pltpu.make_async_copy(prs.at[f, k], prow.at[f, slot], p_recv).start()

    class Sums:
        def __init__(self, w, z, zin, zout, slot):
            self.w, self.z, self.zin, self.zout, self.slot = w, z, zin, zout, slot
            self.send, self.out_recv, *self.in_recv = [new_sem() for _ in range(4)]

        def to_target(self, j, kind, chip, core):
            return remote(
                self.z.at[2 * j + core], self.zout.at[3 * self.slot + kind], self.send, self.out_recv, chip, core
            )

        def part(self, j):
            return self.w[block(order[j]), :]

        def ready(self, j, value):
            self.z[2 * j : 2 * j + 2] = value.astype(jnp.bfloat16).reshape(2, slab // 2, value.shape[1])

        def begin(self):
            @pl.when(outer)
            def _():
                for j in range(2):
                    self.ready(j, self.part(j))
                    two = pl.ds(2 * j, 2)
                    remote(
                        self.z.at[two], self.zin.at[two], self.send, self.in_recv[j], 2 * mate + xi, c
                    ).start()

            self.ready(2, self.part(2))
            for core in range(2):
                self.to_target(2, 0, 2 * mate + xi, core).start()
            self.ready(3, self.part(3))
            pltpu.make_async_copy(
                self.z.at[6 + c], self.zout.at[3 * self.slot + 2], self.out_recv
            ).start()
            self.to_target(3, 2, k, 1 - c).start()

        def combine(self):
            @pl.when(inner)
            def _():
                for j in range(2):
                    landed(self.zin.at[pl.ds(2 * j, 2)], self.in_recv[j])
                    passed = self.zin[2 * j : 2 * j + 2].astype(jnp.float32).reshape(slab, self.w.shape[1])
                    self.ready(j, self.part(j) + passed)
                    for core in range(2):
                        self.to_target(j, 1, 2 * order[j] + xi, core).start()

        def drain(self):
            landed(self.z.at[pl.ds(0, 7)], self.send)

    col_sums = Sums(wc, zs, zc, zr, 0)
    row_sums = Sums(wq, zq, zcq, zrq, c)

    @pl.when(c == 0)
    def _():
        with scope("back_project_0"):
            for f, w_ref in enumerate((wa, wb)):
                prs[f] = project_back(gp, w_ref)

                @pl.when(inner)
                def _():
                    return_rows(f)

        with scope("wait_n0"):
            landed(nx.at[:, pair[0]], n_recv)
        with scope("row_product_0"):
            wq[...] = mm(halves(ga), normed_s[:, :256], TN) + mm(gx[...].reshape(toks, part), nx[:, :256], TN)

    @pl.when(c == 1)
    def _():
        with scope("col_back_1"):
            for n, w_ref in enumerate((wa, wb)):
                pcs[n * chips : (n + 1) * chips] = project_back(gp, w_ref)
                col_back(n).start()
                pcol[n] = pcs[n * chips + rows : (n + 1) * chips]
        with scope("wait_n1"):
            landed(gcx, gc_recv)
            landed(nx, n_recv)
        with scope("col_product"):
            wc[...] = mm(halves(ga), normed_s[...], TN) + mm(gcx[...].reshape(toks, part), nx[...], TN)
            col_sums.begin()
        with scope("lent_wait"):
            for copy in (lend_a, lend_x, lend_n, n_row):
                copy.wait_recv()
        with scope("row_product_1"):
            wq[...] = mm(halves(la), ln[...], TN) + mm(lx[...].reshape(toks, part), lnx[...], TN)

    with scope("row_begin"):
        row_sums.begin()

    with scope("return_rows"):
        @pl.when(jnp.logical_and(c == 0, outer))
        def _():
            for f in range(2):
                return_rows(f)


    @pl.when(c == 1)
    def _():
        with scope("col_combine"):
            col_sums.combine()

    with scope("row_combine"):
        row_sums.combine()

    with scope("parts_wait"):

        @pl.when(c == 0)
        def _():
            landed(pcol, c_recv)

        landed(prow, p_recv)

    with scope("patch_grad"):
        for f in range(2):
            by_row, by_col = prow.at[f], pcol.at[1 - f]
            for i in range(rows):
                keep = visible_t[:, i : i + 1]
                both = by_row[i].astype(jnp.float32) + by_col[i].astype(jnp.float32)
                pg_ref[i, :, f * part : (f + 1) * part] = (both * keep).astype(pg_ref.dtype)

    results = [
        pltpu.make_async_copy(pg_ref, pg_out, in_sem[0]),
        pltpu.make_async_copy(out_ref, sum_out, in_sem[1]),
    ]
    results[0].start()

    with scope("sums_wait"):
        landed(zr, col_sums.out_recv)
        landed(zrq, row_sums.out_recv)

    with scope("weight_sum"):
        for ref, at, size in ((zrq.at[0:3], 0, 256), (zrq.at[3:6], 256, 256), (zr, half, half)):
            acc = ref[0].astype(jnp.float32) + ref[1].astype(jnp.float32)
            acc += ref[2].astype(jnp.float32)
            out_ref[:, at : at + size] = acc * scale
    results[1].start()

    with scope("drain"):
        drained(db, d_send, rows, 1, rows)
        drained(mb, m_send, 2 * rows, 2, 2 * rows)
        drained(gx, g_send, rows, 1, 0)
        landed(gsx, gc_send)
        landed(wb, w_send)
        row_sums.drain()
        landed(normed_s, n_send)

        @pl.when(jnp.logical_and(c == 0, home == 0))
        def _():
            landed(pcs.at[pl.ds(0, 2 * chips - 2)], p_send)

        @pl.when(jnp.logical_and(c == 0, home == 1))
        def _():
            landed(pcs, p_send)

        @pl.when(c == 0)
        def _():
            for copy in (lend_a, lend_x, lend_n):
                copy.wait_send()

        @pl.when(c == 1)
        def _():
            col_sums.drain()
            landed(pcol, c_send)

        for copy in results:
            copy.wait()


def store_kernel(a_ref, b_ref, a_hbm, b_hbm, sem):
    copies = [
        pltpu.make_async_copy(a_ref, a_hbm, sem.at[0]),
        pltpu.make_async_copy(b_ref, b_hbm, sem.at[1]),
    ]
    for copy in copies:
        copy.start()
    for copy in copies:
        copy.wait()


def owned(
    patches, mask_token, masked, tissue, in_weight, out_weight, row_decay, col_decay, cotangent
):
    rows, cols, feat = patches.shape
    chips = lax.axis_size("gcol")
    toks, heads = chips * cols, row_decay.shape[0]
    half, part = out_weight.shape[1], in_weight.shape[1]
    width = 2 * half + 2 * N
    slab = feat // chips
    bf, fl = jnp.bfloat16, jnp.float32
    vmem, dma = pltpu.VMEM, pltpu.SemaphoreType.DMA
    anywhere = pl.BlockSpec(memory_space=pltpu.HBM)
    place = pl.BlockSpec(memory_space=pl.ANY)
    scale = 1.0 / math.sqrt(2 * rows * cols * chips)
    aux = heads + 8
    results = pl.pallas_call(
        functools.partial(layer_kernel, chips, rows, scale),
        name="layer",
        out_shape=(vmem(patches.shape, bf), vmem((slab // 2, 2 * half), fl)),
        in_specs=[anywhere] * 9,
        out_specs=(place, place),
        scratch_shapes=[
            dma((36,)), vmem(patches.shape, bf), vmem((slab // 2, 2 * half), fl),
            vmem((2,) + patches.shape, bf), vmem(mask_token.shape, bf),
            vmem((2,) + masked.shape, masked.dtype), vmem((2,) + row_decay.shape, fl),
            vmem((2, rows, cols, part), bf), vmem((2 * chips, cols, part), bf),
            vmem((rows, aux, cols), fl), vmem((rows, aux, cols), fl), vmem((chips, aux, cols), fl),
            vmem((width, part), bf), vmem((width, part), bf), vmem((width, part), bf), vmem(out_weight.shape, bf),
            vmem((toks, feat), bf), vmem((rows, cols, part), bf), vmem((2, toks, part // 2), bf),
            vmem((chips, cols, part), bf), vmem((rows, cols, part), bf), vmem((chips, cols, part), bf),
            vmem((toks, half), bf), vmem((2, toks, part // 2), bf),
            vmem((chips, cols, part), bf), vmem((toks, half // 2), bf), vmem((toks, half // 2), bf),
            vmem((toks, half), bf), vmem((toks, half), bf), vmem((toks, half), fl), vmem((toks, half), fl),
            vmem((toks, half), bf), vmem((toks, 2 * N), bf), vmem((toks, half), bf),
            vmem((toks, half), fl), vmem((toks, half), fl),
            vmem((heads, toks, toks), bf), vmem((heads, toks, toks), fl),
            vmem((heads, toks, toks), fl), vmem((toks, aux), fl), vmem((aux, toks), fl),
            vmem((toks, width), bf), vmem((2, chips, cols, part), bf), vmem((2 * chips, cols, part), bf),
            vmem((2, rows, cols, part), bf), vmem((2, rows, cols, part), bf),
            vmem((half, half), fl), vmem((half, half // 2), fl),
            vmem((8, slab // 2, half), bf), vmem((8, slab // 2, half // 2), bf),
            vmem((4, slab // 2, half), bf), vmem((4, slab // 2, half // 2), bf),
            vmem((3, slab // 2, half), bf), vmem((6, slab // 2, half // 2), bf),
        ],
        compiler_params=pltpu.CompilerParams(
            collective_id=0, has_side_effects=True, vmem_limit_bytes=60 << 20
        ),
    )(
        patches, mask_token, cotangent, masked, tissue, row_decay, col_decay,
        in_weight, out_weight,
    )
    return pl.pallas_call(
        store_kernel,
        name="store",
        out_shape=tuple(jax.ShapeDtypeStruct(r.shape, r.dtype) for r in results),
        in_specs=[place] * 2,
        out_specs=[anywhere] * 2,
        scratch_shapes=[dma((2,))],
        compiler_params=pltpu.CompilerParams(vmem_limit_bytes=1 << 20),
    )(*results)


def body(*args):
    rows = args[0].shape[0]
    cols = args[0].shape[1]
    if lax.axis_size("grow") == 2 and rows == 4 and lax.axis_size("gcol") == 2 * rows and cols & (cols - 1) == 0:
        return owned(*args)
    return shards(*args)


def solution(mesh):
    return jax.shard_map(
        body,
        mesh=mesh,
        in_specs=(
            P(("groups", "grow"), "gcol", None),
            P(),
            P(("groups", "grow"), "gcol"),
            P(("groups", "grow"), "gcol"),
            P(None, "grow"),
            P(None, "grow"),
            P(None, ("groups", "grow"), "gcol"),
            P(None, ("groups", "grow"), "gcol"),
            P(("groups", "grow"), "gcol", None),
        ),
        out_specs=(P(("groups", "grow"), "gcol", None), P(("groups", "gcol", "grow"), None)),
        check_vma=False,
    )
```

```python
import functools
import itertools
import math

import jax
import jax.numpy as jnp
from jax import lax
from jax.experimental import pallas as pl
from jax.experimental.pallas import tpu as pltpu
from jax.sharding import PartitionSpec as P

E = 1024
HEADS = 16
N = 64


EPSILON = 1e-05
PRECISE = lax.Precision.HIGHEST


def prefix(value, axis, join, neutral):
    count, mine = (lax.axis_size(axis), lax.axis_index(axis))
    pieces = jax.tree.map(lambda part: lax.all_gather(part, axis), value)
    so_far = jax.tree.map(
        lambda part, zero: jnp.full_like(part, 0) + jnp.asarray(zero, part.dtype), value, neutral
    )

    def prefix_hop(position, so_far):
        longer = join(so_far, jax.tree.map(lambda part: part[position], pieces))
        return jax.tree.map(lambda new, old: jnp.where(position < mine, new, old), longer, so_far)

    return lax.fori_loop(0, count - 1, prefix_hop, so_far)


def carried_in(shard, axis, combine, identity):
    length, position = (lax.axis_size(axis), lax.axis_index(axis))
    everything = jax.tree.map(
        lambda part, kind: lax.all_gather(part.astype(kind), axis),
        shard,
        jax.tree.map(lambda a: jnp.bfloat16 if a.dtype == jnp.float32 else a.dtype, shard),
    )
    start = jax.tree.map(
        lambda part, zero: jnp.broadcast_to(jnp.asarray(zero, part.dtype), part.shape),
        shard,
        identity,
    )

    def carried_hop(k, before):
        at = length - 1 - k
        reached = at > position
        new = combine(
            before, jax.tree.map(lambda part, own: part[at].astype(own.dtype), everything, shard)
        )
        return jax.tree.map(lambda a, b: jnp.where(reached, a, b), new, before)

    return lax.fori_loop(0, length, carried_hop, start)


def shortened(shard):

    def short(part):
        return part.astype(jnp.bfloat16) if part.dtype == jnp.float32 else part

    return jax.tree.map(short, shard)


def silu_grad(pre_act):
    sigmoid_v = jax.nn.sigmoid(pre_act)
    return sigmoid_v * (1.0 + pre_act * (1.0 - sigmoid_v))


def per_channel(head_part, channels):
    return jnp.repeat(head_part, channels // head_part.shape[-1], axis=-1)


def line_form(head_lines, channels):
    return per_channel(head_lines.transpose(1, 2, 0), channels)


def carry_on(log_lines, state):
    return per_channel(jnp.exp(log_lines), state.shape[2])[:, None, :] * state


def prepare(log_decay):
    length = log_decay.shape[2]
    causal = jnp.arange(length)[:, None] >= jnp.arange(length)[None, :]
    running = jnp.einsum(
        "glk,tk->glt", log_decay, causal.astype(log_decay.dtype), precision=PRECISE
    )
    whole_log = running[:, :, -1]
    log_gaps = running[:, :, :, None] - running[:, :, None, :]
    decay_mat = jnp.where(causal, jnp.exp(jnp.where(causal, log_gaps, 0.0)), 0.0)
    return (running, whole_log, decay_mat)


def chain_link(earlier, later):
    return (earlier[0] + later[0], carry_on(later[0], earlier[1]) + later[1])


def split_heads(lines, head_count):
    line_count, length, channels = lines.shape
    return lines.reshape(line_count, length, head_count, channels // head_count)


def local_summary(inputs, key_vecs, prepared):
    running, whole_log, decay_mat = prepared
    to_end = line_form(jnp.exp(whole_log[:, :, None] - running), inputs.shape[2])
    fresh = jnp.einsum("ltc,ltn->lnc", inputs * to_end, key_vecs, precision=PRECISE)
    return (whole_log.T, fresh)


def local_return(query_vecs, prepared, upstream):
    running, whole_log, decay_mat = prepared
    from_start = line_form(jnp.exp(running), upstream.shape[2])
    backward = jnp.einsum("ltc,ltn->lnc", upstream * from_start, query_vecs, precision=PRECISE)
    return (whole_log.T, backward)


def local_outputs(inputs, key_vecs, query_vecs, prepared, incoming):
    running, whole_log, decay_mat = prepared
    head_count = decay_mat.shape[0]
    line_count, length, channels = inputs.shape
    scores = jnp.einsum("ltn,lkn->ltk", query_vecs, key_vecs, precision=PRECISE)
    within = jnp.einsum(
        "gltk,lkgp->ltgp",
        decay_mat * scores[None],
        split_heads(inputs, head_count),
        precision=PRECISE,
    )
    within = within.reshape(line_count, length, channels)
    carried = jnp.einsum("ltn,lnc->ltc", query_vecs, incoming, precision=PRECISE)
    return within + carried * line_form(jnp.exp(running), channels)


def local_grads(inputs, key_vecs, query_vecs, prepared, incoming, returning, upstream):
    running, whole_log, decay_mat = prepared
    head_count = decay_mat.shape[0]
    line_count, length, channels = inputs.shape
    from_start = line_form(jnp.exp(running), channels)
    to_end = line_form(jnp.exp(whole_log[:, :, None] - running), channels)
    scores = jnp.einsum("ltn,lkn->ltk", query_vecs, key_vecs, precision=PRECISE)
    heads_up = split_heads(upstream, head_count)
    heads_in = split_heads(inputs, head_count)
    grad_inputs = jnp.einsum(
        "gltk,ltgp->lkgp", decay_mat * scores[None], heads_up, precision=PRECISE
    ).reshape(line_count, length, channels)
    grad_inputs = (
        grad_inputs + jnp.einsum("lnc,lkn->lkc", returning, key_vecs, precision=PRECISE) * to_end
    )
    mixed = jnp.einsum("ltgp,lkgp->gltk", heads_up, heads_in, precision=PRECISE) * decay_mat
    grad_keys = jnp.einsum("gltk,ltn->lkn", mixed, query_vecs, precision=PRECISE)
    grad_keys = grad_keys + jnp.einsum(
        "lkc,lnc->lkn", inputs * to_end, returning, precision=PRECISE
    )
    grad_queries = jnp.einsum("gltk,lkn->ltn", mixed, key_vecs, precision=PRECISE)
    grad_queries = grad_queries + jnp.einsum(
        "ltc,lnc->ltn", upstream * from_start, incoming, precision=PRECISE
    )
    return (grad_inputs, grad_keys, grad_queries)


def shards(
    patches, mask_token, masked, tissue, in_weight, out_weight, row_decay, col_decay, cotangent
):
    grid_rows, grid_cols, feat_width = patches.shape
    tok_count = grid_rows * grid_cols
    chosen = (masked == 1)[:, :, None]
    present = tissue.astype(jnp.bfloat16)[:, :, None]
    model_in = jnp.where(chosen, mask_token[None, None, :], patches) * present
    flat_in = model_in.reshape(tok_count, feat_width)
    inner_width = E
    half_width = inner_width // 2
    state_size = N
    number_of_heads = HEADS // 2
    offset = 2 * inner_width
    full_in, full_out = (
        lax.all_gather(in_weight, "grow", axis=1, tiled=True),
        lax.all_gather(out_weight, "grow", axis=1, tiled=True),
    )
    projected = lax.dot_general(
        flat_in, full_in, (((1,), (1,)), ((), ())), preferred_element_type=jnp.float32
    )
    proj_bf = projected.astype(jnp.bfloat16)
    pre_values = proj_bf[:, :inner_width].astype(jnp.float32)
    gate_pre = proj_bf[:, inner_width:offset].astype(jnp.float32)
    key_rows = (
        proj_bf[:, offset : offset + state_size]
        .astype(jnp.float32)
        .reshape(grid_rows, grid_cols, state_size)
    )
    query_rows = (
        proj_bf[:, offset + state_size : offset + 2 * state_size]
        .astype(jnp.float32)
        .reshape(grid_rows, grid_cols, state_size)
    )
    key_cols = (
        proj_bf[:, offset + 2 * state_size : offset + 3 * state_size]
        .astype(jnp.float32)
        .reshape(grid_rows, grid_cols, state_size)
        .transpose(1, 0, 2)
    )
    query_cols = (
        proj_bf[:, offset + 3 * state_size : offset + 4 * state_size]
        .astype(jnp.float32)
        .reshape(grid_rows, grid_cols, state_size)
        .transpose(1, 0, 2)
    )
    values = jax.nn.silu(pre_values)
    row_inputs = values[:, :half_width].reshape(grid_rows, grid_cols, half_width)
    col_inputs = values[:, half_width:].reshape(grid_rows, grid_cols, half_width).transpose(1, 0, 2)
    row_prep = prepare(row_decay)
    col_prep = prepare(col_decay.transpose(0, 2, 1))
    row_zero = (
        jnp.zeros((grid_rows, number_of_heads), jnp.float32),
        jnp.zeros((grid_rows, state_size, half_width), jnp.float32),
    )
    col_zero = (
        jnp.zeros((grid_cols, number_of_heads), jnp.float32),
        jnp.zeros((grid_cols, state_size, half_width), jnp.float32),
    )
    row_entry = prefix(local_summary(row_inputs, key_rows, row_prep), "gcol", chain_link, row_zero)[
        1
    ]
    grow_size = lax.axis_size("grow")
    my_block = lax.axis_index("grow")
    parts_in, parts_key, parts_log = (
        lax.all_gather(
            proj_bf[:, half_width:inner_width].reshape(grid_rows, grid_cols, half_width),
            "grow",
            axis=0,
            tiled=True,
        ),
        lax.all_gather(
            proj_bf[:, offset + 2 * state_size : offset + 3 * state_size].reshape(
                grid_rows, grid_cols, state_size
            ),
            "grow",
            axis=0,
            tiled=True,
        ),
        lax.all_gather(
            col_decay.transpose(1, 0, 2).astype(jnp.bfloat16), "grow", axis=0, tiled=True
        ).astype(jnp.float32),
    )
    col_entry = col_zero[1]
    for block_idx in range(grow_size):
        lower_row = block_idx * grid_rows
        piece_in = jax.nn.silu(
            parts_in[lower_row : lower_row + grid_rows].astype(jnp.float32)
        ).transpose(1, 0, 2)
        piece_keys = (
            parts_key[lower_row : lower_row + grid_rows].astype(jnp.float32).transpose(1, 0, 2)
        )
        piece_log = parts_log[lower_row : lower_row + grid_rows].transpose(1, 2, 0)
        whole_log, piece_state = local_summary(piece_in, piece_keys, prepare(piece_log))
        moved = carry_on(whole_log, col_entry) + piece_state
        col_entry = jnp.where(block_idx < my_block, moved, col_entry)
    row_out = local_outputs(row_inputs, key_rows, query_rows, row_prep, row_entry)
    col_out = local_outputs(col_inputs, key_cols, query_cols, col_prep, col_entry).transpose(
        1, 0, 2
    )
    mixed = jnp.concatenate(
        [row_out.reshape(tok_count, half_width), col_out.reshape(tok_count, half_width)], axis=1
    )
    gate_act = jax.nn.silu(gate_pre)
    head_size = inner_width // HEADS
    gated = (mixed * gate_act).reshape(tok_count, HEADS, head_size)
    inv_rms = lax.rsqrt(jnp.mean(gated * gated, axis=2, keepdims=True) + EPSILON)
    normed = gated * inv_rms
    normed_bf = normed.reshape(tok_count, inner_width).astype(jnp.bfloat16)
    grad_out = (cotangent * masked.astype(jnp.bfloat16)[:, :, None]).reshape(tok_count, feat_width)
    total_patches = tok_count * lax.axis_size("gcol") * lax.axis_size("grow")
    weight_sum = lax.psum_scatter(
        lax.dot_general(
            grad_out, normed_bf, (((0,), (0,)), ((), ())), preferred_element_type=jnp.float32
        ),
        ("gcol", "grow"),
        scatter_dimension=0,
        tiled=True,
    )
    out_weight_grad = weight_sum * (1.0 / math.sqrt(total_patches))
    grad_normed_bf = jnp.dot(grad_out, full_out, preferred_element_type=jnp.float32).astype(
        jnp.bfloat16
    )
    grad_normed = lax.optimization_barrier(grad_normed_bf).astype(jnp.float32)
    grad_normed = grad_normed.reshape(tok_count, HEADS, head_size)
    grad_gated = inv_rms * (
        grad_normed - normed * jnp.mean(grad_normed * normed, axis=2, keepdims=True)
    )
    grad_gated = grad_gated.reshape(tok_count, inner_width)
    grad_mixed = grad_gated * gate_act
    grad_gate = grad_gated * mixed * silu_grad(gate_pre)
    row_up = grad_mixed[:, :half_width].reshape(grid_rows, grid_cols, half_width)
    col_up = grad_mixed[:, half_width:].reshape(grid_rows, grid_cols, half_width).transpose(1, 0, 2)
    row_exit = carried_in(local_return(query_rows, row_prep, row_up), "gcol", chain_link, row_zero)[
        1
    ]
    parts_up, parts_query = (
        lax.all_gather(
            shortened(grad_mixed[:, half_width:].reshape(grid_rows, grid_cols, half_width)),
            "grow",
            axis=0,
            tiled=True,
        ),
        lax.all_gather(
            proj_bf[:, offset + 3 * state_size : offset + 4 * state_size].reshape(
                grid_rows, grid_cols, state_size
            ),
            "grow",
            axis=0,
            tiled=True,
        ),
    )
    col_exit = col_zero[1]
    for block_idx in reversed(range(grow_size)):
        lower_row = block_idx * grid_rows
        piece_up = parts_up[lower_row : lower_row + grid_rows].transpose(1, 0, 2)
        piece_queries = (
            parts_query[lower_row : lower_row + grid_rows].astype(jnp.float32).transpose(1, 0, 2)
        )
        piece_log = parts_log[lower_row : lower_row + grid_rows].transpose(1, 2, 0)
        whole_log, piece_back = local_return(piece_queries, prepare(piece_log), piece_up)
        moved = carry_on(whole_log, col_exit) + piece_back
        col_exit = jnp.where(block_idx > my_block, moved, col_exit)
    grad_row_in, grad_row_key, grad_row_query = local_grads(
        row_inputs, key_rows, query_rows, row_prep, row_entry, row_exit, row_up
    )
    grad_col_in, grad_col_key, grad_col_query = local_grads(
        col_inputs, key_cols, query_cols, col_prep, col_entry, col_exit, col_up
    )
    grad_values = jnp.concatenate(
        [
            grad_row_in.reshape(tok_count, half_width),
            grad_col_in.transpose(1, 0, 2).reshape(tok_count, half_width),
        ],
        axis=1,
    )
    grad_proj = jnp.concatenate(
        [
            grad_values * silu_grad(pre_values),
            grad_gate,
            grad_row_key.reshape(tok_count, state_size),
            grad_row_query.reshape(tok_count, state_size),
            grad_col_key.transpose(1, 0, 2).reshape(tok_count, state_size),
            grad_col_query.transpose(1, 0, 2).reshape(tok_count, state_size),
        ],
        axis=1,
    ).astype(jnp.bfloat16)
    keep_mask = present * (1 - masked).astype(jnp.bfloat16)[:, :, None]
    grad_model_in = jnp.dot(grad_proj, full_in, preferred_element_type=jnp.float32).reshape(
        grid_rows, grid_cols, feat_width
    )
    patch_grad = (grad_model_in * keep_mask).astype(jnp.bfloat16)
    return (patch_grad, out_weight_grad)


MESH = pl.DeviceIdType.MESH
NT = (((1,), (1,)), ((), ()))
NN = (((1,), (0,)), ((), ()))
TN = (((0,), (0,)), ((), ()))


def mm(a, b, dims):
    return lax.dot_general(a, b, dims, preferred_element_type=jnp.float32)


def layer_kernel(
    chips, rows, scale,
    patch_hbm, token_hbm, cot_hbm, hidden_hbm, present_hbm, rdec_hbm, cdec_hbm, w_hbm, wout_hbm,
    pg_out, sum_out,
    sems, pg_ref, out_ref, pair_ref, token_ref, flag_ref, dec_ref,
    ms, mb, rd, cd, db, wa, wb, wr, wout, gb, gsr, ga, gx, gsx, gcx, nx, la, lx, ln, lnx, u_s, z_s, su_s, sz_s, gn_s, bc_s,
    normed_s, y_s, inv_s, mat_s, dec_s, turned_s, run_a, run_b, gp, prs, pcs, prow, pcol,
    wca, wcb, wq, zsa, zsb, zq, zca, zcb, zcq, zr, zrq,
):
    k, c = lax.axis_index("gcol"), lax.axis_index("grow")
    depth = chips // 2
    zi, xi = k // 2, lax.rem(k, 2)
    cols = ms.shape[2]
    toks = chips * cols
    feat, half, part = token_ref.shape[0], wout.shape[1], wa.shape[1]
    heads, width = dec_ref.shape[1], wa.shape[0]
    total = 2 * chips
    slab = feat // chips
    scope = jax.named_scope
    ids = itertools.count()

    def new_sem():
        return sems.at[next(ids)]

    def landed(ref, sem):
        pltpu.make_async_copy(ref, ref, sem).wait()

    me = 2 * k + c
    barrier = pltpu.get_barrier_semaphore()
    for d in range(1, total):
        to = lax.rem(me + d, total)
        pl.semaphore_signal(
            barrier, inc=1, device_id={"gcol": to // 2, "grow": lax.rem(to, 2)}, device_id_type=MESH
        )

    side = zi // 2
    mate = zi + 1 - 2 * lax.rem(zi, 2)
    near_far, end_far = 2 - side, 3 - 3 * side
    order = (end_far, near_far, mate, zi)
    outer = zi == 3 * side
    inner = jnp.logical_not(outer)
    beside = 2 * zi + 1 - xi

    def block(q):
        return pl.ds(pl.multiple_of(q * slab, slab), slab)

    pieces = ((0, 0, half), (2 * half, half, half), (4 * half, 2 * half, 2 * N))

    def packed(ref, core):
        return [
            (ref.at[pl.ds(pl.multiple_of(base + core * size, 128), size)], pl.ds(at, size))
            for base, at, size in pieces
        ]

    in_sem = [new_sem() for _ in range(4)]
    loads = [
        pltpu.make_async_copy(src, dst, s)
        for src, dst, s in (
            (hidden_hbm, flag_ref.at[0], in_sem[0]), (present_hbm, flag_ref.at[1], in_sem[0]),
            (token_hbm, token_ref, in_sem[1]),
            (rdec_hbm, dec_ref.at[0], in_sem[2]), (cdec_hbm, dec_ref.at[1], in_sem[2]),
            (patch_hbm, pair_ref.at[0], in_sem[3]), (cot_hbm, pair_ref.at[1], in_sem[3]),
        )
    ]
    for copy in loads:
        copy.start()
    load_w = [pltpu.make_async_copy(src, wa.at[at], in_sem[0]) for src, at in packed(w_hbm, c)]
    load_o = pltpu.make_async_copy(wout_hbm, wout, in_sem[1])
    load_r = [pltpu.make_async_copy(src, wr.at[at], in_sem[2]) for src, at in packed(w_hbm, 1 - c)]
    patch_ref, cot_ref = pair_ref.at[0], pair_ref.at[1]

    def remote(src, dst, s, r, chip, core):
        return pltpu.make_async_remote_copy(
            src_ref=src, dst_ref=dst, send_sem=s, recv_sem=r,
            device_id={"gcol": chip, "grow": core}, device_id_type=MESH,
        )

    def across_lanes(column):
        one = jnp.broadcast_to(column, (column.shape[0], 128)).astype(jnp.bfloat16)
        return jnp.concatenate([one] * (part // 128), axis=1)

    with scope("prep"):
        for ref, sem in zip((flag_ref, token_ref, dec_ref, pair_ref), in_sem):
            landed(ref, sem)
        for copy in load_w:
            copy.start()
        load_o.start()
        for copy in load_r:
            copy.start()
        square = (cols, cols)
        eye = lax.broadcasted_iota(jnp.int32, square, 0) == lax.broadcasted_iota(jnp.int32, square, 1)
        eye = eye.astype(jnp.float32)
        hidden_f, present_f = flag_ref[0].astype(jnp.float32), flag_ref[1].astype(jnp.float32)
        hidden_t, present_t = mm(eye, hidden_f, NT), mm(eye, present_f, NT)
        visible_t = present_t * (1.0 - hidden_t)
        for i in range(rows):
            hidden, visible = across_lanes(hidden_t[:, i : i + 1]), across_lanes(visible_t[:, i : i + 1])
            for f in range(2):
                at = slice(f * part, (f + 1) * part)
                ms[f, i] = patch_ref[i, :, at] * visible + cot_ref[i, :, at] * hidden
            for q in range(depth):
                at = slice(q * slab, (q + 1) * slab)
                gsx[i, :, at] = cot_ref[i, :, block(2 * q + 1 - xi)] * hidden[:, :slab]
                turn = (2 * q + 1 - i % 2) * slab
                gsr[i, :, at] = cot_ref[i, :, turn : turn + slab] * hidden[:, :slab]
            blank = jnp.zeros((rd.shape[1] - heads - 2, cols), jnp.float32)
            flags = jnp.concatenate([hidden_f[i : i + 1], present_f[i : i + 1], blank], axis=0)
            for n, dst in enumerate((rd, cd)):
                dst[i, :heads] = dec_ref[n, :, i, :]
                dst[i, heads:] = flags

    m_send, d_send, g_send, gc_send, w_send, n_send, p_send, c_send = [new_sem() for _ in range(8)]
    m_recv, (d_recv, g_recv, gc_recv, w_recv, n_recv, nc_recv, nr_recv, p_recv, c_recv) = (
        [sems.at[next(ids)] for _ in range(2)], [new_sem() for _ in range(9)]
    )

    g_col = remote(gsx, gcx.at[pl.ds(rows * c, rows)], gc_send, gc_recv, beside, 1)

    def g_row(i):
        return remote(gsr.at[i], gx.at[k], g_send, g_recv, rows * c + (i ^ 1), 0)

    def m_row(f, i):
        return remote(ms.at[f, i], mb.at[f * chips + k], m_send, m_recv[f], rows * c + i, 0)

    def m_col(f):
        return remote(ms.at[f], mb.at[pl.ds(f * chips, rows)], m_send, m_recv[f], k, 1)

    def d_row(i):
        return remote(rd.at[i], db.at[k], d_send, d_recv, rows * c + i, 0)

    d_col = remote(cd, db.at[pl.ds(0, rows)], d_send, d_recv, k, 1)

    def not_me(i):
        return jnp.logical_or(c == 1, k != i)

    def each_row(copy_of, owner=lambda i: i):
        for i in range(rows):

            @pl.when(not_me(owner(i)))
            def _():
                copy_of(i).start()

    def each_g_row():
        each_row(g_row, lambda i: i ^ 1)

    def drained(ref, sem, count, own, extra):
        @pl.when(c == 1)
        def _():
            landed(ref.at[pl.ds(0, count)], sem)

        for mine, less in ((k < rows, own), (k >= rows, 0)):

            @pl.when(jnp.logical_and(c == 0, mine))
            def _():
                landed(ref.at[pl.ds(0, count - less + extra)], sem)

    w_out = remote(wr, wb, w_send, w_recv, k, 1 - c)
    with scope("own_rows"):
        @pl.when(c == 1)
        def _():
            pltpu.make_async_copy(cd, db.at[pl.ds(rows, rows)], d_recv).start()
            for f in range(2):
                pltpu.make_async_copy(ms.at[f], mb.at[pl.ds(f * chips + rows, rows)], m_recv[f]).start()

        for i in range(rows):

            @pl.when(jnp.logical_and(c == 0, k == i))
            def _():
                pltpu.make_async_copy(rd.at[i], db.at[i], d_recv).start()
                pltpu.make_async_copy(gsr.at[i ^ 1], gx.at[i], g_recv).start()
                for f in range(2):
                    pltpu.make_async_copy(ms.at[f, i], mb.at[f * chips + i], m_recv[f]).start()

    with scope("barrier_wait"):
        pl.semaphore_wait(barrier, total - 1)
    with scope("launch"):
        each_row(d_row)

        @pl.when(c == 0)
        def _():
            d_col.start()
            m_col(1).start()
            m_col(0).start()

        for f in range(2):
            each_row(functools.partial(m_row, f))
        landed(wr, in_sem[2])
        w_out.start()
        g_col.start()

    t_at = lax.broadcasted_iota(jnp.int32, (toks, toks), 0)
    k_at = lax.broadcasted_iota(jnp.int32, (toks, toks), 1)
    gap_at = t_at - k_at
    mask = jnp.logical_and(gap_at >= 0, (gap_at & (cols - 1)) * c == 0)
    low = lax.broadcasted_iota(jnp.int32, (toks, 128), 1) < N
    same = (128, 128)
    head_of = [lax.broadcasted_iota(jnp.int32, same, d) // N for d in range(2)]
    averages = jnp.where(head_of[0] == head_of[1], 1.0 / N, 0.0).astype(jnp.bfloat16)

    with scope("arrive_decay"):
        landed(db, d_recv)
    with scope("decay"):
        ones = mask.astype(jnp.float32)
        dec = jnp.concatenate([db[i] for i in range(chips)], axis=1)
        run_s = lax.dot_general(ones, dec, NT, precision=PRECISE, preferred_element_type=jnp.float32)
        run_l = lax.dot_general(dec, ones, NT, precision=PRECISE, preferred_element_type=jnp.float32)
        run_a[...], run_b[...] = run_s, run_l
        for h in range(heads):
            gap = run_s[:, h : h + 1] - run_l[h : h + 1, :]
            dec_s[h] = jnp.where(mask, jnp.exp(jnp.minimum(gap, 0.0)), 0.0)
        unit = (t_at == k_at).astype(jnp.float32)
        flags_t = mm(unit, dec[heads:], NT)
        tok_hidden, tok_filled = across_lanes(flags_t[:, 0:1]), across_lanes(flags_t[:, 0:1] * flags_t[:, 1:2])
        tok_shown = across_lanes(1.0 - flags_t[:, 0:1])

    with scope("load_w"):
        landed(wa, in_sem[0])
        landed(wout, in_sem[1])

    def turn_decay():
        late = k_at - t_at
        reach = jnp.logical_and(late >= 0, (late & (cols - 1)) * c == 0)
        for h in range(heads):
            gap = run_b[h : h + 1, :] - run_a[:, h : h + 1]
            turned_s[h] = jnp.where(reach, jnp.exp(jnp.minimum(gap, 0.0)), 0.0)

    def halves(ref):
        return jnp.concatenate([ref[0], ref[1]], axis=1)

    def unpack(f):
        at = pl.ds(pl.multiple_of(f * part, part), part)
        either = mb[pl.ds(f * chips, chips)].reshape(toks, part)
        gb[:, at] = either * tok_hidden
        return either * tok_shown + token_ref[at].reshape(1, part) * tok_filled

    def split(f):
        for i in range(depth // 2):
            q = f * (depth // 2) + i
            at_i = slice(i * slab, (i + 1) * slab)
            ga[f, :, at_i] = gb[:, block(2 * q + xi)]

    def half_gn(f):
        at = pl.ds(pl.multiple_of(f * part, part), part)
        return mm(gb[:, at], wout[at, :], NN)

    def arrive_m(core):
        for f in range(2):

            @pl.when(core == f)
            def _():
                landed(mb.at[pl.ds(f * chips, chips)], m_recv[f])

    lend_sems = [(new_sem(), new_sem()) for _ in range(3)]

    def lend(i, src, dst):
        return remote(src, dst, *lend_sems[i], k, 1)

    pair = [pl.ds(i * 256, 256) for i in range(4)]
    lend_a = lend(0, ga, la)
    lend_x = lend(1, gx, lx)
    lend_n = lend(2, normed_s.at[:, pair[1]], ln)
    n_first = remote(normed_s.at[:, pair[0]], nx.at[:, pair[0]], n_send, n_recv, beside, c)
    n_col = remote(normed_s.at[:, pair[1]], nx.at[:, pair[1]], n_send, nc_recv, beside, 1)
    n_row = remote(normed_s.at[:, pair[1]], lnx, n_send, nr_recv, beside, 1)
    with scope("arrive_first"):
        arrive_m(c)
    with scope("proj_first"):
        own = unpack(c)
        firsts = [mm(own, wa[at : at + size], NT) for _, at, size in pieces]
        split(c)
        gn_first = half_gn(c)

        @pl.when(c == 0)
        def _():
            each_g_row()
            turn_decay()

    with scope("arrive_second"):
        arrive_m(1 - c)
    with scope("weights_wait"):
        landed(wb, w_recv)
    with scope("proj_second"):
        oth = unpack(1 - c)
        for dst, (_, at, size), first in zip((u_s, z_s, bc_s), pieces, firsts):
            dst[...] = (first + mm(oth, wb[at : at + size], NT)).astype(jnp.bfloat16)
        split(1 - c)


    def per_head(x):
        high = x.astype(jnp.bfloat16)
        rest = (x - high.astype(jnp.float32)).astype(jnp.bfloat16)
        return mm(high, averages, NN) + mm(rest, averages, NN)

    def if_core(core, copies):
        @pl.when(c == core)
        def _():
            for copy in copies:
                copy.start()

    if_core(0, [lend_a])

    with scope("forward"):
        b_bf, c_bf = bc_s[:, :N], bc_s[:, N:]
        scores = mm(c_bf, b_bf, NT)
        rest_at = pl.ds(pl.multiple_of((1 - c) * part, part), part)
        for p in range(half // 128):
            cols_p = slice(p * 128, (p + 1) * 128)
            if p >= 2:
                two = slice((p - 2) * 256, (p - 1) * 256)
                gn = gn_first[:, two] + mm(gb[:, rest_at], wout[rest_at, two], NN)
                gn_s[:, two] = gn.astype(jnp.bfloat16)
            u = u_s[:, cols_p].astype(jnp.float32)
            sig_u = 0.5 + 0.5 * jnp.tanh(0.5 * u)
            su_s[:, cols_p] = sig_u
            val_bf = (u * sig_u).astype(jnp.bfloat16)
            for h in (2 * p, 2 * p + 1):
                mat_s[h] = (dec_s[h] * scores).astype(jnp.bfloat16)
            y = jnp.where(low, mm(mat_s[2 * p], val_bf, NN), mm(mat_s[2 * p + 1], val_bf, NN))
            y_s[:, cols_p] = y
            z = z_s[:, cols_p].astype(jnp.float32)
            sig_z = 0.5 + 0.5 * jnp.tanh(0.5 * z)
            sz_s[:, cols_p] = sig_z
            gated = y * (z * sig_z)
            inv = lax.rsqrt(per_head(gated * gated) + EPSILON)
            inv_s[:, cols_p] = inv
            normed_s[:, cols_p] = (gated * inv).astype(jnp.bfloat16)
            if p == 1:
                n_first.start()
            if p == 3:
                if_core(1, [n_col])

                @pl.when(c == 1)
                def _():
                    each_g_row()

                if_core(0, [n_row, lend_n])

    with scope("turn_decay"):
        @pl.when(c == 1)
        def _():
            turn_decay()

    with scope("backward"):
        turned_scores = mm(b_bf, c_bf, NT)
        d_scores = jnp.zeros((toks, toks), jnp.float32)
        for p in range(half // 128):
            cols_p = slice(p * 128, (p + 1) * 128)
            z, sig_z, y, inv = z_s[:, cols_p].astype(jnp.float32), sz_s[:, cols_p], y_s[:, cols_p], inv_s[:, cols_p]
            act = z * sig_z
            normed = y * act * inv
            u, sig_u = u_s[:, cols_p].astype(jnp.float32), su_s[:, cols_p]
            val = u * sig_u
            val_bf = val.astype(jnp.bfloat16)
            gn = gn_s[:, cols_p].astype(jnp.float32)
            gg = inv * (gn - normed * per_head(gn * normed))
            dy = gg * act
            dz = gg * y * (sig_z + act * (1.0 - sig_z))
            dy_bf = dy.astype(jnp.bfloat16)
            dec_a, dec_b = turned_s[2 * p], turned_s[2 * p + 1]
            dv = jnp.where(
                low,
                mm((dec_a * turned_scores).astype(jnp.bfloat16), dy_bf, NN),
                mm((dec_b * turned_scores).astype(jnp.bfloat16), dy_bf, NN),
            )
            du = dv * (sig_u + val * (1.0 - sig_u))
            gp[:, cols_p] = du.astype(jnp.bfloat16)
            gp[:, half + p * 128 : half + (p + 1) * 128] = dz.astype(jnp.bfloat16)
            zero = jnp.zeros_like(dy)
            d_scores += dec_a * mm(val_bf, jnp.where(low, dy, zero).astype(jnp.bfloat16), NT)
            d_scores += dec_b * mm(val_bf, jnp.where(low, zero, dy).astype(jnp.bfloat16), NT)
        ds_bf = d_scores.astype(jnp.bfloat16)
        d_bc = jnp.concatenate([mm(ds_bf, c_bf, NN), mm(ds_bf, b_bf, TN)], axis=1)
        gp[:, 2 * half :] = d_bc.astype(jnp.bfloat16)

    with scope("pass_gx"):

        @pl.when(c == 0)
        def _():
            landed(gx, g_recv)

        if_core(0, [lend_x])

    home, slot = k // rows, lax.rem(k, rows)

    def row_back(f, chip):
        return remote(prs.at[f, chip], prow.at[f, slot], p_send, p_recv, chip, home)

    def col_back(n):
        return remote(pcs.at[pl.ds(n * chips, rows)], pcol.at[n], c_send, c_recv, k, 0)

    others = [
        2 * z + x
        for z in (end_far, near_far, mate)
        for x in (1 - xi, xi)
    ] + [2 * zi + 1 - xi]

    def project_back(g_ref, w_ref):
        return mm(g_ref[...], w_ref[...], NN).astype(jnp.bfloat16).reshape(chips, cols, part)

    def return_rows(f):
        for chip in others:
            row_back(f, chip).start()

        @pl.when(home == 1)
        def _():
            row_back(f, k).start()

        @pl.when(home == 0)
        def _():
            pltpu.make_async_copy(prs.at[f, k], prow.at[f, slot], p_recv).start()

    class Sums:
        def __init__(self, w, z, zin, zout, slot):
            self.w, self.z, self.zin, self.zout, self.slot = w, z, zin, zout, slot
            self.send, self.out_recv, *self.in_recv = [new_sem() for _ in range(4)]

        def to_target(self, j, kind, chip, core):
            return remote(
                self.z.at[2 * j + core], self.zout.at[3 * self.slot + kind], self.send, self.out_recv, chip, core
            )

        def part(self, j):
            return self.w[block(order[j]), :]

        def ready(self, j, value):
            self.z[2 * j : 2 * j + 2] = value.astype(jnp.bfloat16).reshape(2, slab // 2, value.shape[1])

        def begin(self):
            @pl.when(outer)
            def _():
                for j in range(2):
                    self.ready(j, self.part(j))
                    two = pl.ds(2 * j, 2)
                    remote(
                        self.z.at[two], self.zin.at[two], self.send, self.in_recv[j], 2 * mate + xi, c
                    ).start()

            self.ready(2, self.part(2))
            for core in range(2):
                self.to_target(2, 0, 2 * mate + xi, core).start()
            self.ready(3, self.part(3))
            pltpu.make_async_copy(
                self.z.at[6 + c], self.zout.at[3 * self.slot + 2], self.out_recv
            ).start()
            self.to_target(3, 2, k, 1 - c).start()

        def combine(self):
            @pl.when(inner)
            def _():
                for j in range(2):
                    landed(self.zin.at[pl.ds(2 * j, 2)], self.in_recv[j])
                    passed = self.zin[2 * j : 2 * j + 2].astype(jnp.float32).reshape(slab, self.w.shape[1])
                    self.ready(j, self.part(j) + passed)
                    for core in range(2):
                        self.to_target(j, 1, 2 * order[j] + xi, core).start()

        def drain(self):
            landed(self.z.at[pl.ds(0, 7)], self.send)

    col_first = Sums(wca, zsa, zca, zr, 0)
    col_second = Sums(wcb, zsb, zcb, zr, 1)
    row_sums = Sums(wq, zq, zcq, zrq, c)

    @pl.when(c == 0)
    def _():
        with scope("back_project_0"):
            for f, w_ref in enumerate((wa, wb)):
                prs[f] = project_back(gp, w_ref)

                @pl.when(inner)
                def _():
                    return_rows(f)

        with scope("wait_n0"):
            landed(nx.at[:, pair[0]], n_recv)
        with scope("row_product_0"):
            wq[...] = mm(halves(ga), normed_s[:, :256], TN) + mm(gx[...].reshape(toks, part), nx[:, :256], TN)

    @pl.when(c == 1)
    def _():
        with scope("col_back_1"):
            for n, w_ref in enumerate((wa, wb)):
                pcs[n * chips : (n + 1) * chips] = project_back(gp, w_ref)
                col_back(n).start()
                pcol[n] = pcs[n * chips + rows : (n + 1) * chips]
        with scope("wait_n1"):
            landed(gcx, gc_recv)
            landed(nx.at[:, pair[0]], n_recv)

        def col_product(i):
            own = mm(halves(ga), normed_s[:, i * 256 : (i + 1) * 256], TN)
            return own + mm(gcx[...].reshape(toks, part), nx[:, i * 256 : (i + 1) * 256], TN)

        with scope("col_first"):
            wca[...] = col_product(0)
            col_first.begin()
        with scope("wait_n2"):
            landed(nx.at[:, pair[1]], nc_recv)
        with scope("col_second"):
            wcb[...] = col_product(1)
            col_second.begin()
        with scope("lent_wait"):
            for copy in (lend_a, lend_x, lend_n, n_row):
                copy.wait_recv()
        with scope("row_product_1"):
            wq[...] = mm(halves(la), ln[...], TN) + mm(lx[...].reshape(toks, part), lnx[...], TN)

    with scope("row_begin"):
        row_sums.begin()

    with scope("return_rows"):
        @pl.when(jnp.logical_and(c == 0, outer))
        def _():
            for f in range(2):
                return_rows(f)


    @pl.when(c == 1)
    def _():
        with scope("col_combine"):
            col_first.combine()
            col_second.combine()

    with scope("row_combine"):
        row_sums.combine()

    with scope("parts_wait"):

        @pl.when(c == 0)
        def _():
            landed(pcol, c_recv)

        landed(prow, p_recv)

    with scope("patch_grad"):
        for f in range(2):
            by_row, by_col = prow.at[f], pcol.at[1 - f]
            for i in range(rows):
                keep = visible_t[:, i : i + 1]
                both = by_row[i].astype(jnp.float32) + by_col[i].astype(jnp.float32)
                pg_ref[i, :, f * part : (f + 1) * part] = (both * keep).astype(pg_ref.dtype)

    results = [
        pltpu.make_async_copy(pg_ref, pg_out, in_sem[0]),
        pltpu.make_async_copy(out_ref, sum_out, in_sem[1]),
    ]
    results[0].start()

    with scope("sums_wait"):
        landed(zr.at[pl.ds(0, 3)], col_first.out_recv)
        landed(zr.at[pl.ds(3, 3)], col_second.out_recv)
        landed(zrq, row_sums.out_recv)

    with scope("weight_sum"):
        for ref, at, size in ((zrq.at[0:3], 0, 256), (zrq.at[3:6], 256, 256), (zr.at[0:3], half, 256), (zr.at[3:6], half + 256, 256)):
            acc = ref[0].astype(jnp.float32) + ref[1].astype(jnp.float32)
            acc += ref[2].astype(jnp.float32)
            out_ref[:, at : at + size] = acc * scale
    results[1].start()

    with scope("drain"):
        drained(db, d_send, rows, 1, rows)
        drained(mb, m_send, 2 * rows, 2, 2 * rows)
        drained(gx, g_send, rows, 1, 0)
        landed(gsx, gc_send)
        landed(wb, w_send)
        row_sums.drain()
        landed(normed_s, n_send)

        @pl.when(jnp.logical_and(c == 0, home == 0))
        def _():
            landed(pcs.at[pl.ds(0, 2 * chips - 2)], p_send)

        @pl.when(jnp.logical_and(c == 0, home == 1))
        def _():
            landed(pcs, p_send)

        @pl.when(c == 0)
        def _():
            for copy in (lend_a, lend_x, lend_n):
                copy.wait_send()

        @pl.when(c == 1)
        def _():
            col_first.drain()
            col_second.drain()
            landed(pcol, c_send)

        for copy in results:
            copy.wait()


def store_kernel(a_ref, b_ref, a_hbm, b_hbm, sem):
    copies = [
        pltpu.make_async_copy(a_ref, a_hbm, sem.at[0]),
        pltpu.make_async_copy(b_ref, b_hbm, sem.at[1]),
    ]
    for copy in copies:
        copy.start()
    for copy in copies:
        copy.wait()


def owned(
    patches, mask_token, masked, tissue, in_weight, out_weight, row_decay, col_decay, cotangent
):
    rows, cols, feat = patches.shape
    chips = lax.axis_size("gcol")
    toks, heads = chips * cols, row_decay.shape[0]
    half, part = out_weight.shape[1], in_weight.shape[1]
    width = 2 * half + 2 * N
    slab = feat // chips
    bf, fl = jnp.bfloat16, jnp.float32
    vmem, dma = pltpu.VMEM, pltpu.SemaphoreType.DMA
    anywhere = pl.BlockSpec(memory_space=pltpu.HBM)
    place = pl.BlockSpec(memory_space=pl.ANY)
    scale = 1.0 / math.sqrt(2 * rows * cols * chips)
    aux = heads + 8
    results = pl.pallas_call(
        functools.partial(layer_kernel, chips, rows, scale),
        name="layer",
        out_shape=(vmem(patches.shape, bf), vmem((slab // 2, 2 * half), fl)),
        in_specs=[anywhere] * 9,
        out_specs=(place, place),
        scratch_shapes=[
            dma((41,)), vmem(patches.shape, bf), vmem((slab // 2, 2 * half), fl),
            vmem((2,) + patches.shape, bf), vmem(mask_token.shape, bf),
            vmem((2,) + masked.shape, masked.dtype), vmem((2,) + row_decay.shape, fl),
            vmem((2, rows, cols, part), bf), vmem((2 * chips, cols, part), bf),
            vmem((rows, aux, cols), fl), vmem((rows, aux, cols), fl), vmem((chips, aux, cols), fl),
            vmem((width, part), bf), vmem((width, part), bf), vmem((width, part), bf), vmem(out_weight.shape, bf),
            vmem((toks, feat), bf), vmem((rows, cols, part), bf), vmem((2, toks, part // 2), bf),
            vmem((chips, cols, part), bf), vmem((rows, cols, part), bf), vmem((chips, cols, part), bf),
            vmem((toks, half), bf), vmem((2, toks, part // 2), bf),
            vmem((chips, cols, part), bf), vmem((toks, half // 2), bf), vmem((toks, half // 2), bf),
            vmem((toks, half), bf), vmem((toks, half), bf), vmem((toks, half), fl), vmem((toks, half), fl),
            vmem((toks, half), bf), vmem((toks, 2 * N), bf), vmem((toks, half), bf),
            vmem((toks, half), fl), vmem((toks, half), fl),
            vmem((heads, toks, toks), bf), vmem((heads, toks, toks), fl),
            vmem((heads, toks, toks), fl), vmem((toks, aux), fl), vmem((aux, toks), fl),
            vmem((toks, width), bf), vmem((2, chips, cols, part), bf), vmem((2 * chips, cols, part), bf),
            vmem((2, rows, cols, part), bf), vmem((2, rows, cols, part), bf),
            vmem((half, half // 2), fl), vmem((half, half // 2), fl), vmem((half, half // 2), fl),
            vmem((8, slab // 2, half // 2), bf), vmem((8, slab // 2, half // 2), bf), vmem((8, slab // 2, half // 2), bf),
            vmem((4, slab // 2, half // 2), bf), vmem((4, slab // 2, half // 2), bf), vmem((4, slab // 2, half // 2), bf),
            vmem((6, slab // 2, half // 2), bf), vmem((6, slab // 2, half // 2), bf),
        ],
        compiler_params=pltpu.CompilerParams(
            collective_id=0, has_side_effects=True, vmem_limit_bytes=60 << 20
        ),
    )(
        patches, mask_token, cotangent, masked, tissue, row_decay, col_decay,
        in_weight, out_weight,
    )
    return pl.pallas_call(
        store_kernel,
        name="store",
        out_shape=tuple(jax.ShapeDtypeStruct(r.shape, r.dtype) for r in results),
        in_specs=[place] * 2,
        out_specs=[anywhere] * 2,
        scratch_shapes=[dma((2,))],
        compiler_params=pltpu.CompilerParams(vmem_limit_bytes=1 << 20),
    )(*results)


def body(*args):
    rows = args[0].shape[0]
    cols = args[0].shape[1]
    if lax.axis_size("grow") == 2 and rows == 4 and lax.axis_size("gcol") == 2 * rows and cols & (cols - 1) == 0:
        return owned(*args)
    return shards(*args)


def solution(mesh):
    return jax.shard_map(
        body,
        mesh=mesh,
        in_specs=(
            P(("groups", "grow"), "gcol", None),
            P(),
            P(("groups", "grow"), "gcol"),
            P(("groups", "grow"), "gcol"),
            P(None, "grow"),
            P(None, "grow"),
            P(None, ("groups", "grow"), "gcol"),
            P(None, ("groups", "grow"), "gcol"),
            P(("groups", "grow"), "gcol", None),
        ),
        out_specs=(P(("groups", "grow"), "gcol", None), P(("groups", "gcol", "grow"), None)),
        check_vma=False,
    )
```

```python
import functools
import itertools
import math

import jax
import jax.numpy as jnp
from jax import lax
from jax.experimental import pallas as pl
from jax.experimental.pallas import tpu as pltpu
from jax.sharding import PartitionSpec as P

E = 1024
HEADS = 16
N = 64


EPSILON = 1e-05
PRECISE = lax.Precision.HIGHEST


def prefix(value, axis, join, neutral):
    count, mine = (lax.axis_size(axis), lax.axis_index(axis))
    pieces = jax.tree.map(lambda part: lax.all_gather(part, axis), value)
    so_far = jax.tree.map(
        lambda part, zero: jnp.full_like(part, 0) + jnp.asarray(zero, part.dtype), value, neutral
    )

    def prefix_hop(position, so_far):
        longer = join(so_far, jax.tree.map(lambda part: part[position], pieces))
        return jax.tree.map(lambda new, old: jnp.where(position < mine, new, old), longer, so_far)

    return lax.fori_loop(0, count - 1, prefix_hop, so_far)


def carried_in(shard, axis, combine, identity):
    length, position = (lax.axis_size(axis), lax.axis_index(axis))
    everything = jax.tree.map(
        lambda part, kind: lax.all_gather(part.astype(kind), axis),
        shard,
        jax.tree.map(lambda a: jnp.bfloat16 if a.dtype == jnp.float32 else a.dtype, shard),
    )
    start = jax.tree.map(
        lambda part, zero: jnp.broadcast_to(jnp.asarray(zero, part.dtype), part.shape),
        shard,
        identity,
    )

    def carried_hop(k, before):
        at = length - 1 - k
        reached = at > position
        new = combine(
            before, jax.tree.map(lambda part, own: part[at].astype(own.dtype), everything, shard)
        )
        return jax.tree.map(lambda a, b: jnp.where(reached, a, b), new, before)

    return lax.fori_loop(0, length, carried_hop, start)


def shortened(shard):

    def short(part):
        return part.astype(jnp.bfloat16) if part.dtype == jnp.float32 else part

    return jax.tree.map(short, shard)


def silu_grad(pre_act):
    sigmoid_v = jax.nn.sigmoid(pre_act)
    return sigmoid_v * (1.0 + pre_act * (1.0 - sigmoid_v))


def per_channel(head_part, channels):
    return jnp.repeat(head_part, channels // head_part.shape[-1], axis=-1)


def line_form(head_lines, channels):
    return per_channel(head_lines.transpose(1, 2, 0), channels)


def carry_on(log_lines, state):
    return per_channel(jnp.exp(log_lines), state.shape[2])[:, None, :] * state


def prepare(log_decay):
    length = log_decay.shape[2]
    causal = jnp.arange(length)[:, None] >= jnp.arange(length)[None, :]
    running = jnp.einsum(
        "glk,tk->glt", log_decay, causal.astype(log_decay.dtype), precision=PRECISE
    )
    whole_log = running[:, :, -1]
    log_gaps = running[:, :, :, None] - running[:, :, None, :]
    decay_mat = jnp.where(causal, jnp.exp(jnp.where(causal, log_gaps, 0.0)), 0.0)
    return (running, whole_log, decay_mat)


def chain_link(earlier, later):
    return (earlier[0] + later[0], carry_on(later[0], earlier[1]) + later[1])


def split_heads(lines, head_count):
    line_count, length, channels = lines.shape
    return lines.reshape(line_count, length, head_count, channels // head_count)


def local_summary(inputs, key_vecs, prepared):
    running, whole_log, decay_mat = prepared
    to_end = line_form(jnp.exp(whole_log[:, :, None] - running), inputs.shape[2])
    fresh = jnp.einsum("ltc,ltn->lnc", inputs * to_end, key_vecs, precision=PRECISE)
    return (whole_log.T, fresh)


def local_return(query_vecs, prepared, upstream):
    running, whole_log, decay_mat = prepared
    from_start = line_form(jnp.exp(running), upstream.shape[2])
    backward = jnp.einsum("ltc,ltn->lnc", upstream * from_start, query_vecs, precision=PRECISE)
    return (whole_log.T, backward)


def local_outputs(inputs, key_vecs, query_vecs, prepared, incoming):
    running, whole_log, decay_mat = prepared
    head_count = decay_mat.shape[0]
    line_count, length, channels = inputs.shape
    scores = jnp.einsum("ltn,lkn->ltk", query_vecs, key_vecs, precision=PRECISE)
    within = jnp.einsum(
        "gltk,lkgp->ltgp",
        decay_mat * scores[None],
        split_heads(inputs, head_count),
        precision=PRECISE,
    )
    within = within.reshape(line_count, length, channels)
    carried = jnp.einsum("ltn,lnc->ltc", query_vecs, incoming, precision=PRECISE)
    return within + carried * line_form(jnp.exp(running), channels)


def local_grads(inputs, key_vecs, query_vecs, prepared, incoming, returning, upstream):
    running, whole_log, decay_mat = prepared
    head_count = decay_mat.shape[0]
    line_count, length, channels = inputs.shape
    from_start = line_form(jnp.exp(running), channels)
    to_end = line_form(jnp.exp(whole_log[:, :, None] - running), channels)
    scores = jnp.einsum("ltn,lkn->ltk", query_vecs, key_vecs, precision=PRECISE)
    heads_up = split_heads(upstream, head_count)
    heads_in = split_heads(inputs, head_count)
    grad_inputs = jnp.einsum(
        "gltk,ltgp->lkgp", decay_mat * scores[None], heads_up, precision=PRECISE
    ).reshape(line_count, length, channels)
    grad_inputs = (
        grad_inputs + jnp.einsum("lnc,lkn->lkc", returning, key_vecs, precision=PRECISE) * to_end
    )
    mixed = jnp.einsum("ltgp,lkgp->gltk", heads_up, heads_in, precision=PRECISE) * decay_mat
    grad_keys = jnp.einsum("gltk,ltn->lkn", mixed, query_vecs, precision=PRECISE)
    grad_keys = grad_keys + jnp.einsum(
        "lkc,lnc->lkn", inputs * to_end, returning, precision=PRECISE
    )
    grad_queries = jnp.einsum("gltk,lkn->ltn", mixed, key_vecs, precision=PRECISE)
    grad_queries = grad_queries + jnp.einsum(
        "ltc,lnc->ltn", upstream * from_start, incoming, precision=PRECISE
    )
    return (grad_inputs, grad_keys, grad_queries)


def shards(
    patches, mask_token, masked, tissue, in_weight, out_weight, row_decay, col_decay, cotangent
):
    grid_rows, grid_cols, feat_width = patches.shape
    tok_count = grid_rows * grid_cols
    chosen = (masked == 1)[:, :, None]
    present = tissue.astype(jnp.bfloat16)[:, :, None]
    model_in = jnp.where(chosen, mask_token[None, None, :], patches) * present
    flat_in = model_in.reshape(tok_count, feat_width)
    inner_width = E
    half_width = inner_width // 2
    state_size = N
    number_of_heads = HEADS // 2
    offset = 2 * inner_width
    full_in, full_out = (
        lax.all_gather(in_weight, "grow", axis=1, tiled=True),
        lax.all_gather(out_weight, "grow", axis=1, tiled=True),
    )
    projected = lax.dot_general(
        flat_in, full_in, (((1,), (1,)), ((), ())), preferred_element_type=jnp.float32
    )
    proj_bf = projected.astype(jnp.bfloat16)
    pre_values = proj_bf[:, :inner_width].astype(jnp.float32)
    gate_pre = proj_bf[:, inner_width:offset].astype(jnp.float32)
    key_rows = (
        proj_bf[:, offset : offset + state_size]
        .astype(jnp.float32)
        .reshape(grid_rows, grid_cols, state_size)
    )
    query_rows = (
        proj_bf[:, offset + state_size : offset + 2 * state_size]
        .astype(jnp.float32)
        .reshape(grid_rows, grid_cols, state_size)
    )
    key_cols = (
        proj_bf[:, offset + 2 * state_size : offset + 3 * state_size]
        .astype(jnp.float32)
        .reshape(grid_rows, grid_cols, state_size)
        .transpose(1, 0, 2)
    )
    query_cols = (
        proj_bf[:, offset + 3 * state_size : offset + 4 * state_size]
        .astype(jnp.float32)
        .reshape(grid_rows, grid_cols, state_size)
        .transpose(1, 0, 2)
    )
    values = jax.nn.silu(pre_values)
    row_inputs = values[:, :half_width].reshape(grid_rows, grid_cols, half_width)
    col_inputs = values[:, half_width:].reshape(grid_rows, grid_cols, half_width).transpose(1, 0, 2)
    row_prep = prepare(row_decay)
    col_prep = prepare(col_decay.transpose(0, 2, 1))
    row_zero = (
        jnp.zeros((grid_rows, number_of_heads), jnp.float32),
        jnp.zeros((grid_rows, state_size, half_width), jnp.float32),
    )
    col_zero = (
        jnp.zeros((grid_cols, number_of_heads), jnp.float32),
        jnp.zeros((grid_cols, state_size, half_width), jnp.float32),
    )
    row_entry = prefix(local_summary(row_inputs, key_rows, row_prep), "gcol", chain_link, row_zero)[
        1
    ]
    grow_size = lax.axis_size("grow")
    my_block = lax.axis_index("grow")
    parts_in, parts_key, parts_log = (
        lax.all_gather(
            proj_bf[:, half_width:inner_width].reshape(grid_rows, grid_cols, half_width),
            "grow",
            axis=0,
            tiled=True,
        ),
        lax.all_gather(
            proj_bf[:, offset + 2 * state_size : offset + 3 * state_size].reshape(
                grid_rows, grid_cols, state_size
            ),
            "grow",
            axis=0,
            tiled=True,
        ),
        lax.all_gather(
            col_decay.transpose(1, 0, 2).astype(jnp.bfloat16), "grow", axis=0, tiled=True
        ).astype(jnp.float32),
    )
    col_entry = col_zero[1]
    for block_idx in range(grow_size):
        lower_row = block_idx * grid_rows
        piece_in = jax.nn.silu(
            parts_in[lower_row : lower_row + grid_rows].astype(jnp.float32)
        ).transpose(1, 0, 2)
        piece_keys = (
            parts_key[lower_row : lower_row + grid_rows].astype(jnp.float32).transpose(1, 0, 2)
        )
        piece_log = parts_log[lower_row : lower_row + grid_rows].transpose(1, 2, 0)
        whole_log, piece_state = local_summary(piece_in, piece_keys, prepare(piece_log))
        moved = carry_on(whole_log, col_entry) + piece_state
        col_entry = jnp.where(block_idx < my_block, moved, col_entry)
    row_out = local_outputs(row_inputs, key_rows, query_rows, row_prep, row_entry)
    col_out = local_outputs(col_inputs, key_cols, query_cols, col_prep, col_entry).transpose(
        1, 0, 2
    )
    mixed = jnp.concatenate(
        [row_out.reshape(tok_count, half_width), col_out.reshape(tok_count, half_width)], axis=1
    )
    gate_act = jax.nn.silu(gate_pre)
    head_size = inner_width // HEADS
    gated = (mixed * gate_act).reshape(tok_count, HEADS, head_size)
    inv_rms = lax.rsqrt(jnp.mean(gated * gated, axis=2, keepdims=True) + EPSILON)
    normed = gated * inv_rms
    normed_bf = normed.reshape(tok_count, inner_width).astype(jnp.bfloat16)
    grad_out = (cotangent * masked.astype(jnp.bfloat16)[:, :, None]).reshape(tok_count, feat_width)
    total_patches = tok_count * lax.axis_size("gcol") * lax.axis_size("grow")
    weight_sum = lax.psum_scatter(
        lax.dot_general(
            grad_out, normed_bf, (((0,), (0,)), ((), ())), preferred_element_type=jnp.float32
        ),
        ("gcol", "grow"),
        scatter_dimension=0,
        tiled=True,
    )
    out_weight_grad = weight_sum * (1.0 / math.sqrt(total_patches))
    grad_normed_bf = jnp.dot(grad_out, full_out, preferred_element_type=jnp.float32).astype(
        jnp.bfloat16
    )
    grad_normed = lax.optimization_barrier(grad_normed_bf).astype(jnp.float32)
    grad_normed = grad_normed.reshape(tok_count, HEADS, head_size)
    grad_gated = inv_rms * (
        grad_normed - normed * jnp.mean(grad_normed * normed, axis=2, keepdims=True)
    )
    grad_gated = grad_gated.reshape(tok_count, inner_width)
    grad_mixed = grad_gated * gate_act
    grad_gate = grad_gated * mixed * silu_grad(gate_pre)
    row_up = grad_mixed[:, :half_width].reshape(grid_rows, grid_cols, half_width)
    col_up = grad_mixed[:, half_width:].reshape(grid_rows, grid_cols, half_width).transpose(1, 0, 2)
    row_exit = carried_in(local_return(query_rows, row_prep, row_up), "gcol", chain_link, row_zero)[
        1
    ]
    parts_up, parts_query = (
        lax.all_gather(
            shortened(grad_mixed[:, half_width:].reshape(grid_rows, grid_cols, half_width)),
            "grow",
            axis=0,
            tiled=True,
        ),
        lax.all_gather(
            proj_bf[:, offset + 3 * state_size : offset + 4 * state_size].reshape(
                grid_rows, grid_cols, state_size
            ),
            "grow",
            axis=0,
            tiled=True,
        ),
    )
    col_exit = col_zero[1]
    for block_idx in reversed(range(grow_size)):
        lower_row = block_idx * grid_rows
        piece_up = parts_up[lower_row : lower_row + grid_rows].transpose(1, 0, 2)
        piece_queries = (
            parts_query[lower_row : lower_row + grid_rows].astype(jnp.float32).transpose(1, 0, 2)
        )
        piece_log = parts_log[lower_row : lower_row + grid_rows].transpose(1, 2, 0)
        whole_log, piece_back = local_return(piece_queries, prepare(piece_log), piece_up)
        moved = carry_on(whole_log, col_exit) + piece_back
        col_exit = jnp.where(block_idx > my_block, moved, col_exit)
    grad_row_in, grad_row_key, grad_row_query = local_grads(
        row_inputs, key_rows, query_rows, row_prep, row_entry, row_exit, row_up
    )
    grad_col_in, grad_col_key, grad_col_query = local_grads(
        col_inputs, key_cols, query_cols, col_prep, col_entry, col_exit, col_up
    )
    grad_values = jnp.concatenate(
        [
            grad_row_in.reshape(tok_count, half_width),
            grad_col_in.transpose(1, 0, 2).reshape(tok_count, half_width),
        ],
        axis=1,
    )
    grad_proj = jnp.concatenate(
        [
            grad_values * silu_grad(pre_values),
            grad_gate,
            grad_row_key.reshape(tok_count, state_size),
            grad_row_query.reshape(tok_count, state_size),
            grad_col_key.transpose(1, 0, 2).reshape(tok_count, state_size),
            grad_col_query.transpose(1, 0, 2).reshape(tok_count, state_size),
        ],
        axis=1,
    ).astype(jnp.bfloat16)
    keep_mask = present * (1 - masked).astype(jnp.bfloat16)[:, :, None]
    grad_model_in = jnp.dot(grad_proj, full_in, preferred_element_type=jnp.float32).reshape(
        grid_rows, grid_cols, feat_width
    )
    patch_grad = (grad_model_in * keep_mask).astype(jnp.bfloat16)
    return (patch_grad, out_weight_grad)


MESH = pl.DeviceIdType.MESH
NT = (((1,), (1,)), ((), ()))
NN = (((1,), (0,)), ((), ()))
TN = (((0,), (0,)), ((), ()))


def mm(a, b, dims):
    return lax.dot_general(a, b, dims, preferred_element_type=jnp.float32)


def layer_kernel(
    chips, rows, scale,
    patch_hbm, token_hbm, cot_hbm, hidden_hbm, present_hbm, rdec_hbm, cdec_hbm, w_hbm, wout_hbm,
    pg_out, sum_out,
    sems, pg_ref, out_ref, pair_ref, token_ref, flag_ref, dec_ref,
    ms, mb, rd, cd, db, wa, wb, wr, wout, gb, gsr, ga, gx, gsx, gcx, nx, la, lx, ln, lnx, u_s, z_s, su_s, sz_s, gn_s, bc_s,
    normed_s, y_s, inv_s, mat_s, dec_s, turned_s, run_a, run_b, gp, prs, pcs, prow, pcol,
    wca, wcb, wq, zsa, zsb, zq, zca, zcb, zcq, zr, zrq,
):
    k, c = lax.axis_index("gcol"), lax.axis_index("grow")
    depth = chips // 2
    zi, xi = k // 2, lax.rem(k, 2)
    cols = ms.shape[2]
    toks = chips * cols
    feat, half, part = token_ref.shape[0], wout.shape[1], wa.shape[1]
    heads, width = dec_ref.shape[1], wa.shape[0]
    total = 2 * chips
    slab = feat // chips
    scope = jax.named_scope
    ids = itertools.count()

    def new_sem():
        return sems.at[next(ids)]

    def landed(ref, sem):
        pltpu.make_async_copy(ref, ref, sem).wait()

    me = 2 * k + c
    barrier = pltpu.get_barrier_semaphore()
    for d in range(1, total):
        to = lax.rem(me + d, total)
        pl.semaphore_signal(
            barrier, inc=1, device_id={"gcol": to // 2, "grow": lax.rem(to, 2)}, device_id_type=MESH
        )

    side = zi // 2
    mate = zi + 1 - 2 * lax.rem(zi, 2)
    near_far, end_far = 2 - side, 3 - 3 * side
    order = (end_far, near_far, mate, zi)
    outer = zi == 3 * side
    inner = jnp.logical_not(outer)
    beside = 2 * zi + 1 - xi

    def block(q):
        return pl.ds(pl.multiple_of(q * slab, slab), slab)

    pieces = ((0, 0, half), (2 * half, half, half), (4 * half, 2 * half, 2 * N))

    def packed(ref, core):
        return [
            (ref.at[pl.ds(pl.multiple_of(base + core * size, 128), size)], pl.ds(at, size))
            for base, at, size in pieces
        ]

    in_sem = [new_sem() for _ in range(4)]
    loads = [
        pltpu.make_async_copy(src, dst, s)
        for src, dst, s in (
            (hidden_hbm, flag_ref.at[0], in_sem[0]), (present_hbm, flag_ref.at[1], in_sem[0]),
            (token_hbm, token_ref, in_sem[1]),
            (rdec_hbm, dec_ref.at[0], in_sem[2]), (cdec_hbm, dec_ref.at[1], in_sem[2]),
            (patch_hbm, pair_ref.at[0], in_sem[3]), (cot_hbm, pair_ref.at[1], in_sem[3]),
        )
    ]
    for copy in loads:
        copy.start()
    load_w = [pltpu.make_async_copy(src, wa.at[at], in_sem[0]) for src, at in packed(w_hbm, c)]
    load_o = pltpu.make_async_copy(wout_hbm, wout, in_sem[1])
    load_r = [pltpu.make_async_copy(src, wr.at[at], in_sem[2]) for src, at in packed(w_hbm, 1 - c)]
    patch_ref, cot_ref = pair_ref.at[0], pair_ref.at[1]

    def remote(src, dst, s, r, chip, core):
        return pltpu.make_async_remote_copy(
            src_ref=src, dst_ref=dst, send_sem=s, recv_sem=r,
            device_id={"gcol": chip, "grow": core}, device_id_type=MESH,
        )

    def across_lanes(column):
        one = jnp.broadcast_to(column, (column.shape[0], 128)).astype(jnp.bfloat16)
        return jnp.concatenate([one] * (part // 128), axis=1)

    with scope("prep"):
        for ref, sem in zip((flag_ref, token_ref, dec_ref, pair_ref), in_sem):
            landed(ref, sem)
        for copy in load_w:
            copy.start()
        load_o.start()
        for copy in load_r:
            copy.start()
        square = (cols, cols)
        eye = lax.broadcasted_iota(jnp.int32, square, 0) == lax.broadcasted_iota(jnp.int32, square, 1)
        eye = eye.astype(jnp.float32)
        hidden_f, present_f = flag_ref[0].astype(jnp.float32), flag_ref[1].astype(jnp.float32)
        hidden_t, present_t = mm(eye, hidden_f, NT), mm(eye, present_f, NT)
        visible_t = present_t * (1.0 - hidden_t)
        for i in range(rows):
            hidden, visible = across_lanes(hidden_t[:, i : i + 1]), across_lanes(visible_t[:, i : i + 1])
            for f in range(2):
                at = slice(f * part, (f + 1) * part)
                ms[f, i] = patch_ref[i, :, at] * visible + cot_ref[i, :, at] * hidden
            for q in range(depth):
                at = slice(q * slab, (q + 1) * slab)
                gsx[i, :, at] = cot_ref[i, :, block(2 * q + 1 - xi)] * hidden[:, :slab]
                turn = (2 * q + 1 - i % 2) * slab
                gsr[i, :, at] = cot_ref[i, :, turn : turn + slab] * hidden[:, :slab]
            blank = jnp.zeros((rd.shape[1] - heads - 2, cols), jnp.float32)
            flags = jnp.concatenate([hidden_f[i : i + 1], present_f[i : i + 1], blank], axis=0)
            for n, dst in enumerate((rd, cd)):
                dst[i, :heads] = dec_ref[n, :, i, :]
                dst[i, heads:] = flags

    m_send, d_send, g_send, gc_send, w_send, n_send, p_send, c_send = [new_sem() for _ in range(8)]
    m_recv, (d_recv, g_recv, gc_recv, w_recv, n_recv, nc_recv, nr_recv, p_recv, c_recv) = (
        [sems.at[next(ids)] for _ in range(2)], [new_sem() for _ in range(9)]
    )

    g_col = remote(gsx, gcx.at[pl.ds(rows * c, rows)], gc_send, gc_recv, beside, 1)

    def g_row(i):
        return remote(gsr.at[i], gx.at[k], g_send, g_recv, rows * c + (i ^ 1), 0)

    def m_row(f, i):
        return remote(ms.at[f, i], mb.at[f * chips + k], m_send, m_recv[f], rows * c + i, 0)

    def m_col(f):
        return remote(ms.at[f], mb.at[pl.ds(f * chips, rows)], m_send, m_recv[f], k, 1)

    def d_row(i):
        return remote(rd.at[i], db.at[k], d_send, d_recv, rows * c + i, 0)

    d_col = remote(cd, db.at[pl.ds(0, rows)], d_send, d_recv, k, 1)

    def not_me(i):
        return jnp.logical_or(c == 1, k != i)

    def each_row(copy_of, owner=lambda i: i):
        for i in range(rows):

            @pl.when(not_me(owner(i)))
            def _():
                copy_of(i).start()

    def each_g_row():
        each_row(g_row, lambda i: i ^ 1)

    def drained(ref, sem, count, own, extra):
        @pl.when(c == 1)
        def _():
            landed(ref.at[pl.ds(0, count)], sem)

        for mine, less in ((k < rows, own), (k >= rows, 0)):

            @pl.when(jnp.logical_and(c == 0, mine))
            def _():
                landed(ref.at[pl.ds(0, count - less + extra)], sem)

    w_out = remote(wr, wb, w_send, w_recv, k, 1 - c)
    with scope("own_rows"):
        @pl.when(c == 1)
        def _():
            pltpu.make_async_copy(cd, db.at[pl.ds(rows, rows)], d_recv).start()
            for f in range(2):
                pltpu.make_async_copy(ms.at[f], mb.at[pl.ds(f * chips + rows, rows)], m_recv[f]).start()

        for i in range(rows):

            @pl.when(jnp.logical_and(c == 0, k == i))
            def _():
                pltpu.make_async_copy(rd.at[i], db.at[i], d_recv).start()
                pltpu.make_async_copy(gsr.at[i ^ 1], gx.at[i], g_recv).start()
                for f in range(2):
                    pltpu.make_async_copy(ms.at[f, i], mb.at[f * chips + i], m_recv[f]).start()

    with scope("barrier_wait"):
        pl.semaphore_wait(barrier, total - 1)
    with scope("launch"):
        each_row(d_row)

        @pl.when(c == 0)
        def _():
            d_col.start()
            m_col(1).start()
            m_col(0).start()

        for f in range(2):
            each_row(functools.partial(m_row, f))
        landed(wr, in_sem[2])
        w_out.start()
        g_col.start()

    t_at = lax.broadcasted_iota(jnp.int32, (toks, toks), 0)
    k_at = lax.broadcasted_iota(jnp.int32, (toks, toks), 1)
    gap_at = t_at - k_at
    mask = jnp.logical_and(gap_at >= 0, (gap_at & (cols - 1)) * c == 0)
    low = lax.broadcasted_iota(jnp.int32, (toks, 128), 1) < N
    same = (128, 128)
    head_of = [lax.broadcasted_iota(jnp.int32, same, d) // N for d in range(2)]
    averages = jnp.where(head_of[0] == head_of[1], 1.0 / N, 0.0).astype(jnp.bfloat16)

    with scope("arrive_decay"):
        landed(db, d_recv)
    with scope("decay"):
        ones = mask.astype(jnp.float32)
        dec = jnp.concatenate([db[i] for i in range(chips)], axis=1)
        run_s = lax.dot_general(ones, dec, NT, precision=PRECISE, preferred_element_type=jnp.float32)
        run_l = lax.dot_general(dec, ones, NT, precision=PRECISE, preferred_element_type=jnp.float32)
        run_a[...], run_b[...] = run_s, run_l
        for h in range(heads):
            gap = run_s[:, h : h + 1] - run_l[h : h + 1, :]
            dec_s[h] = jnp.where(mask, jnp.exp(jnp.minimum(gap, 0.0)), 0.0)
        unit = (t_at == k_at).astype(jnp.float32)
        flags_t = mm(unit, dec[heads:], NT)
        tok_hidden, tok_filled = across_lanes(flags_t[:, 0:1]), across_lanes(flags_t[:, 0:1] * flags_t[:, 1:2])
        tok_shown = across_lanes(1.0 - flags_t[:, 0:1])

    with scope("load_w"):
        landed(wa, in_sem[0])
        landed(wout, in_sem[1])

    def turn_decay():
        late = k_at - t_at
        reach = jnp.logical_and(late >= 0, (late & (cols - 1)) * c == 0)
        for h in range(heads):
            gap = run_b[h : h + 1, :] - run_a[:, h : h + 1]
            turned_s[h] = jnp.where(reach, jnp.exp(jnp.minimum(gap, 0.0)), 0.0)

    def halves(ref):
        return jnp.concatenate([ref[0], ref[1]], axis=1)

    def unpack(f):
        at = pl.ds(pl.multiple_of(f * part, part), part)
        either = mb[pl.ds(f * chips, chips)].reshape(toks, part)
        gb[:, at] = either * tok_hidden
        return either * tok_shown + token_ref[at].reshape(1, part) * tok_filled

    def split(f):
        for i in range(depth // 2):
            q = f * (depth // 2) + i
            at_i = slice(i * slab, (i + 1) * slab)
            ga[f, :, at_i] = gb[:, block(2 * q + xi)]

    def half_gn(f):
        at = pl.ds(pl.multiple_of(f * part, part), part)
        return mm(gb[:, at], wout[at, :], NN)

    def arrive_m(core):
        for f in range(2):

            @pl.when(core == f)
            def _():
                landed(mb.at[pl.ds(f * chips, chips)], m_recv[f])

    lend_sems = [(new_sem(), new_sem()) for _ in range(3)]

    def lend(i, src, dst):
        return remote(src, dst, *lend_sems[i], k, 1)

    pair = [pl.ds(i * 256, 256) for i in range(4)]
    lend_a = lend(0, ga, la)
    lend_x = lend(1, gx, lx)
    lend_n = lend(2, normed_s.at[:, pair[1]], ln)
    n_first = remote(normed_s.at[:, pair[0]], nx.at[:, pair[0]], n_send, n_recv, beside, c)
    n_col = remote(normed_s.at[:, pair[1]], nx.at[:, pair[1]], n_send, nc_recv, beside, 1)
    n_row = remote(normed_s.at[:, pair[1]], lnx, n_send, nr_recv, beside, 1)
    with scope("arrive_first"):
        arrive_m(c)
    with scope("proj_first"):
        own = unpack(c)
        firsts = [mm(own, wa[at : at + size], NT) for _, at, size in pieces]
        split(c)
        gn_first = half_gn(c)

        @pl.when(c == 0)
        def _():
            each_g_row()
            turn_decay()

    with scope("arrive_second"):
        arrive_m(1 - c)
    with scope("weights_wait"):
        landed(wb, w_recv)
    with scope("proj_second"):
        oth = unpack(1 - c)
        for dst, (_, at, size), first in zip((u_s, z_s, bc_s), pieces, firsts):
            dst[...] = (first + mm(oth, wb[at : at + size], NT)).astype(jnp.bfloat16)
        split(1 - c)


    def per_head(x):
        high = x.astype(jnp.bfloat16)
        rest = (x - high.astype(jnp.float32)).astype(jnp.bfloat16)
        return mm(high, averages, NN) + mm(rest, averages, NN)

    def if_core(core, copies):
        @pl.when(c == core)
        def _():
            for copy in copies:
                copy.start()

    if_core(0, [lend_a])

    with scope("forward"):
        b_bf, c_bf = bc_s[:, :N], bc_s[:, N:]
        scores = mm(c_bf, b_bf, NT)
        rest_at = pl.ds(pl.multiple_of((1 - c) * part, part), part)
        for p in range(half // 128):
            cols_p = slice(p * 128, (p + 1) * 128)
            if p >= 2:
                two = slice((p - 2) * 256, (p - 1) * 256)
                gn = gn_first[:, two] + mm(gb[:, rest_at], wout[rest_at, two], NN)
                gn_s[:, two] = gn.astype(jnp.bfloat16)
            u = u_s[:, cols_p].astype(jnp.float32)
            sig_u = 0.5 + 0.5 * jnp.tanh(0.5 * u)
            su_s[:, cols_p] = sig_u
            val_bf = (u * sig_u).astype(jnp.bfloat16)
            for h in (2 * p, 2 * p + 1):
                mat_s[h] = (dec_s[h] * scores).astype(jnp.bfloat16)
            y = jnp.where(low, mm(mat_s[2 * p], val_bf, NN), mm(mat_s[2 * p + 1], val_bf, NN))
            y_s[:, cols_p] = y
            z = z_s[:, cols_p].astype(jnp.float32)
            sig_z = 0.5 + 0.5 * jnp.tanh(0.5 * z)
            sz_s[:, cols_p] = sig_z
            gated = y * (z * sig_z)
            inv = lax.rsqrt(per_head(gated * gated) + EPSILON)
            inv_s[:, cols_p] = inv
            normed_s[:, cols_p] = (gated * inv).astype(jnp.bfloat16)
            if p == 1:
                n_first.start()
            if p == 3:
                if_core(1, [n_col])

                @pl.when(c == 1)
                def _():
                    each_g_row()

                if_core(0, [n_row, lend_n])

    with scope("turn_decay"):
        @pl.when(c == 1)
        def _():
            turn_decay()

    with scope("backward"):
        turned_scores = mm(b_bf, c_bf, NT)
        d_scores = jnp.zeros((toks, toks), jnp.float32)
        for p in range(half // 128):
            cols_p = slice(p * 128, (p + 1) * 128)
            z, sig_z, y, inv = z_s[:, cols_p].astype(jnp.float32), sz_s[:, cols_p], y_s[:, cols_p], inv_s[:, cols_p]
            act = z * sig_z
            normed = y * act * inv
            u, sig_u = u_s[:, cols_p].astype(jnp.float32), su_s[:, cols_p]
            val = u * sig_u
            val_bf = val.astype(jnp.bfloat16)
            gn = gn_s[:, cols_p].astype(jnp.float32)
            gg = inv * (gn - normed * per_head(gn * normed))
            dy = gg * act
            dz = gg * y * (sig_z + act * (1.0 - sig_z))
            dy_bf = dy.astype(jnp.bfloat16)
            dec_a, dec_b = turned_s[2 * p], turned_s[2 * p + 1]
            dv = jnp.where(
                low,
                mm((dec_a * turned_scores).astype(jnp.bfloat16), dy_bf, NN),
                mm((dec_b * turned_scores).astype(jnp.bfloat16), dy_bf, NN),
            )
            du = dv * (sig_u + val * (1.0 - sig_u))
            gp[:, cols_p] = du.astype(jnp.bfloat16)
            gp[:, half + p * 128 : half + (p + 1) * 128] = dz.astype(jnp.bfloat16)
            zero = jnp.zeros_like(dy)
            d_scores += dec_a * mm(val_bf, jnp.where(low, dy, zero).astype(jnp.bfloat16), NT)
            d_scores += dec_b * mm(val_bf, jnp.where(low, zero, dy).astype(jnp.bfloat16), NT)
        ds_bf = d_scores.astype(jnp.bfloat16)
        d_bc = jnp.concatenate([mm(ds_bf, c_bf, NN), mm(ds_bf, b_bf, TN)], axis=1)
        gp[:, 2 * half :] = d_bc.astype(jnp.bfloat16)

    with scope("pass_gx"):

        @pl.when(c == 0)
        def _():
            landed(gx, g_recv)

        if_core(0, [lend_x])

    home, slot = k // rows, lax.rem(k, rows)

    def row_back(f, chip):
        return remote(prs.at[f, chip], prow.at[f, slot], p_send, p_recv, chip, home)

    def col_back(n):
        return remote(pcs.at[pl.ds(n * chips, rows)], pcol.at[n], c_send, c_recv, k, 0)

    others = [
        2 * z + x
        for z in (end_far, near_far, mate)
        for x in (1 - xi, xi)
    ] + [2 * zi + 1 - xi]

    def project_back(g_ref, w_ref):
        return mm(g_ref[...], w_ref[...], NN).astype(jnp.bfloat16).reshape(chips, cols, part)

    def return_rows(f, some=others):
        for chip in some:
            row_back(f, chip).start()

    def keep_rows(f):

        @pl.when(home == 1)
        def _():
            row_back(f, k).start()

        @pl.when(home == 0)
        def _():
            pltpu.make_async_copy(prs.at[f, k], prow.at[f, slot], p_recv).start()

    class Sums:
        def __init__(self, w, z, zin, zout, slot):
            self.w, self.z, self.zin, self.zout, self.slot = w, z, zin, zout, slot
            self.send, self.out_recv, *self.in_recv = [new_sem() for _ in range(4)]

        def to_target(self, j, kind, chip, core):
            return remote(
                self.z.at[2 * j + core], self.zout.at[3 * self.slot + kind], self.send, self.out_recv, chip, core
            )

        def part(self, j):
            return self.w[block(order[j]), :]

        def ready(self, j, value):
            self.z[2 * j : 2 * j + 2] = value.astype(jnp.bfloat16).reshape(2, slab // 2, value.shape[1])

        def begin(self):
            @pl.when(outer)
            def _():
                for j in range(2):
                    self.ready(j, self.part(j))
                    two = pl.ds(2 * j, 2)
                    remote(
                        self.z.at[two], self.zin.at[two], self.send, self.in_recv[j], 2 * mate + xi, c
                    ).start()

            self.ready(2, self.part(2))
            for core in range(2):
                self.to_target(2, 0, 2 * mate + xi, core).start()
            self.ready(3, self.part(3))
            pltpu.make_async_copy(
                self.z.at[6 + c], self.zout.at[3 * self.slot + 2], self.out_recv
            ).start()
            self.to_target(3, 2, k, 1 - c).start()

        def combine(self):
            @pl.when(inner)
            def _():
                for j in range(2):
                    landed(self.zin.at[pl.ds(2 * j, 2)], self.in_recv[j])
                    passed = self.zin[2 * j : 2 * j + 2].astype(jnp.float32).reshape(slab, self.w.shape[1])
                    self.ready(j, self.part(j) + passed)
                    for core in range(2):
                        self.to_target(j, 1, 2 * order[j] + xi, core).start()

        def drain(self):
            landed(self.z.at[pl.ds(0, 7)], self.send)

    col_first = Sums(wca, zsa, zca, zr, 0)
    col_second = Sums(wcb, zsb, zcb, zr, 1)
    row_sums = Sums(wq, zq, zcq, zrq, c)

    @pl.when(c == 0)
    def _():
        with scope("back_project_0"):
            for f, w_ref in enumerate((wa, wb)):
                prs[f] = project_back(gp, w_ref)

                keep_rows(f)

                @pl.when(inner)
                def _():
                    return_rows(f)

                if f == 0:

                    @pl.when(outer)
                    def _():
                        return_rows(0, others[:4])

        with scope("wait_n0"):
            landed(nx.at[:, pair[0]], n_recv)
        with scope("row_product_0"):
            wq[...] = mm(halves(ga), normed_s[:, :256], TN) + mm(gx[...].reshape(toks, part), nx[:, :256], TN)

    @pl.when(c == 1)
    def _():
        with scope("col_back_1"):
            for n, w_ref in enumerate((wa, wb)):
                pcs[n * chips : (n + 1) * chips] = project_back(gp, w_ref)
                col_back(n).start()
                pcol[n] = pcs[n * chips + rows : (n + 1) * chips]
        with scope("wait_n1"):
            landed(gcx, gc_recv)
            landed(nx.at[:, pair[0]], n_recv)

        def col_product(i):
            own = mm(halves(ga), normed_s[:, i * 256 : (i + 1) * 256], TN)
            return own + mm(gcx[...].reshape(toks, part), nx[:, i * 256 : (i + 1) * 256], TN)

        with scope("col_first"):
            wca[...] = col_product(0)
            col_first.begin()
        with scope("wait_n2"):
            landed(nx.at[:, pair[1]], nc_recv)
        with scope("col_second"):
            wcb[...] = col_product(1)
            col_second.begin()
        with scope("lent_wait"):
            for copy in (lend_a, lend_x, lend_n, n_row):
                copy.wait_recv()
        with scope("row_product_1"):
            wq[...] = mm(halves(la), ln[...], TN) + mm(lx[...].reshape(toks, part), lnx[...], TN)

    with scope("row_begin"):
        row_sums.begin()

    with scope("return_rows"):
        @pl.when(jnp.logical_and(c == 0, outer))
        def _():
            return_rows(0, others[4:])
            return_rows(1)


    @pl.when(c == 1)
    def _():
        with scope("col_combine"):
            col_first.combine()
            col_second.combine()

    with scope("row_combine"):
        row_sums.combine()

    with scope("parts_wait"):

        @pl.when(c == 0)
        def _():
            landed(pcol, c_recv)

        landed(prow, p_recv)

    with scope("patch_grad"):
        for f in range(2):
            by_row, by_col = prow.at[f], pcol.at[1 - f]
            for i in range(rows):
                keep = visible_t[:, i : i + 1]
                both = by_row[i].astype(jnp.float32) + by_col[i].astype(jnp.float32)
                pg_ref[i, :, f * part : (f + 1) * part] = (both * keep).astype(pg_ref.dtype)

    results = [
        pltpu.make_async_copy(pg_ref, pg_out, in_sem[0]),
        pltpu.make_async_copy(out_ref, sum_out, in_sem[1]),
    ]
    results[0].start()

    with scope("sums_wait"):
        landed(zr.at[pl.ds(0, 3)], col_first.out_recv)
        landed(zr.at[pl.ds(3, 3)], col_second.out_recv)
        landed(zrq, row_sums.out_recv)

    with scope("weight_sum"):
        for ref, at, size in ((zrq.at[0:3], 0, 256), (zrq.at[3:6], 256, 256), (zr.at[0:3], half, 256), (zr.at[3:6], half + 256, 256)):
            acc = ref[0].astype(jnp.float32) + ref[1].astype(jnp.float32)
            acc += ref[2].astype(jnp.float32)
            out_ref[:, at : at + size] = acc * scale
    results[1].start()

    with scope("drain"):
        drained(db, d_send, rows, 1, rows)
        drained(mb, m_send, 2 * rows, 2, 2 * rows)
        drained(gx, g_send, rows, 1, 0)
        landed(gsx, gc_send)
        landed(wb, w_send)
        row_sums.drain()
        landed(normed_s, n_send)

        @pl.when(jnp.logical_and(c == 0, home == 0))
        def _():
            landed(pcs.at[pl.ds(0, 2 * chips - 2)], p_send)

        @pl.when(jnp.logical_and(c == 0, home == 1))
        def _():
            landed(pcs, p_send)

        @pl.when(c == 0)
        def _():
            for copy in (lend_a, lend_x, lend_n):
                copy.wait_send()

        @pl.when(c == 1)
        def _():
            col_first.drain()
            col_second.drain()
            landed(pcol, c_send)

        for copy in results:
            copy.wait()


def store_kernel(a_ref, b_ref, a_hbm, b_hbm, sem):
    copies = [
        pltpu.make_async_copy(a_ref, a_hbm, sem.at[0]),
        pltpu.make_async_copy(b_ref, b_hbm, sem.at[1]),
    ]
    for copy in copies:
        copy.start()
    for copy in copies:
        copy.wait()


def owned(
    patches, mask_token, masked, tissue, in_weight, out_weight, row_decay, col_decay, cotangent
):
    rows, cols, feat = patches.shape
    chips = lax.axis_size("gcol")
    toks, heads = chips * cols, row_decay.shape[0]
    half, part = out_weight.shape[1], in_weight.shape[1]
    width = 2 * half + 2 * N
    slab = feat // chips
    bf, fl = jnp.bfloat16, jnp.float32
    vmem, dma = pltpu.VMEM, pltpu.SemaphoreType.DMA
    anywhere = pl.BlockSpec(memory_space=pltpu.HBM)
    place = pl.BlockSpec(memory_space=pl.ANY)
    scale = 1.0 / math.sqrt(2 * rows * cols * chips)
    aux = heads + 8
    results = pl.pallas_call(
        functools.partial(layer_kernel, chips, rows, scale),
        name="layer",
        out_shape=(vmem(patches.shape, bf), vmem((slab // 2, 2 * half), fl)),
        in_specs=[anywhere] * 9,
        out_specs=(place, place),
        scratch_shapes=[
            dma((41,)), vmem(patches.shape, bf), vmem((slab // 2, 2 * half), fl),
            vmem((2,) + patches.shape, bf), vmem(mask_token.shape, bf),
            vmem((2,) + masked.shape, masked.dtype), vmem((2,) + row_decay.shape, fl),
            vmem((2, rows, cols, part), bf), vmem((2 * chips, cols, part), bf),
            vmem((rows, aux, cols), fl), vmem((rows, aux, cols), fl), vmem((chips, aux, cols), fl),
            vmem((width, part), bf), vmem((width, part), bf), vmem((width, part), bf), vmem(out_weight.shape, bf),
            vmem((toks, feat), bf), vmem((rows, cols, part), bf), vmem((2, toks, part // 2), bf),
            vmem((chips, cols, part), bf), vmem((rows, cols, part), bf), vmem((chips, cols, part), bf),
            vmem((toks, half), bf), vmem((2, toks, part // 2), bf),
            vmem((chips, cols, part), bf), vmem((toks, half // 2), bf), vmem((toks, half // 2), bf),
            vmem((toks, half), bf), vmem((toks, half), bf), vmem((toks, half), fl), vmem((toks, half), fl),
            vmem((toks, half), bf), vmem((toks, 2 * N), bf), vmem((toks, half), bf),
            vmem((toks, half), fl), vmem((toks, half), fl),
            vmem((heads, toks, toks), bf), vmem((heads, toks, toks), fl),
            vmem((heads, toks, toks), fl), vmem((toks, aux), fl), vmem((aux, toks), fl),
            vmem((toks, width), bf), vmem((2, chips, cols, part), bf), vmem((2 * chips, cols, part), bf),
            vmem((2, rows, cols, part), bf), vmem((2, rows, cols, part), bf),
            vmem((half, half // 2), fl), vmem((half, half // 2), fl), vmem((half, half // 2), fl),
            vmem((8, slab // 2, half // 2), bf), vmem((8, slab // 2, half // 2), bf), vmem((8, slab // 2, half // 2), bf),
            vmem((4, slab // 2, half // 2), bf), vmem((4, slab // 2, half // 2), bf), vmem((4, slab // 2, half // 2), bf),
            vmem((6, slab // 2, half // 2), bf), vmem((6, slab // 2, half // 2), bf),
        ],
        compiler_params=pltpu.CompilerParams(
            collective_id=0, has_side_effects=True, vmem_limit_bytes=60 << 20
        ),
    )(
        patches, mask_token, cotangent, masked, tissue, row_decay, col_decay,
        in_weight, out_weight,
    )
    return pl.pallas_call(
        store_kernel,
        name="store",
        out_shape=tuple(jax.ShapeDtypeStruct(r.shape, r.dtype) for r in results),
        in_specs=[place] * 2,
        out_specs=[anywhere] * 2,
        scratch_shapes=[dma((2,))],
        compiler_params=pltpu.CompilerParams(vmem_limit_bytes=1 << 20),
    )(*results)


def body(*args):
    rows = args[0].shape[0]
    cols = args[0].shape[1]
    if lax.axis_size("grow") == 2 and rows == 4 and lax.axis_size("gcol") == 2 * rows and cols & (cols - 1) == 0:
        return owned(*args)
    return shards(*args)


def solution(mesh):
    return jax.shard_map(
        body,
        mesh=mesh,
        in_specs=(
            P(("groups", "grow"), "gcol", None),
            P(),
            P(("groups", "grow"), "gcol"),
            P(("groups", "grow"), "gcol"),
            P(None, "grow"),
            P(None, "grow"),
            P(None, ("groups", "grow"), "gcol"),
            P(None, ("groups", "grow"), "gcol"),
            P(("groups", "grow"), "gcol", None),
        ),
        out_specs=(P(("groups", "grow"), "gcol", None), P(("groups", "gcol", "grow"), None)),
        check_vma=False,
    )
```

```python
import functools
import itertools
import math

import jax
import jax.numpy as jnp
from jax import lax
from jax.experimental import pallas as pl
from jax.experimental.pallas import tpu as pltpu
from jax.sharding import PartitionSpec as P

E = 1024
HEADS = 16
N = 64


EPSILON = 1e-05
PRECISE = lax.Precision.HIGHEST


def prefix(value, axis, join, neutral):
    count, mine = (lax.axis_size(axis), lax.axis_index(axis))
    pieces = jax.tree.map(lambda part: lax.all_gather(part, axis), value)
    so_far = jax.tree.map(
        lambda part, zero: jnp.full_like(part, 0) + jnp.asarray(zero, part.dtype), value, neutral
    )

    def prefix_hop(position, so_far):
        longer = join(so_far, jax.tree.map(lambda part: part[position], pieces))
        return jax.tree.map(lambda new, old: jnp.where(position < mine, new, old), longer, so_far)

    return lax.fori_loop(0, count - 1, prefix_hop, so_far)


def carried_in(shard, axis, combine, identity):
    length, position = (lax.axis_size(axis), lax.axis_index(axis))
    everything = jax.tree.map(
        lambda part, kind: lax.all_gather(part.astype(kind), axis),
        shard,
        jax.tree.map(lambda a: jnp.bfloat16 if a.dtype == jnp.float32 else a.dtype, shard),
    )
    start = jax.tree.map(
        lambda part, zero: jnp.broadcast_to(jnp.asarray(zero, part.dtype), part.shape),
        shard,
        identity,
    )

    def carried_hop(k, before):
        at = length - 1 - k
        reached = at > position
        new = combine(
            before, jax.tree.map(lambda part, own: part[at].astype(own.dtype), everything, shard)
        )
        return jax.tree.map(lambda a, b: jnp.where(reached, a, b), new, before)

    return lax.fori_loop(0, length, carried_hop, start)


def shortened(shard):

    def short(part):
        return part.astype(jnp.bfloat16) if part.dtype == jnp.float32 else part

    return jax.tree.map(short, shard)


def silu_grad(pre_act):
    sigmoid_v = jax.nn.sigmoid(pre_act)
    return sigmoid_v * (1.0 + pre_act * (1.0 - sigmoid_v))


def per_channel(head_part, channels):
    return jnp.repeat(head_part, channels // head_part.shape[-1], axis=-1)


def line_form(head_lines, channels):
    return per_channel(head_lines.transpose(1, 2, 0), channels)


def carry_on(log_lines, state):
    return per_channel(jnp.exp(log_lines), state.shape[2])[:, None, :] * state


def prepare(log_decay):
    length = log_decay.shape[2]
    causal = jnp.arange(length)[:, None] >= jnp.arange(length)[None, :]
    running = jnp.einsum(
        "glk,tk->glt", log_decay, causal.astype(log_decay.dtype), precision=PRECISE
    )
    whole_log = running[:, :, -1]
    log_gaps = running[:, :, :, None] - running[:, :, None, :]
    decay_mat = jnp.where(causal, jnp.exp(jnp.where(causal, log_gaps, 0.0)), 0.0)
    return (running, whole_log, decay_mat)


def chain_link(earlier, later):
    return (earlier[0] + later[0], carry_on(later[0], earlier[1]) + later[1])


def split_heads(lines, head_count):
    line_count, length, channels = lines.shape
    return lines.reshape(line_count, length, head_count, channels // head_count)


def local_summary(inputs, key_vecs, prepared):
    running, whole_log, decay_mat = prepared
    to_end = line_form(jnp.exp(whole_log[:, :, None] - running), inputs.shape[2])
    fresh = jnp.einsum("ltc,ltn->lnc", inputs * to_end, key_vecs, precision=PRECISE)
    return (whole_log.T, fresh)


def local_return(query_vecs, prepared, upstream):
    running, whole_log, decay_mat = prepared
    from_start = line_form(jnp.exp(running), upstream.shape[2])
    backward = jnp.einsum("ltc,ltn->lnc", upstream * from_start, query_vecs, precision=PRECISE)
    return (whole_log.T, backward)


def local_outputs(inputs, key_vecs, query_vecs, prepared, incoming):
    running, whole_log, decay_mat = prepared
    head_count = decay_mat.shape[0]
    line_count, length, channels = inputs.shape
    scores = jnp.einsum("ltn,lkn->ltk", query_vecs, key_vecs, precision=PRECISE)
    within = jnp.einsum(
        "gltk,lkgp->ltgp",
        decay_mat * scores[None],
        split_heads(inputs, head_count),
        precision=PRECISE,
    )
    within = within.reshape(line_count, length, channels)
    carried = jnp.einsum("ltn,lnc->ltc", query_vecs, incoming, precision=PRECISE)
    return within + carried * line_form(jnp.exp(running), channels)


def local_grads(inputs, key_vecs, query_vecs, prepared, incoming, returning, upstream):
    running, whole_log, decay_mat = prepared
    head_count = decay_mat.shape[0]
    line_count, length, channels = inputs.shape
    from_start = line_form(jnp.exp(running), channels)
    to_end = line_form(jnp.exp(whole_log[:, :, None] - running), channels)
    scores = jnp.einsum("ltn,lkn->ltk", query_vecs, key_vecs, precision=PRECISE)
    heads_up = split_heads(upstream, head_count)
    heads_in = split_heads(inputs, head_count)
    grad_inputs = jnp.einsum(
        "gltk,ltgp->lkgp", decay_mat * scores[None], heads_up, precision=PRECISE
    ).reshape(line_count, length, channels)
    grad_inputs = (
        grad_inputs + jnp.einsum("lnc,lkn->lkc", returning, key_vecs, precision=PRECISE) * to_end
    )
    mixed = jnp.einsum("ltgp,lkgp->gltk", heads_up, heads_in, precision=PRECISE) * decay_mat
    grad_keys = jnp.einsum("gltk,ltn->lkn", mixed, query_vecs, precision=PRECISE)
    grad_keys = grad_keys + jnp.einsum(
        "lkc,lnc->lkn", inputs * to_end, returning, precision=PRECISE
    )
    grad_queries = jnp.einsum("gltk,lkn->ltn", mixed, key_vecs, precision=PRECISE)
    grad_queries = grad_queries + jnp.einsum(
        "ltc,lnc->ltn", upstream * from_start, incoming, precision=PRECISE
    )
    return (grad_inputs, grad_keys, grad_queries)


def shards(
    patches, mask_token, masked, tissue, in_weight, out_weight, row_decay, col_decay, cotangent
):
    grid_rows, grid_cols, feat_width = patches.shape
    tok_count = grid_rows * grid_cols
    chosen = (masked == 1)[:, :, None]
    present = tissue.astype(jnp.bfloat16)[:, :, None]
    model_in = jnp.where(chosen, mask_token[None, None, :], patches) * present
    flat_in = model_in.reshape(tok_count, feat_width)
    inner_width = E
    half_width = inner_width // 2
    state_size = N
    number_of_heads = HEADS // 2
    offset = 2 * inner_width
    full_in, full_out = (
        lax.all_gather(in_weight, "grow", axis=1, tiled=True),
        lax.all_gather(out_weight, "grow", axis=1, tiled=True),
    )
    projected = lax.dot_general(
        flat_in, full_in, (((1,), (1,)), ((), ())), preferred_element_type=jnp.float32
    )
    proj_bf = projected.astype(jnp.bfloat16)
    pre_values = proj_bf[:, :inner_width].astype(jnp.float32)
    gate_pre = proj_bf[:, inner_width:offset].astype(jnp.float32)
    key_rows = (
        proj_bf[:, offset : offset + state_size]
        .astype(jnp.float32)
        .reshape(grid_rows, grid_cols, state_size)
    )
    query_rows = (
        proj_bf[:, offset + state_size : offset + 2 * state_size]
        .astype(jnp.float32)
        .reshape(grid_rows, grid_cols, state_size)
    )
    key_cols = (
        proj_bf[:, offset + 2 * state_size : offset + 3 * state_size]
        .astype(jnp.float32)
        .reshape(grid_rows, grid_cols, state_size)
        .transpose(1, 0, 2)
    )
    query_cols = (
        proj_bf[:, offset + 3 * state_size : offset + 4 * state_size]
        .astype(jnp.float32)
        .reshape(grid_rows, grid_cols, state_size)
        .transpose(1, 0, 2)
    )
    values = jax.nn.silu(pre_values)
    row_inputs = values[:, :half_width].reshape(grid_rows, grid_cols, half_width)
    col_inputs = values[:, half_width:].reshape(grid_rows, grid_cols, half_width).transpose(1, 0, 2)
    row_prep = prepare(row_decay)
    col_prep = prepare(col_decay.transpose(0, 2, 1))
    row_zero = (
        jnp.zeros((grid_rows, number_of_heads), jnp.float32),
        jnp.zeros((grid_rows, state_size, half_width), jnp.float32),
    )
    col_zero = (
        jnp.zeros((grid_cols, number_of_heads), jnp.float32),
        jnp.zeros((grid_cols, state_size, half_width), jnp.float32),
    )
    row_entry = prefix(local_summary(row_inputs, key_rows, row_prep), "gcol", chain_link, row_zero)[
        1
    ]
    grow_size = lax.axis_size("grow")
    my_block = lax.axis_index("grow")
    parts_in, parts_key, parts_log = (
        lax.all_gather(
            proj_bf[:, half_width:inner_width].reshape(grid_rows, grid_cols, half_width),
            "grow",
            axis=0,
            tiled=True,
        ),
        lax.all_gather(
            proj_bf[:, offset + 2 * state_size : offset + 3 * state_size].reshape(
                grid_rows, grid_cols, state_size
            ),
            "grow",
            axis=0,
            tiled=True,
        ),
        lax.all_gather(
            col_decay.transpose(1, 0, 2).astype(jnp.bfloat16), "grow", axis=0, tiled=True
        ).astype(jnp.float32),
    )
    col_entry = col_zero[1]
    for block_idx in range(grow_size):
        lower_row = block_idx * grid_rows
        piece_in = jax.nn.silu(
            parts_in[lower_row : lower_row + grid_rows].astype(jnp.float32)
        ).transpose(1, 0, 2)
        piece_keys = (
            parts_key[lower_row : lower_row + grid_rows].astype(jnp.float32).transpose(1, 0, 2)
        )
        piece_log = parts_log[lower_row : lower_row + grid_rows].transpose(1, 2, 0)
        whole_log, piece_state = local_summary(piece_in, piece_keys, prepare(piece_log))
        moved = carry_on(whole_log, col_entry) + piece_state
        col_entry = jnp.where(block_idx < my_block, moved, col_entry)
    row_out = local_outputs(row_inputs, key_rows, query_rows, row_prep, row_entry)
    col_out = local_outputs(col_inputs, key_cols, query_cols, col_prep, col_entry).transpose(
        1, 0, 2
    )
    mixed = jnp.concatenate(
        [row_out.reshape(tok_count, half_width), col_out.reshape(tok_count, half_width)], axis=1
    )
    gate_act = jax.nn.silu(gate_pre)
    head_size = inner_width // HEADS
    gated = (mixed * gate_act).reshape(tok_count, HEADS, head_size)
    inv_rms = lax.rsqrt(jnp.mean(gated * gated, axis=2, keepdims=True) + EPSILON)
    normed = gated * inv_rms
    normed_bf = normed.reshape(tok_count, inner_width).astype(jnp.bfloat16)
    grad_out = (cotangent * masked.astype(jnp.bfloat16)[:, :, None]).reshape(tok_count, feat_width)
    total_patches = tok_count * lax.axis_size("gcol") * lax.axis_size("grow")
    weight_sum = lax.psum_scatter(
        lax.dot_general(
            grad_out, normed_bf, (((0,), (0,)), ((), ())), preferred_element_type=jnp.float32
        ),
        ("gcol", "grow"),
        scatter_dimension=0,
        tiled=True,
    )
    out_weight_grad = weight_sum * (1.0 / math.sqrt(total_patches))
    grad_normed_bf = jnp.dot(grad_out, full_out, preferred_element_type=jnp.float32).astype(
        jnp.bfloat16
    )
    grad_normed = lax.optimization_barrier(grad_normed_bf).astype(jnp.float32)
    grad_normed = grad_normed.reshape(tok_count, HEADS, head_size)
    grad_gated = inv_rms * (
        grad_normed - normed * jnp.mean(grad_normed * normed, axis=2, keepdims=True)
    )
    grad_gated = grad_gated.reshape(tok_count, inner_width)
    grad_mixed = grad_gated * gate_act
    grad_gate = grad_gated * mixed * silu_grad(gate_pre)
    row_up = grad_mixed[:, :half_width].reshape(grid_rows, grid_cols, half_width)
    col_up = grad_mixed[:, half_width:].reshape(grid_rows, grid_cols, half_width).transpose(1, 0, 2)
    row_exit = carried_in(local_return(query_rows, row_prep, row_up), "gcol", chain_link, row_zero)[
        1
    ]
    parts_up, parts_query = (
        lax.all_gather(
            shortened(grad_mixed[:, half_width:].reshape(grid_rows, grid_cols, half_width)),
            "grow",
            axis=0,
            tiled=True,
        ),
        lax.all_gather(
            proj_bf[:, offset + 3 * state_size : offset + 4 * state_size].reshape(
                grid_rows, grid_cols, state_size
            ),
            "grow",
            axis=0,
            tiled=True,
        ),
    )
    col_exit = col_zero[1]
    for block_idx in reversed(range(grow_size)):
        lower_row = block_idx * grid_rows
        piece_up = parts_up[lower_row : lower_row + grid_rows].transpose(1, 0, 2)
        piece_queries = (
            parts_query[lower_row : lower_row + grid_rows].astype(jnp.float32).transpose(1, 0, 2)
        )
        piece_log = parts_log[lower_row : lower_row + grid_rows].transpose(1, 2, 0)
        whole_log, piece_back = local_return(piece_queries, prepare(piece_log), piece_up)
        moved = carry_on(whole_log, col_exit) + piece_back
        col_exit = jnp.where(block_idx > my_block, moved, col_exit)
    grad_row_in, grad_row_key, grad_row_query = local_grads(
        row_inputs, key_rows, query_rows, row_prep, row_entry, row_exit, row_up
    )
    grad_col_in, grad_col_key, grad_col_query = local_grads(
        col_inputs, key_cols, query_cols, col_prep, col_entry, col_exit, col_up
    )
    grad_values = jnp.concatenate(
        [
            grad_row_in.reshape(tok_count, half_width),
            grad_col_in.transpose(1, 0, 2).reshape(tok_count, half_width),
        ],
        axis=1,
    )
    grad_proj = jnp.concatenate(
        [
            grad_values * silu_grad(pre_values),
            grad_gate,
            grad_row_key.reshape(tok_count, state_size),
            grad_row_query.reshape(tok_count, state_size),
            grad_col_key.transpose(1, 0, 2).reshape(tok_count, state_size),
            grad_col_query.transpose(1, 0, 2).reshape(tok_count, state_size),
        ],
        axis=1,
    ).astype(jnp.bfloat16)
    keep_mask = present * (1 - masked).astype(jnp.bfloat16)[:, :, None]
    grad_model_in = jnp.dot(grad_proj, full_in, preferred_element_type=jnp.float32).reshape(
        grid_rows, grid_cols, feat_width
    )
    patch_grad = (grad_model_in * keep_mask).astype(jnp.bfloat16)
    return (patch_grad, out_weight_grad)


MESH = pl.DeviceIdType.MESH
NT = (((1,), (1,)), ((), ()))
NN = (((1,), (0,)), ((), ()))
TN = (((0,), (0,)), ((), ()))


def mm(a, b, dims):
    return lax.dot_general(a, b, dims, preferred_element_type=jnp.float32)


def layer_kernel(
    chips, rows, scale,
    patch_hbm, token_hbm, cot_hbm, hidden_hbm, present_hbm, rdec_hbm, cdec_hbm, w_hbm, wout_hbm,
    pg_out, sum_out,
    sems, pg_ref, out_ref, pair_ref, token_ref, flag_ref, dec_ref,
    ms, mb, rd, cd, db, wa, wb, wr, wout, gb, gsr, ga, gx, gsx, gcx, nx, la, lx, ln, lnx, u_s, z_s, su_s, sz_s, gn_s, bc_s,
    normed_s, y_s, inv_s, mat_s, dec_s, turned_s, run_a, run_b, gp, prs, pcs, prow, pcol,
    wca, wcb, wq, zsa, zsb, zq, zca, zcb, zcq, zr, zrq,
):
    k, c = lax.axis_index("gcol"), lax.axis_index("grow")
    depth = chips // 2
    zi, xi = k // 2, lax.rem(k, 2)
    cols = ms.shape[2]
    toks = chips * cols
    feat, half, part = token_ref.shape[0], wout.shape[1], wa.shape[1]
    heads, width = dec_ref.shape[1], wa.shape[0]
    total = 2 * chips
    slab = feat // chips
    scope = jax.named_scope
    ids = itertools.count()

    def new_sem():
        return sems.at[next(ids)]

    def landed(ref, sem):
        pltpu.make_async_copy(ref, ref, sem).wait()

    me = 2 * k + c
    barrier = pltpu.get_barrier_semaphore()
    for d in range(1, total):
        to = lax.rem(me + d, total)
        pl.semaphore_signal(
            barrier, inc=1, device_id={"gcol": to // 2, "grow": lax.rem(to, 2)}, device_id_type=MESH
        )

    side = zi // 2
    mate = zi + 1 - 2 * lax.rem(zi, 2)
    near_far, end_far = 2 - side, 3 - 3 * side
    order = (end_far, near_far, mate, zi)
    outer = zi == 3 * side
    inner = jnp.logical_not(outer)
    beside = 2 * zi + 1 - xi

    def block(q):
        return pl.ds(pl.multiple_of(q * slab, slab), slab)

    pieces = ((0, 0, half), (2 * half, half, half), (4 * half, 2 * half, 2 * N))

    def packed(ref, core):
        return [
            (ref.at[pl.ds(pl.multiple_of(base + core * size, 128), size)], pl.ds(at, size))
            for base, at, size in pieces
        ]

    in_sem = [new_sem() for _ in range(4)]
    loads = [
        pltpu.make_async_copy(src, dst, s)
        for src, dst, s in (
            (hidden_hbm, flag_ref.at[0], in_sem[0]), (present_hbm, flag_ref.at[1], in_sem[0]),
            (token_hbm, token_ref, in_sem[1]),
            (rdec_hbm, dec_ref.at[0], in_sem[2]), (cdec_hbm, dec_ref.at[1], in_sem[2]),
            (patch_hbm, pair_ref.at[0], in_sem[3]), (cot_hbm, pair_ref.at[1], in_sem[3]),
        )
    ]
    for copy in loads:
        copy.start()
    load_w = [pltpu.make_async_copy(src, wa.at[at], in_sem[0]) for src, at in packed(w_hbm, c)]
    load_o = pltpu.make_async_copy(wout_hbm, wout, in_sem[1])
    load_r = [pltpu.make_async_copy(src, wr.at[at], in_sem[2]) for src, at in packed(w_hbm, 1 - c)]
    patch_ref, cot_ref = pair_ref.at[0], pair_ref.at[1]

    def remote(src, dst, s, r, chip, core):
        return pltpu.make_async_remote_copy(
            src_ref=src, dst_ref=dst, send_sem=s, recv_sem=r,
            device_id={"gcol": chip, "grow": core}, device_id_type=MESH,
        )

    def across_lanes(column):
        one = jnp.broadcast_to(column, (column.shape[0], 128)).astype(jnp.bfloat16)
        return jnp.concatenate([one] * (part // 128), axis=1)

    with scope("prep"):
        for ref, sem in zip((flag_ref, token_ref, dec_ref, pair_ref), in_sem):
            landed(ref, sem)
        for copy in load_w:
            copy.start()
        load_o.start()
        for copy in load_r:
            copy.start()
        square = (cols, cols)
        eye = lax.broadcasted_iota(jnp.int32, square, 0) == lax.broadcasted_iota(jnp.int32, square, 1)
        eye = eye.astype(jnp.float32)
        hidden_f, present_f = flag_ref[0].astype(jnp.float32), flag_ref[1].astype(jnp.float32)
        hidden_t, present_t = mm(eye, hidden_f, NT), mm(eye, present_f, NT)
        visible_t = present_t * (1.0 - hidden_t)
        for i in range(rows):
            hidden, visible = across_lanes(hidden_t[:, i : i + 1]), across_lanes(visible_t[:, i : i + 1])
            for f in range(2):
                at = slice(f * part, (f + 1) * part)
                ms[f, i] = patch_ref[i, :, at] * visible + cot_ref[i, :, at] * hidden
            for q in range(depth):
                at = slice(q * slab, (q + 1) * slab)
                gsx[i, :, at] = cot_ref[i, :, block(2 * q + 1 - xi)] * hidden[:, :slab]
                turn = (2 * q + 1 - i % 2) * slab
                gsr[i, :, at] = cot_ref[i, :, turn : turn + slab] * hidden[:, :slab]
            blank = jnp.zeros((rd.shape[1] - heads - 2, cols), jnp.float32)
            flags = jnp.concatenate([hidden_f[i : i + 1], present_f[i : i + 1], blank], axis=0)
            for n, dst in enumerate((rd, cd)):
                dst[i, :heads] = dec_ref[n, :, i, :]
                dst[i, heads:] = flags

    m_send, d_send, g_send, gc_send, w_send, n_send, p_send, c_send = [new_sem() for _ in range(8)]
    m_recv, (d_recv, g_recv, gc_recv, w_recv, n_recv, nc_recv, nr_recv, p_recv, c_recv) = (
        [sems.at[next(ids)] for _ in range(2)], [new_sem() for _ in range(9)]
    )

    g_col = remote(gsx, gcx.at[pl.ds(rows * c, rows)], gc_send, gc_recv, beside, 1)

    def g_row(i):
        return remote(gsr.at[i], gx.at[k], g_send, g_recv, rows * c + (i ^ 1), 0)

    def m_row(f, i):
        return remote(ms.at[f, i], mb.at[f * chips + k], m_send, m_recv[f], rows * c + i, 0)

    def m_col(f):
        return remote(ms.at[f], mb.at[pl.ds(f * chips, rows)], m_send, m_recv[f], k, 1)

    def d_row(i):
        return remote(rd.at[i], db.at[k], d_send, d_recv, rows * c + i, 0)

    d_col = remote(cd, db.at[pl.ds(0, rows)], d_send, d_recv, k, 1)

    def not_me(i):
        return jnp.logical_or(c == 1, k != i)

    def each_row(copy_of, owner=lambda i: i):
        for i in range(rows):

            @pl.when(not_me(owner(i)))
            def _():
                copy_of(i).start()

    def each_g_row():
        each_row(g_row, lambda i: i ^ 1)

    def drained(ref, sem, count, own, extra):
        @pl.when(c == 1)
        def _():
            landed(ref.at[pl.ds(0, count)], sem)

        for mine, less in ((k < rows, own), (k >= rows, 0)):

            @pl.when(jnp.logical_and(c == 0, mine))
            def _():
                landed(ref.at[pl.ds(0, count - less + extra)], sem)

    w_out = remote(wr, wb, w_send, w_recv, k, 1 - c)
    with scope("own_rows"):
        @pl.when(c == 1)
        def _():
            pltpu.make_async_copy(cd, db.at[pl.ds(rows, rows)], d_recv).start()
            for f in range(2):
                pltpu.make_async_copy(ms.at[f], mb.at[pl.ds(f * chips + rows, rows)], m_recv[f]).start()

        for i in range(rows):

            @pl.when(jnp.logical_and(c == 0, k == i))
            def _():
                pltpu.make_async_copy(rd.at[i], db.at[i], d_recv).start()
                pltpu.make_async_copy(gsr.at[i ^ 1], gx.at[i], g_recv).start()
                for f in range(2):
                    pltpu.make_async_copy(ms.at[f, i], mb.at[f * chips + i], m_recv[f]).start()

    with scope("barrier_wait"):
        pl.semaphore_wait(barrier, total - 1)
    with scope("launch"):
        each_row(d_row)

        @pl.when(c == 0)
        def _():
            d_col.start()
            m_col(1).start()
            m_col(0).start()

        for f in range(2):
            each_row(functools.partial(m_row, f))
        landed(wr, in_sem[2])
        w_out.start()
        g_col.start()

    t_at = lax.broadcasted_iota(jnp.int32, (toks, toks), 0)
    k_at = lax.broadcasted_iota(jnp.int32, (toks, toks), 1)
    gap_at = t_at - k_at
    mask = jnp.logical_and(gap_at >= 0, (gap_at & (cols - 1)) * c == 0)
    low = lax.broadcasted_iota(jnp.int32, (toks, 128), 1) < N
    same = (128, 128)
    head_of = [lax.broadcasted_iota(jnp.int32, same, d) // N for d in range(2)]
    averages = jnp.where(head_of[0] == head_of[1], 1.0 / N, 0.0).astype(jnp.bfloat16)

    with scope("arrive_decay"):
        landed(db, d_recv)
    with scope("decay"):
        ones = mask.astype(jnp.float32)
        dec = jnp.concatenate([db[i] for i in range(chips)], axis=1)
        run_s = lax.dot_general(ones, dec, NT, precision=PRECISE, preferred_element_type=jnp.float32)
        run_l = lax.dot_general(dec, ones, NT, precision=PRECISE, preferred_element_type=jnp.float32)
        run_a[...], run_b[...] = run_s, run_l
        for h in range(heads):
            gap = run_s[:, h : h + 1] - run_l[h : h + 1, :]
            dec_s[h] = jnp.where(mask, jnp.exp(jnp.minimum(gap, 0.0)), 0.0)
        unit = (t_at == k_at).astype(jnp.float32)
        flags_t = mm(unit, dec[heads:], NT)
        tok_hidden, tok_filled = across_lanes(flags_t[:, 0:1]), across_lanes(flags_t[:, 0:1] * flags_t[:, 1:2])
        tok_shown = across_lanes(1.0 - flags_t[:, 0:1])

    with scope("load_w"):
        landed(wa, in_sem[0])
        landed(wout, in_sem[1])

    def turn_decay():
        late = k_at - t_at
        reach = jnp.logical_and(late >= 0, (late & (cols - 1)) * c == 0)
        for h in range(heads):
            gap = run_b[h : h + 1, :] - run_a[:, h : h + 1]
            turned_s[h] = jnp.where(reach, jnp.exp(jnp.minimum(gap, 0.0)), 0.0)

    def halves(ref):
        return jnp.concatenate([ref[0], ref[1]], axis=1)

    def unpack(f):
        at = pl.ds(pl.multiple_of(f * part, part), part)
        either = mb[pl.ds(f * chips, chips)].reshape(toks, part)
        gb[:, at] = either * tok_hidden
        return either * tok_shown + token_ref[at].reshape(1, part) * tok_filled

    def split(f):
        for i in range(depth // 2):
            q = f * (depth // 2) + i
            at_i = slice(i * slab, (i + 1) * slab)
            ga[f, :, at_i] = gb[:, block(2 * q + xi)]

    def half_gn(f):
        at = pl.ds(pl.multiple_of(f * part, part), part)
        return mm(gb[:, at], wout[at, :], NN)

    def arrive_m(core):
        for f in range(2):

            @pl.when(core == f)
            def _():
                landed(mb.at[pl.ds(f * chips, chips)], m_recv[f])

    lend_sems = [(new_sem(), new_sem()) for _ in range(3)]

    def lend(i, src, dst):
        return remote(src, dst, *lend_sems[i], k, 1)

    pair = [pl.ds(i * 256, 256) for i in range(4)]
    lend_a = lend(0, ga, la)
    lend_x = lend(1, gx, lx)
    lend_n = lend(2, normed_s.at[:, pair[1]], ln)
    n_first = remote(normed_s.at[:, pair[0]], nx.at[:, pair[0]], n_send, n_recv, beside, c)
    n_col = remote(normed_s.at[:, pair[1]], nx.at[:, pair[1]], n_send, nc_recv, beside, 1)
    n_row = remote(normed_s.at[:, pair[1]], lnx, n_send, nr_recv, beside, 1)
    with scope("arrive_first"):
        arrive_m(c)
    with scope("proj_first"):
        own = unpack(c)
        firsts = [mm(own, wa[at : at + size], NT) for _, at, size in pieces]
        split(c)
        gn_first = half_gn(c)

        @pl.when(c == 0)
        def _():
            each_g_row()
            turn_decay()

    with scope("arrive_second"):
        arrive_m(1 - c)
    with scope("weights_wait"):
        landed(wb, w_recv)
    with scope("proj_second"):
        oth = unpack(1 - c)
        for dst, (_, at, size), first in zip((u_s, z_s, bc_s), pieces, firsts):
            dst[...] = (first + mm(oth, wb[at : at + size], NT)).astype(jnp.bfloat16)
        split(1 - c)


    def per_head(x):
        high = x.astype(jnp.bfloat16)
        rest = (x - high.astype(jnp.float32)).astype(jnp.bfloat16)
        return mm(high, averages, NN) + mm(rest, averages, NN)

    def if_core(core, copies):
        @pl.when(c == core)
        def _():
            for copy in copies:
                copy.start()

    if_core(0, [lend_a])

    with scope("forward"):
        b_bf, c_bf = bc_s[:, :N], bc_s[:, N:]
        scores = mm(c_bf, b_bf, NT)
        rest_at = pl.ds(pl.multiple_of((1 - c) * part, part), part)
        for p in range(half // 128):
            cols_p = slice(p * 128, (p + 1) * 128)
            if p >= 2:
                two = slice((p - 2) * 256, (p - 1) * 256)
                gn = gn_first[:, two] + mm(gb[:, rest_at], wout[rest_at, two], NN)
                gn_s[:, two] = gn.astype(jnp.bfloat16)
            u = u_s[:, cols_p].astype(jnp.float32)
            sig_u = 0.5 + 0.5 * jnp.tanh(0.5 * u)
            su_s[:, cols_p] = sig_u
            val_bf = (u * sig_u).astype(jnp.bfloat16)
            for h in (2 * p, 2 * p + 1):
                mat_s[h] = (dec_s[h] * scores).astype(jnp.bfloat16)
            y = jnp.where(low, mm(mat_s[2 * p], val_bf, NN), mm(mat_s[2 * p + 1], val_bf, NN))
            y_s[:, cols_p] = y
            z = z_s[:, cols_p].astype(jnp.float32)
            sig_z = 0.5 + 0.5 * jnp.tanh(0.5 * z)
            sz_s[:, cols_p] = sig_z
            gated = y * (z * sig_z)
            inv = lax.rsqrt(per_head(gated * gated) + EPSILON)
            inv_s[:, cols_p] = inv
            normed_s[:, cols_p] = (gated * inv).astype(jnp.bfloat16)
            if p == 1:
                n_first.start()
            if p == 3:
                if_core(1, [n_col])

                @pl.when(c == 1)
                def _():
                    each_g_row()

                if_core(0, [n_row, lend_n])

    with scope("turn_decay"):
        @pl.when(c == 1)
        def _():
            turn_decay()

    with scope("backward"):
        turned_scores = mm(b_bf, c_bf, NT)
        d_scores = jnp.zeros((toks, toks), jnp.float32)
        for p in range(half // 128):
            cols_p = slice(p * 128, (p + 1) * 128)
            z, sig_z, y, inv = z_s[:, cols_p].astype(jnp.float32), sz_s[:, cols_p], y_s[:, cols_p], inv_s[:, cols_p]
            act = z * sig_z
            normed = y * act * inv
            u, sig_u = u_s[:, cols_p].astype(jnp.float32), su_s[:, cols_p]
            val = u * sig_u
            val_bf = val.astype(jnp.bfloat16)
            gn = gn_s[:, cols_p].astype(jnp.float32)
            gg = inv * (gn - normed * per_head(gn * normed))
            dy = gg * act
            dz = gg * y * (sig_z + act * (1.0 - sig_z))
            dy_bf = dy.astype(jnp.bfloat16)
            dec_a, dec_b = turned_s[2 * p], turned_s[2 * p + 1]
            dv = jnp.where(
                low,
                mm((dec_a * turned_scores).astype(jnp.bfloat16), dy_bf, NN),
                mm((dec_b * turned_scores).astype(jnp.bfloat16), dy_bf, NN),
            )
            du = dv * (sig_u + val * (1.0 - sig_u))
            gp[:, cols_p] = du.astype(jnp.bfloat16)
            gp[:, half + p * 128 : half + (p + 1) * 128] = dz.astype(jnp.bfloat16)
            zero = jnp.zeros_like(dy)
            d_scores += dec_a * mm(val_bf, jnp.where(low, dy, zero).astype(jnp.bfloat16), NT)
            d_scores += dec_b * mm(val_bf, jnp.where(low, zero, dy).astype(jnp.bfloat16), NT)
        ds_bf = d_scores.astype(jnp.bfloat16)
        d_bc = jnp.concatenate([mm(ds_bf, c_bf, NN), mm(ds_bf, b_bf, TN)], axis=1)
        gp[:, 2 * half :] = d_bc.astype(jnp.bfloat16)

    with scope("pass_gx"):

        @pl.when(c == 0)
        def _():
            landed(gx, g_recv)

        if_core(0, [lend_x])

    home, slot = k // rows, lax.rem(k, rows)

    def row_back(f, chip):
        return remote(prs.at[f, chip], prow.at[f, slot], p_send, p_recv, chip, home)

    def col_back(n):
        return remote(pcs.at[pl.ds(n * chips, rows)], pcol.at[n], c_send, c_recv, k, 0)

    others = [
        2 * z + x
        for z in (end_far, near_far, mate)
        for x in (1 - xi, xi)
    ] + [2 * zi + 1 - xi]

    def project_back(g_ref, w_ref):
        return mm(g_ref[...], w_ref[...], NN).astype(jnp.bfloat16).reshape(chips, cols, part)

    def return_rows(f, some=others):
        for chip in some:
            row_back(f, chip).start()

    def keep_rows(f):

        @pl.when(home == 1)
        def _():
            row_back(f, k).start()

        @pl.when(home == 0)
        def _():
            pltpu.make_async_copy(prs.at[f, k], prow.at[f, slot], p_recv).start()

    class Sums:
        def __init__(self, w, z, zin, zout, slot):
            self.w, self.z, self.zin, self.zout, self.slot = w, z, zin, zout, slot
            self.send, self.out_recv, *self.in_recv = [new_sem() for _ in range(4)]

        def to_target(self, j, kind, chip, core):
            return remote(
                self.z.at[2 * j + core], self.zout.at[3 * self.slot + kind], self.send, self.out_recv, chip, core
            )

        def part(self, j):
            return self.w[block(order[j]), :]

        def ready(self, j, value):
            self.z[2 * j : 2 * j + 2] = value.astype(jnp.bfloat16).reshape(2, slab // 2, value.shape[1])

        def begin(self):
            @pl.when(outer)
            def _():
                for j in range(2):
                    self.ready(j, self.part(j))
                    two = pl.ds(2 * j, 2)
                    remote(
                        self.z.at[two], self.zin.at[two], self.send, self.in_recv[j], 2 * mate + xi, c
                    ).start()

            self.ready(2, self.part(2))
            for core in range(2):
                self.to_target(2, 0, 2 * mate + xi, core).start()
            self.ready(3, self.part(3))
            pltpu.make_async_copy(
                self.z.at[6 + c], self.zout.at[3 * self.slot + 2], self.out_recv
            ).start()
            self.to_target(3, 2, k, 1 - c).start()

        def combine(self):
            @pl.when(inner)
            def _():
                for j in range(2):
                    landed(self.zin.at[pl.ds(2 * j, 2)], self.in_recv[j])
                    passed = self.zin[2 * j : 2 * j + 2].astype(jnp.float32).reshape(slab, self.w.shape[1])
                    self.ready(j, self.part(j) + passed)
                    for core in range(2):
                        self.to_target(j, 1, 2 * order[j] + xi, core).start()

        def drain(self):
            landed(self.z.at[pl.ds(0, 7)], self.send)

    col_first = Sums(wca, zsa, zca, zr, 0)
    col_second = Sums(wcb, zsb, zcb, zr, 1)
    row_sums = Sums(wq, zq, zcq, zrq, c)

    @pl.when(c == 0)
    def _():
        with scope("back_project_0"):
            for f, w_ref in enumerate((wa, wb)):
                prs[f] = project_back(gp, w_ref)

                keep_rows(f)

                @pl.when(inner)
                def _():
                    return_rows(f, others if f == 0 else others[:4])

                if f == 0:

                    @pl.when(outer)
                    def _():
                        return_rows(0, others[:4])

        with scope("wait_n0"):
            landed(nx.at[:, pair[0]], n_recv)
        with scope("row_product_0"):
            wq[...] = mm(halves(ga), normed_s[:, :256], TN) + mm(gx[...].reshape(toks, part), nx[:, :256], TN)

    @pl.when(c == 1)
    def _():
        with scope("col_back_1"):
            for n, w_ref in enumerate((wa, wb)):
                pcs[n * chips : (n + 1) * chips] = project_back(gp, w_ref)
                col_back(n).start()
                pcol[n] = pcs[n * chips + rows : (n + 1) * chips]
        with scope("wait_n1"):
            landed(gcx, gc_recv)
            landed(nx.at[:, pair[0]], n_recv)

        def col_product(i):
            own = mm(halves(ga), normed_s[:, i * 256 : (i + 1) * 256], TN)
            return own + mm(gcx[...].reshape(toks, part), nx[:, i * 256 : (i + 1) * 256], TN)

        with scope("col_first"):
            wca[...] = col_product(0)
            col_first.begin()
        with scope("wait_n2"):
            landed(nx.at[:, pair[1]], nc_recv)
        with scope("col_second"):
            wcb[...] = col_product(1)
            col_second.begin()
        with scope("lent_wait"):
            for copy in (lend_a, lend_x, lend_n, n_row):
                copy.wait_recv()
        with scope("row_product_1"):
            wq[...] = mm(halves(la), ln[...], TN) + mm(lx[...].reshape(toks, part), lnx[...], TN)

    with scope("row_begin"):
        row_sums.begin()

    with scope("return_rows"):
        @pl.when(jnp.logical_and(c == 0, inner))
        def _():
            return_rows(1, others[4:])

        @pl.when(jnp.logical_and(c == 0, outer))
        def _():
            return_rows(0, others[4:])
            return_rows(1)


    @pl.when(c == 1)
    def _():
        with scope("col_combine"):
            col_first.combine()
            col_second.combine()

    with scope("row_combine"):
        row_sums.combine()

    with scope("parts_wait"):

        @pl.when(c == 0)
        def _():
            landed(pcol, c_recv)

        landed(prow, p_recv)

    with scope("patch_grad"):
        for f in range(2):
            by_row, by_col = prow.at[f], pcol.at[1 - f]
            for i in range(rows):
                keep = visible_t[:, i : i + 1]
                both = by_row[i].astype(jnp.float32) + by_col[i].astype(jnp.float32)
                pg_ref[i, :, f * part : (f + 1) * part] = (both * keep).astype(pg_ref.dtype)

    results = [
        pltpu.make_async_copy(pg_ref, pg_out, in_sem[0]),
        pltpu.make_async_copy(out_ref, sum_out, in_sem[1]),
    ]
    results[0].start()

    with scope("sums_wait"):
        landed(zr.at[pl.ds(0, 3)], col_first.out_recv)
        landed(zr.at[pl.ds(3, 3)], col_second.out_recv)
        landed(zrq, row_sums.out_recv)

    with scope("weight_sum"):
        for ref, at, size in ((zrq.at[0:3], 0, 256), (zrq.at[3:6], 256, 256), (zr.at[0:3], half, 256), (zr.at[3:6], half + 256, 256)):
            acc = ref[0].astype(jnp.float32) + ref[1].astype(jnp.float32)
            acc += ref[2].astype(jnp.float32)
            out_ref[:, at : at + size] = acc * scale
    results[1].start()

    with scope("drain"):
        drained(db, d_send, rows, 1, rows)
        drained(mb, m_send, 2 * rows, 2, 2 * rows)
        drained(gx, g_send, rows, 1, 0)
        landed(gsx, gc_send)
        landed(wb, w_send)
        row_sums.drain()
        landed(normed_s, n_send)

        @pl.when(jnp.logical_and(c == 0, home == 0))
        def _():
            landed(pcs.at[pl.ds(0, 2 * chips - 2)], p_send)

        @pl.when(jnp.logical_and(c == 0, home == 1))
        def _():
            landed(pcs, p_send)

        @pl.when(c == 0)
        def _():
            for copy in (lend_a, lend_x, lend_n):
                copy.wait_send()

        @pl.when(c == 1)
        def _():
            col_first.drain()
            col_second.drain()
            landed(pcol, c_send)

        for copy in results:
            copy.wait()


def store_kernel(a_ref, b_ref, a_hbm, b_hbm, sem):
    copies = [
        pltpu.make_async_copy(a_ref, a_hbm, sem.at[0]),
        pltpu.make_async_copy(b_ref, b_hbm, sem.at[1]),
    ]
    for copy in copies:
        copy.start()
    for copy in copies:
        copy.wait()


def owned(
    patches, mask_token, masked, tissue, in_weight, out_weight, row_decay, col_decay, cotangent
):
    rows, cols, feat = patches.shape
    chips = lax.axis_size("gcol")
    toks, heads = chips * cols, row_decay.shape[0]
    half, part = out_weight.shape[1], in_weight.shape[1]
    width = 2 * half + 2 * N
    slab = feat // chips
    bf, fl = jnp.bfloat16, jnp.float32
    vmem, dma = pltpu.VMEM, pltpu.SemaphoreType.DMA
    anywhere = pl.BlockSpec(memory_space=pltpu.HBM)
    place = pl.BlockSpec(memory_space=pl.ANY)
    scale = 1.0 / math.sqrt(2 * rows * cols * chips)
    aux = heads + 8
    results = pl.pallas_call(
        functools.partial(layer_kernel, chips, rows, scale),
        name="layer",
        out_shape=(vmem(patches.shape, bf), vmem((slab // 2, 2 * half), fl)),
        in_specs=[anywhere] * 9,
        out_specs=(place, place),
        scratch_shapes=[
            dma((41,)), vmem(patches.shape, bf), vmem((slab // 2, 2 * half), fl),
            vmem((2,) + patches.shape, bf), vmem(mask_token.shape, bf),
            vmem((2,) + masked.shape, masked.dtype), vmem((2,) + row_decay.shape, fl),
            vmem((2, rows, cols, part), bf), vmem((2 * chips, cols, part), bf),
            vmem((rows, aux, cols), fl), vmem((rows, aux, cols), fl), vmem((chips, aux, cols), fl),
            vmem((width, part), bf), vmem((width, part), bf), vmem((width, part), bf), vmem(out_weight.shape, bf),
            vmem((toks, feat), bf), vmem((rows, cols, part), bf), vmem((2, toks, part // 2), bf),
            vmem((chips, cols, part), bf), vmem((rows, cols, part), bf), vmem((chips, cols, part), bf),
            vmem((toks, half), bf), vmem((2, toks, part // 2), bf),
            vmem((chips, cols, part), bf), vmem((toks, half // 2), bf), vmem((toks, half // 2), bf),
            vmem((toks, half), bf), vmem((toks, half), bf), vmem((toks, half), fl), vmem((toks, half), fl),
            vmem((toks, half), bf), vmem((toks, 2 * N), bf), vmem((toks, half), bf),
            vmem((toks, half), fl), vmem((toks, half), fl),
            vmem((heads, toks, toks), bf), vmem((heads, toks, toks), fl),
            vmem((heads, toks, toks), fl), vmem((toks, aux), fl), vmem((aux, toks), fl),
            vmem((toks, width), bf), vmem((2, chips, cols, part), bf), vmem((2 * chips, cols, part), bf),
            vmem((2, rows, cols, part), bf), vmem((2, rows, cols, part), bf),
            vmem((half, half // 2), fl), vmem((half, half // 2), fl), vmem((half, half // 2), fl),
            vmem((8, slab // 2, half // 2), bf), vmem((8, slab // 2, half // 2), bf), vmem((8, slab // 2, half // 2), bf),
            vmem((4, slab // 2, half // 2), bf), vmem((4, slab // 2, half // 2), bf), vmem((4, slab // 2, half // 2), bf),
            vmem((6, slab // 2, half // 2), bf), vmem((6, slab // 2, half // 2), bf),
        ],
        compiler_params=pltpu.CompilerParams(
            collective_id=0, has_side_effects=True, vmem_limit_bytes=60 << 20
        ),
    )(
        patches, mask_token, cotangent, masked, tissue, row_decay, col_decay,
        in_weight, out_weight,
    )
    return pl.pallas_call(
        store_kernel,
        name="store",
        out_shape=tuple(jax.ShapeDtypeStruct(r.shape, r.dtype) for r in results),
        in_specs=[place] * 2,
        out_specs=[anywhere] * 2,
        scratch_shapes=[dma((2,))],
        compiler_params=pltpu.CompilerParams(vmem_limit_bytes=1 << 20),
    )(*results)


def body(*args):
    rows = args[0].shape[0]
    cols = args[0].shape[1]
    if lax.axis_size("grow") == 2 and rows == 4 and lax.axis_size("gcol") == 2 * rows and cols & (cols - 1) == 0:
        return owned(*args)
    return shards(*args)


def solution(mesh):
    return jax.shard_map(
        body,
        mesh=mesh,
        in_specs=(
            P(("groups", "grow"), "gcol", None),
            P(),
            P(("groups", "grow"), "gcol"),
            P(("groups", "grow"), "gcol"),
            P(None, "grow"),
            P(None, "grow"),
            P(None, ("groups", "grow"), "gcol"),
            P(None, ("groups", "grow"), "gcol"),
            P(("groups", "grow"), "gcol", None),
        ),
        out_specs=(P(("groups", "grow"), "gcol", None), P(("groups", "gcol", "grow"), None)),
        check_vma=False,
    )
```
